256 devices in a mesh: scene: 8 (over z_hi, core), tile: 32 (over z_lo, y, x).
Axes of the slice: x: 4, y: 4, z: 8 (z_hi: 4, z_lo: 2; z = z_hi * 2 + z_lo), core: 2. Of those that a mesh axis runs over, the one named last changes fastest.
Arguments:
- gaussians: float32 [8, 64, 59, 128], P('scene', 'tile'), as said below
- consensus: float32 [8, 64, 59, 128], P('scene', 'tile'), as said below
- duals: float32 [8, 64, 59, 128], P('scene', 'tile'), may hold values from -0.6 to 0.6
- step_sizes: float32 [59], replicated, may hold values from 0.02 to 0.2
- cameras: float32 [16, 16], replicated, as said below
- camera_ids: int32 [8, 32], P('scene', 'tile'), may hold values from 0 to 15
- block_lists: int32 [8, 32, 16], P('scene', 'tile'), may hold values from 0 to 63, as said below
- depth_order: int32 [8, 32, 16], P('scene', 'tile'), may hold values from 0 to 15, as said below
- block_counts: int32 [8, 32], P('scene', 'tile'), may hold values from 1 to 16, as said below
- targets: float32 [8, 32, 3, 1024], P('scene', 'tile'), may hold values from 0 to 1
- intersection: int32 [8, 32, 2, 64], P('scene', 'tile'), may hold values from 0 to 255, as said below
Outputs:
- updated: float32 [8, 64, 59, 128], P('scene', 'tile')
- new_duals: float32 [8, 64, 59, 128], P('scene', 'tile')
The draws below stay inside these ranges and needn't reach their ends.
Inputs may be any that keep to these rules, and one draw needn't show every extreme that they name: `gaussians`: rows 0 and 1 of each Gaussian lie in -1.5 to 1.5, row 2 in 3 to 6, rows 3 to 5 in log 0.1 to log 0.5, row 6 in 0.8 to 1.2, row 10 in -2 to 6. `consensus`: drawn like gaussians. `cameras`: rotations within 0.15 of the identity about each axis, translations within 0.3, focal lengths 80 to 120, principal point x 40 to 88, y 16 to 48. `block_lists`: each strip lists 16 block numbers whose quotients by 2 all differ. `depth_order`: each strip's entries are a permutation of its slots. `block_counts`: some strip of every group has all 16 slots live. `intersection`: the 128 entries of a device are different local Gaussian numbers and include 0 and 255.
All inputs are finite; a program needn't handle non-finite values.
Results may differ from the reference program's by a relative error of at most 0.0003.
Values sent between devices are 32-bit elements; how exact they have to be, the bound alone decides.
A program may use at most 64 MiB of HBM per device.

```python
import math
import jax
import jax.numpy as jnp
from jax import lax

PARAMS = 59
BLOCK = 128
BLK_DEV = 2
LISTED = 16
HALF = 64
NCAM = 16
GROUPS = 8
STRIPS = 32
NB = 64
PIX = 1024


def gauss_field(seed_key):
    keys = jax.random.split(seed_key, 7)
    leading = (GROUPS, NB)

    def uniform_rows(subkey, height, lower, upper):
        return jax.random.uniform(subkey, leading + (height, BLOCK), jnp.float32, lower, upper)
    planar = uniform_rows(keys[0], 2, -1.5, 1.5)
    depth_row = uniform_rows(keys[1], 1, 3.0, 6.0)
    log_scale = uniform_rows(keys[2], 3, math.log(0.1), math.log(0.5))
    quat_real = uniform_rows(keys[3], 1, 0.8, 1.2)
    quat_imag = 0.3 * jax.random.normal(keys[4], leading + (3, BLOCK), jnp.float32)
    logit_row = uniform_rows(keys[5], 1, -2.0, 6.0)
    harmonics = 0.3 * jax.random.normal(keys[6], leading + (48, BLOCK), jnp.float32)
    return jnp.concatenate([planar, depth_row, log_scale, quat_real, quat_imag, logit_row, harmonics], 2)


def draw_gaussians(key, part):
    return gauss_field(jax.random.fold_in(key, 11))


def draw_consensus(key, part):
    return gauss_field(jax.random.fold_in(key, 23))


def draw_cameras(key, part):
    keys = jax.random.split(jax.random.fold_in(key, 31), 5)
    angles = jax.random.uniform(keys[0], (NCAM, 3), jnp.float32, -0.15, 0.15)
    cos_v = jnp.cos(angles)
    sin_v = jnp.sin(angles)
    zeros_v = jnp.zeros((NCAM,), jnp.float32)
    ones_v = jnp.ones((NCAM,), jnp.float32)
    turn_x = jnp.stack([jnp.stack([ones_v, zeros_v, zeros_v], -1), jnp.stack([zeros_v, cos_v[:, 0], -sin_v[:, 0]], -1), jnp.stack([zeros_v, sin_v[:, 0], cos_v[:, 0]], -1)], 1)
    turn_y = jnp.stack([jnp.stack([cos_v[:, 1], zeros_v, sin_v[:, 1]], -1), jnp.stack([zeros_v, ones_v, zeros_v], -1), jnp.stack([-sin_v[:, 1], zeros_v, cos_v[:, 1]], -1)], 1)
    turn_z = jnp.stack([jnp.stack([cos_v[:, 2], -sin_v[:, 2], zeros_v], -1), jnp.stack([sin_v[:, 2], cos_v[:, 2], zeros_v], -1), jnp.stack([zeros_v, zeros_v, ones_v], -1)], 1)
    rotation = jnp.einsum('nij,njk,nkl->nil', turn_z, turn_y, turn_x)
    offsets = jax.random.uniform(keys[1], (NCAM, 3), jnp.float32, -0.3, 0.3)
    focal = jax.random.uniform(keys[2], (NCAM, 2), jnp.float32, 80.0, 120.0)
    centre_x = jax.random.uniform(keys[3], (NCAM, 1), jnp.float32, 40.0, 88.0)
    centre_y = jax.random.uniform(keys[4], (NCAM, 1), jnp.float32, 16.0, 48.0)
    return jnp.concatenate([rotation.reshape(NCAM, 9), offsets, focal, centre_x, centre_y], 1)


def distinct_order(seed_key, leading, length):
    scores = jax.random.randint(seed_key, leading + (length,), 0, 1 << 20) * length + jnp.arange(length, dtype=jnp.int32)
    return jnp.argsort(scores, axis=-1).astype(jnp.int32)


def draw_block_lists(key, part):
    keys = jax.random.split(jax.random.fold_in(key, 41), 2)
    owners = distinct_order(keys[0], (GROUPS, STRIPS), STRIPS)[..., :LISTED]
    within = jax.random.randint(keys[1], (GROUPS, STRIPS, LISTED), 0, BLK_DEV)
    return (owners * BLK_DEV + within).astype(jnp.int32)


def draw_depth_order(key, part):
    return distinct_order(jax.random.fold_in(key, 43), (GROUPS, STRIPS), LISTED)


def draw_block_counts(key, part):
    keys = jax.random.split(jax.random.fold_in(key, 47), 3)
    busy = jax.random.randint(keys[0], (GROUPS, STRIPS), 0, 3) == 0
    light = jax.random.randint(keys[1], (GROUPS, STRIPS), 1, max(LISTED // 2, 1) + 1)
    counts_drawn = jnp.where(busy, LISTED, light)
    chosen = jax.random.randint(keys[2], (GROUPS, 1), 0, STRIPS)
    return jnp.where(jnp.arange(STRIPS, dtype=jnp.int32)[None, :] == chosen, LISTED, counts_drawn).astype(jnp.int32)


def draw_intersection(key, part):
    keys = jax.random.split(jax.random.fold_in(key, 53), 2)
    local_size = BLK_DEV * BLOCK
    inner = distinct_order(keys[0], (GROUPS, STRIPS), local_size - 2)[..., :2 * HALF - 2] + 1
    ends = jnp.broadcast_to(jnp.array([0, local_size - 1], jnp.int32), (GROUPS, STRIPS, 2))
    picked = jnp.concatenate([ends, inner], -1)
    mixing = distinct_order(keys[1], (GROUPS, STRIPS), 2 * HALF)
    return jnp.take_along_axis(picked, mixing, axis=-1).reshape(GROUPS, STRIPS, 2, HALF).astype(jnp.int32)


def place_ends(result, rng, smallest, largest):
    place = [jax.random.randint(jax.random.fold_in(rng, axis), (), 0, length) for axis, length in enumerate(result.shape)]
    longest = result.shape.index(max(result.shape))
    next_to = place[:longest] + [(place[longest] + 1) % result.shape[longest]] + place[longest + 1:]
    return result.at[tuple(place)].set(smallest).at[tuple(next_to)].set(largest)


def shard_levels(stream_key, shape, pieces, least, high):
    def one(dim, shards_of):
        draws = jax.random.uniform(jax.random.fold_in(jax.random.fold_in(stream_key, 6), dim), (shards_of,), jnp.float32, least / len(pieces), high / len(pieces))
        return jnp.repeat(jnp.exp(draws), shape[dim] // shards_of).reshape((-1,) + (1,) * (len(shape) - dim - 1))

    gain = one(*pieces[0])
    for cut in pieces[1:]:
        gain = gain * one(*cut)
    return gain


def gaussian(stream_key, extent, deviation, bound, cuts=(), held_as=jnp.bfloat16):
    factor_of = shard_levels(stream_key, extent, cuts, -0.22, 0.18) if cuts else 1.0
    entries = jax.random.normal(stream_key, extent, jnp.float32) * deviation * factor_of
    return jnp.minimum(jnp.maximum(entries, -bound), bound).astype(held_as)


def setup_inputs(seed: int = 0) -> dict:
    seeds = jax.random.split(jax.random.key(seed), 12)
    gaussians = draw_gaussians(jax.random.fold_in(seeds[11], 71), 0)
    consensus = draw_consensus(jax.random.fold_in(seeds[11], 71), 0)
    duals = gaussian(seeds[2], (GROUPS, NB, PARAMS, BLOCK), 0.1, 0.6, ((0, 8), (1, 32)), jnp.float32)
    step_sizes = jnp.clip(jnp.exp(jax.random.uniform(seeds[3], (PARAMS,), jnp.float32, math.log(0.02), math.log(0.2))), 0.02, 0.2)
    cameras = draw_cameras(jax.random.fold_in(seeds[11], 71), 0)
    camera_ids = place_ends(jax.random.randint(seeds[5], (GROUPS, STRIPS), 0, NCAM), jax.random.fold_in(seeds[5], 1), 0, NCAM - 1).astype(jnp.int32)
    block_lists = draw_block_lists(jax.random.fold_in(seeds[11], 71), 0)
    depth_order = draw_depth_order(jax.random.fold_in(seeds[11], 71), 0)
    block_counts = draw_block_counts(jax.random.fold_in(seeds[11], 71), 0)
    targets = jnp.clip(1.0 * jax.random.uniform(seeds[9], (GROUPS, STRIPS, 3, PIX), jnp.float32) ** shard_levels(seeds[9], (GROUPS, STRIPS, 3, PIX), ((0, 8), (1, 32)), -0.2, 0.2), 0.0, 1.0)
    intersection = draw_intersection(jax.random.fold_in(seeds[11], 71), 0)
    return dict(gaussians=gaussians, consensus=consensus, duals=duals, step_sizes=step_sizes, cameras=cameras, camera_ids=camera_ids, block_lists=block_lists, depth_order=depth_order, block_counts=block_counts, targets=targets, intersection=intersection)


highest = lax.Precision.HIGHEST
penalty_weight = 0.5
blur_floor = 0.3
alpha_ceiling = 0.99
sh_zero = 0.28209479177387814
sh_one = 0.4886025119029199
sh_two = (1.0925484305920792, -1.0925484305920792, 0.31539156525252005, -1.0925484305920792, 0.5462742152960396)
sh_three = (-0.5900435899266435, 2.890611442640554, -0.4570457994644658, 0.3731763325901154, -0.4570457994644658, 1.445305721320277, -0.5900435899266435)

def harmonic_basis(toward):
    comp_x, comp_y, comp_z = (toward[0], toward[1], toward[2])
    sq_x, sq_y, sq_z = (comp_x * comp_x, comp_y * comp_y, comp_z * comp_z)
    return jnp.stack([sh_zero + 0.0 * comp_x, -sh_one * comp_y, sh_one * comp_z, -sh_one * comp_x, sh_two[0] * comp_x * comp_y, sh_two[1] * comp_y * comp_z, sh_two[2] * (2.0 * sq_z - sq_x - sq_y), sh_two[3] * comp_x * comp_z, sh_two[4] * (sq_x - sq_y), sh_three[0] * comp_y * (3.0 * sq_x - sq_y), sh_three[1] * comp_x * comp_y * comp_z, sh_three[2] * comp_y * (4.0 * sq_z - sq_x - sq_y), sh_three[3] * comp_z * (2.0 * sq_z - 3.0 * sq_x - 3.0 * sq_y), sh_three[4] * comp_x * (4.0 * sq_z - sq_x - sq_y), sh_three[5] * comp_z * (sq_x - sq_y), sh_three[6] * comp_x * (sq_x - 3.0 * sq_y)])

def gauss_features(gauss_block, camera):
    rotation = camera[0:9].reshape(3, 3)
    shift_vec = camera[9:12]
    focal_x, focal_y, center_x, center_y = (camera[12], camera[13], camera[14], camera[15])
    centre = gauss_block[0:3]
    viewed = jnp.dot(rotation, centre, precision=highest) + shift_vec[:, None]
    inverse = 1.0 / viewed[2]
    screen_x = focal_x * viewed[0] * inverse + center_x
    screen_y = focal_y * viewed[1] * inverse + center_y
    quater = gauss_block[6:10]
    quater = quater / jnp.sqrt(lax.optimization_barrier(jnp.sum(quater * quater, 0)))
    quat_w, quat_x, quat_y, quat_z = (quater[0], quater[1], quater[2], quater[3])
    rot_rows = jnp.stack([jnp.stack([1.0 - 2.0 * (quat_y * quat_y + quat_z * quat_z), 2.0 * (quat_x * quat_y - quat_w * quat_z), 2.0 * (quat_x * quat_z + quat_w * quat_y)]), jnp.stack([2.0 * (quat_x * quat_y + quat_w * quat_z), 1.0 - 2.0 * (quat_x * quat_x + quat_z * quat_z), 2.0 * (quat_y * quat_z - quat_w * quat_x)]), jnp.stack([2.0 * (quat_x * quat_z - quat_w * quat_y), 2.0 * (quat_y * quat_z + quat_w * quat_x), 1.0 - 2.0 * (quat_x * quat_x + quat_y * quat_y)])])
    scales = jnp.exp(gauss_block[3:6])
    spread = rot_rows * scales[None, :, :]
    world_axes = jnp.einsum('ij,jkg->ikg', rotation, spread, precision=highest)
    row_one = focal_x * inverse * world_axes[0] - focal_x * viewed[0] * inverse * inverse * world_axes[2]
    row_two = focal_y * inverse * world_axes[1] - focal_y * viewed[1] * inverse * inverse * world_axes[2]
    cov_xx = lax.optimization_barrier(jnp.sum(row_one * row_one, 0)) + blur_floor
    cov_xy = lax.optimization_barrier(jnp.sum(row_one * row_two, 0))
    cov_yy = lax.optimization_barrier(jnp.sum(row_two * row_two, 0)) + blur_floor
    determ = cov_xx * cov_yy - cov_xy * cov_xy
    conic_a = cov_yy / determ
    conic_b = -cov_xy / determ
    conic_c = cov_xx / determ
    opacity = jax.nn.sigmoid(gauss_block[10])
    eye_pos = -jnp.dot(rotation.T, shift_vec, precision=highest)
    toward = centre - eye_pos[:, None]
    toward = toward / jnp.sqrt(lax.optimization_barrier(jnp.sum(toward * toward, 0)))
    coeffs = gauss_block[11:59].reshape(16, 3, -1)
    colour = lax.optimization_barrier(jnp.sum(harmonic_basis(toward)[:, None, :] * coeffs, 0)) + 0.5
    return (screen_x, screen_y, conic_a, conic_b, conic_c, opacity, colour)

def blend_block(state_pair, gauss_block, camera, pixel_x, pixel_y, strict):
    transmit, colour_sum = state_pair
    screen_x, screen_y, conic_a, conic_b, conic_c, opacity, colour = gauss_features(gauss_block, camera)
    delta_x = pixel_x[:, None] - screen_x[None, :]
    delta_y = pixel_y[:, None] - screen_y[None, :]
    exponent = -0.5 * (conic_a * delta_x * delta_x + conic_c * delta_y * delta_y) - conic_b * delta_x * delta_y
    alpha_px = jnp.minimum(alpha_ceiling, opacity * jnp.exp(exponent))
    logs_kept = jnp.log1p(-alpha_px)
    before = jnp.dot(logs_kept, strict, precision=highest)
    weight = alpha_px * transmit[:, None] * jnp.exp(before)
    colour_sum = colour_sum + jnp.einsum('cg,pg->cp', colour, weight, precision=highest)
    transmit = transmit * jnp.exp(lax.optimization_barrier(jnp.sum(logs_kept, 1)))
    return (transmit, colour_sum)

def strip_loss(listed, camera, strip_index, depth_steps, active_count, target):
    pixels = target.shape[1]
    strip_rows = pixels // 128
    pixel_index = jnp.arange(pixels, dtype=jnp.int32)
    pixel_x = (pixel_index % 128).astype(jnp.float32)
    pixel_y = (pixel_index // 128 + strip_rows * (strip_index % 4)).astype(jnp.float32)
    lane_index = jnp.arange(listed.shape[2], dtype=jnp.int32)
    strict = (lane_index[:, None] < lane_index[None, :]).astype(jnp.float32)
    blender = jax.checkpoint(lambda current, gauss_block: blend_block(current, gauss_block, camera, pixel_x, pixel_y, strict))

    def advance(current, slot_index):
        gauss_block = listed[slot_index]
        current = lax.cond(slot_index < active_count, lambda status: blender(status, gauss_block), lambda status: status, current)
        return (current, None)
    initial = (jnp.ones((pixels,), jnp.float32), jnp.zeros((3, pixels), jnp.float32))
    final_pair, unused = lax.scan(advance, initial, depth_steps)
    residual = final_pair[1] - target
    return 0.5 * jnp.sum(residual * residual)

def strip_gradient(listed, camera, strip_index, depth_steps, active_count, target):
    loss_value, pullback = jax.vjp(lambda blocks: strip_loss(blocks, camera, strip_index, depth_steps, active_count, target), listed)
    return pullback(jnp.ones_like(loss_value))[0]

def place_agreed(field, index_up, index_down, values_up, values_down):
    return field.at[:, index_up].set(values_up).at[:, index_down].set(values_down)

def reference(gaussians, consensus, duals, step_sizes, cameras, camera_ids, block_lists, depth_order, block_counts, targets, intersection):
    num_blocks = gaussians.shape[1]
    block_range = jnp.arange(num_blocks, dtype=jnp.int32)

    def group_sum(group_index):

        def strip_step(running, strip_index):
            listed_ids = block_lists[group_index, strip_index]
            listed = gaussians[group_index][listed_ids]
            camera = cameras[camera_ids[group_index, strip_index]]
            gradients = strip_gradient(listed, camera, strip_index, depth_order[group_index, strip_index], block_counts[group_index, strip_index], targets[group_index, strip_index])
            onehot = (listed_ids[:, None] == block_range[None, :]).astype(jnp.float32)
            return (running + jnp.einsum('kb,kgc->bgc', onehot, gradients, precision=highest), None)
        running, unused = lax.scan(strip_step, jnp.zeros(gaussians.shape[1:], jnp.float32), jnp.arange(STRIPS, dtype=jnp.int32))
        return running
    gradient = lax.map(group_sum, jnp.arange(GROUPS, dtype=jnp.int32))
    updated = gaussians - step_sizes[None, None, :, None] * (gradient + penalty_weight * (gaussians - consensus + duals))
    shifted = updated + duals
    local_view = shifted.reshape(GROUPS, STRIPS, BLK_DEV, PARAMS, BLOCK).transpose(0, 1, 3, 2, 4).reshape(GROUPS, STRIPS, PARAMS, BLK_DEV * BLOCK)
    index_up = intersection[:, :, 0]
    index_down = intersection[:, :, 1]
    up_vals = jnp.take_along_axis(local_view, index_up[:, :, None, :], axis=3)
    down_vals = jnp.take_along_axis(local_view, index_down[:, :, None, :], axis=3)
    from_above = jnp.concatenate([down_vals[1:], jnp.zeros_like(down_vals[:1])], 0)
    from_below = jnp.concatenate([jnp.zeros_like(up_vals[:1]), up_vals[:-1]], 0)
    group_ids = jnp.arange(GROUPS, dtype=jnp.int32)[:, None, None, None]
    agreed_up = jnp.where(group_ids < GROUPS - 1, 0.5 * (up_vals + from_above), up_vals)
    agreed_down = jnp.where(group_ids > 0, 0.5 * (down_vals + from_below), down_vals)
    agreed = jax.vmap(jax.vmap(place_agreed))(local_view, index_up, index_down, agreed_up, agreed_down)
    dual_local = local_view - agreed
    new_duals = dual_local.reshape(GROUPS, STRIPS, PARAMS, BLK_DEV, BLOCK).transpose(0, 1, 3, 2, 4).reshape(GROUPS, STRIPS * BLK_DEV, PARAMS, BLOCK)
    return (updated, new_duals)
```

```python
import functools

import jax
import jax.numpy as jnp
from jax import lax
from jax.experimental import pallas as pl
from jax.experimental.pallas import tpu as pltpu
from jax.sharding import PartitionSpec as P

HI = lax.Precision.HIGHEST
f32, bf16 = jnp.float32, jnp.bfloat16
MESH = pl.DeviceIdType.MESH
S = 132
SB = 8 * S
NI = 4
LN2 = 0.6931471805599453

def part2(v):
    a = v.astype(bf16)
    return a, (v - a.astype(f32)).astype(bf16)

def part3(v):
    a = v.astype(bf16).astype(f32)
    r = v - a
    b = r.astype(bf16).astype(f32)
    return a, b, (r - b).astype(bf16).astype(f32)

def render_body(ybase, feats, targ, bias, alpha, wts, gbuf, wbuf, lhs, csp, tb, cb, bend, rbuf, grhs, acc):
    sx, sy, fa, fb, fc, lo, k0, k1, k2 = feats
    sxc = sx - 64.0
    syc = sy - (ybase + 4.0)
    lob = lo + bias
    zero32 = jnp.zeros((32, 128), f32)
    pa = part3(fa)
    lhs_a = jnp.concatenate(list(pa) + list(pa) + [zero32], 0).T.astype(bf16)
    for y in range(8):
        dy = (y - 4.0) - syc
        c1 = fb * dy - 2.0 * fa * sxc
        c0 = (fa * sxc - fb * dy) * sxc + fc * dy * dy + lob
        m = jnp.concatenate(list(part3(c0)) + list(part3(c1)) + [zero32], 0)
        lhs[y * 128:(y + 1) * 128, 0:128] = m.T.astype(bf16)
        lhs[y * 128:(y + 1) * 128, 128:256] = lhs_a
    colt = jnp.concatenate([k0, k1, k2, jnp.zeros((80, 128), f32)], 0).T
    for c in range(3):
        for b in range(16):
            csp[c, b * 128:(b + 1) * 128, :] = jnp.broadcast_to(colt[:, c * 16 + b:c * 16 + b + 1], (128, 128))
    kr = lax.broadcasted_iota(jnp.int32, (256, 256), 0)
    ln = lax.broadcasted_iota(jnp.int32, (256, 256), 1)
    xi = ((ln & 127) - 64).astype(f32)
    x2 = xi * xi
    x2h = x2.astype(bf16).astype(f32)
    x2l = x2 - x2h
    basis = jnp.where(kr < 48, 1.0, jnp.where(kr < 96, xi, jnp.where(kr < 128, 0.0, jnp.where(kr < 176, x2h, jnp.where(kr < 224, x2l, 0.0)))))
    grhs[...] = basis
    def alpha_pair(p, _):
        rhs = jnp.where((kr & 15) == 2 * p + (ln >> 7), grhs[...], 0.0).astype(bf16)
        for y in range(8):
            e = jnp.dot(lhs[y * 128:(y + 1) * 128, :], rhs, preferred_element_type=f32)
            a = jnp.minimum(0.99, jnp.exp2(e))
            alpha[pl.ds(pl.multiple_of(2 * p * SB, 8) + y * S, 128), :] = a[:, :128]
            alpha[pl.ds(pl.multiple_of((2 * p + 1) * SB, 8) + y * S, 128), :] = a[:, 128:]
        return 0
    lax.fori_loop(0, 8, alpha_pair, 0)
    one = jnp.ones((8, 128), f32)
    zero = jnp.zeros((8, 128), f32)
    U = 8
    for q0 in range(0, 16, NI):
        def fwd(i, carry):
            st = [list(t) for t in carry]
            for u in range(U):
                g = i * U + u
                for j in range(NI):
                    b = q0 + j
                    a = alpha[pl.ds(b * SB + g, 8, stride=S), :]
                    t, s0, s1, s2 = st[j]
                    w = a * t
                    t = t * (1.0 - a)
                    row = b * 128 + g
                    s0 = s0 + w * csp[0, pl.ds(row, 8, stride=0), :]
                    s1 = s1 + w * csp[1, pl.ds(row, 8, stride=0), :]
                    s2 = s2 + w * csp[2, pl.ds(row, 8, stride=0), :]
                    wts[pl.ds(b * SB + g, 8, stride=S), :] = w
                    st[j] = [t, s0, s1, s2]
            return tuple(tuple(t) for t in st)
        out = lax.fori_loop(0, 128 // U, fwd, tuple((one, zero, zero, zero) for _ in range(NI)))
        for j in range(NI):
            tb[q0 + j] = out[j][0]
            for c in range(3):
                cb[c, q0 + j] = out[j][1 + c]
    t = one
    prods = [tb[b] for b in range(16)]
    cs = [zero, zero, zero]
    for b in range(16):
        tb[b] = t
        for c in range(3):
            cs[c] = cs[c] + t * cb[c, b]
        t = t * prods[b]
    r = [cs[c] - targ[c] for c in range(3)]
    e = zero
    for b in range(15, -1, -1):
        bend[b] = e
        e = prods[b] * e + (cb[0, b] * r[0] + cb[1, b] * r[1] + cb[2, b] * r[2])
    for q0 in range(0, 16, NI):
        tbs = [tb[q0 + j] for j in range(NI)]
        def bwd(i, carry):
            st = list(carry)
            for u in range(U):
                g = 127 - (i * U + u)
                for j in range(NI):
                    b = q0 + j
                    a = alpha[pl.ds(b * SB + g, 8, stride=S), :]
                    w = wts[pl.ds(b * SB + g, 8, stride=S), :] * tbs[j]
                    row = b * 128 + g
                    q = (r[0] * csp[0, pl.ds(row, 8, stride=0), :] + r[1] * csp[1, pl.ds(row, 8, stride=0), :]) + r[2] * csp[2, pl.ds(row, 8, stride=0), :]
                    d = q - st[j]
                    gg = jnp.where(a < 0.99, w * d, 0.0)
                    st[j] = st[j] + a * d
                    gbuf[pl.ds(b * SB + g, 8, stride=S), :] = gg
                    wbuf[pl.ds(b * SB + g, 8, stride=S), :] = w
            return tuple(st)
        lax.fori_loop(0, 128 // U, bwd, tuple(bend[q0 + j] for j in range(NI)))
    xs = lax.broadcasted_iota(jnp.int32, (128, 128), 0) - 64
    cl = lax.broadcasted_iota(jnp.int32, (128, 128), 1)
    xf = xs.astype(f32)
    xx = xf * xf
    xxh = xx.astype(bf16).astype(f32)
    for y in range(8):
        yv = y - 4.0
        phi = jnp.where(cl == 0, 1.0, jnp.where(cl == 1, xf, jnp.where(cl == 2, yv, jnp.where(cl == 3, xxh, jnp.where(cl == 4, xx - xxh, jnp.where(cl == 5, xf * yv, jnp.where(cl == 6, yv * yv, 0.0)))))))
        phi = phi.astype(bf16)
        rbuf[...] = jnp.zeros((128, 128), f32)
        for c in range(3):
            h, l = r[c][y:y + 1, :].astype(bf16), None
            hf = h.astype(f32)
            rbuf[8 + c:9 + c, :] = hf
            rbuf[11 + c:12 + c, :] = r[c][y:y + 1, :] - hf
        rt = rbuf[...].T.astype(bf16)
        grhsb = acc[1]
        grhsb[y * 512:y * 512 + 128, :] = phi
        grhsb[y * 512 + 128:y * 512 + 256, :] = phi
        grhsb[y * 512 + 256:y * 512 + 384, :] = rt
        grhsb[y * 512 + 384:y * 512 + 512, :] = rt
    accr = acc[0]
    accr[...] = jnp.zeros((256, 128), f32)
    def red(b, _):
        o = jnp.zeros((128, 128), f32)
        for y in range(8):
            base = pl.multiple_of(b * SB, 8) + y * S
            gh, gl = part2(gbuf[pl.ds(base, 128), :])
            wh, wl = part2(wbuf[pl.ds(base, 128), :])
            l = jnp.concatenate([gh, gl, wh, wl], 1)
            o = o + jnp.dot(l, acc[1][y * 512:(y + 1) * 512, :], preferred_element_type=f32)
        rolled = pltpu.roll(o, (b & 7) * 16, 1)
        row = pl.multiple_of((b >> 3) * 128, 128)
        accr[pl.ds(row, 128), :] = accr[pl.ds(row, 128), :] + rolled
        return 0
    lax.fori_loop(0, 16, red, 0)
    m0 = accr[0:128, :].T
    m1 = accr[128:256, :].T
    mt = acc[2]
    for b in range(16):
        src = m0 if b < 8 else m1
        for k in range(14):
            i = (b & 7) * 16 + k
            mt[k, b:b + 1, :] = src[i:i + 1, :]
    M = [mt[k] for k in range(14)]
    M0 = M[0] * LN2
    Mx = M[1] * LN2
    My = M[2] * LN2
    Mxx = (M[3] + M[4]) * LN2
    Mxy = M[5] * LN2
    Myy = M[6] * LN2
    ux = Mx - sxc * M0
    uy = My - syc * M0
    d_a = Mxx - sxc * (Mx + ux)
    d_b = Mxy - syc * Mx - sxc * uy
    d_c = Myy - syc * (My + uy)
    d_sx = -(2.0 * fa * ux + fb * uy)
    d_sy = -(fb * ux + 2.0 * fc * uy)
    return [d_sx, d_sy, d_a, d_b, d_c, M0, M[8] + M[11], M[9] + M[12], M[10] + M[13]]

RENDER_SCRATCH = [
    pltpu.VMEM((16 * SB, 128), f32), pltpu.VMEM((16 * SB, 128), f32), pltpu.VMEM((16 * SB, 128), f32), pltpu.VMEM((16 * SB, 128), f32),
    pltpu.VMEM((1024, 256), bf16), pltpu.VMEM((3, 2048, 128), f32),
    pltpu.VMEM((16, 8, 128), f32), pltpu.VMEM((3, 16, 8, 128), f32), pltpu.VMEM((16, 8, 128), f32),
    pltpu.VMEM((128, 128), f32), pltpu.VMEM((256, 256), f32),
    pltpu.VMEM((256, 128), f32), pltpu.VMEM((4096, 128), bf16), pltpu.VMEM((16, 16, 128), f32),
]

LOG2E = 1.4426950408889634
blur_floor = 0.3
penalty_weight = 0.5
sh_zero = 0.28209479177387814
sh_one = 0.4886025119029199
sh_two = (1.0925484305920792, -1.0925484305920792, 0.31539156525252005, -1.0925484305920792, 0.5462742152960396)
sh_three = (-0.5900435899266435, 2.890611442640554, -0.4570457994644658, 0.3731763325901154, -0.4570457994644658, 1.445305721320277, -0.5900435899266435)
NT = 32
NF = 9
ROWS = 16


def features(rows, cam):
    rot = [[cam[3 * i + j] for j in range(3)] for i in range(3)]
    shift = cam[9:12]
    fx, fy, cx, cy = cam[12:16]
    m = rows[0:3]
    e = [rot[i][0] * m[0] + rot[i][1] * m[1] + rot[i][2] * m[2] + shift[i] for i in range(3)]
    inv = 1.0 / e[2]
    px = e[0] * inv
    py = e[1] * inv
    sx = fx * px + cx
    sy = fy * py + cy
    qn = rows[6] * rows[6] + rows[7] * rows[7] + rows[8] * rows[8] + rows[9] * rows[9]
    qi = 1.0 / jnp.sqrt(qn)
    w, x, y, z = [rows[6 + i] * qi for i in range(4)]
    rq = [
        [1.0 - 2.0 * (y * y + z * z), 2.0 * (x * y - w * z), 2.0 * (x * z + w * y)],
        [2.0 * (x * y + w * z), 1.0 - 2.0 * (x * x + z * z), 2.0 * (y * z - w * x)],
        [2.0 * (x * z - w * y), 2.0 * (y * z + w * x), 1.0 - 2.0 * (x * x + y * y)],
    ]
    sc = [jnp.exp(rows[3 + k]) for k in range(3)]
    mm = [[rq[j][k] * sc[k] for k in range(3)] for j in range(3)]
    ww = [[rot[i][0] * mm[0][k] + rot[i][1] * mm[1][k] + rot[i][2] * mm[2][k] for k in range(3)] for i in range(3)]
    ax, ay = fx * inv, fy * inv
    r1 = [ax * (ww[0][k] - px * ww[2][k]) for k in range(3)]
    r2 = [ay * (ww[1][k] - py * ww[2][k]) for k in range(3)]
    cxx = r1[0] * r1[0] + r1[1] * r1[1] + r1[2] * r1[2] + blur_floor
    cxy = r1[0] * r2[0] + r1[1] * r2[1] + r1[2] * r2[2]
    cyy = r2[0] * r2[0] + r2[1] * r2[1] + r2[2] * r2[2] + blur_floor
    idet = 1.0 / (cxx * cyy - cxy * cxy)
    fa = (-0.5 * LOG2E) * (cyy * idet)
    fb = LOG2E * (cxy * idet)
    fc = (-0.5 * LOG2E) * (cxx * idet)
    lo = (-LOG2E) * jnp.log(1.0 + jnp.exp(-rows[10]))
    eye = [-(rot[0][i] * shift[0] + rot[1][i] * shift[1] + rot[2][i] * shift[2]) for i in range(3)]
    tw = [m[i] - eye[i] for i in range(3)]
    ti = 1.0 / jnp.sqrt(tw[0] * tw[0] + tw[1] * tw[1] + tw[2] * tw[2])
    dx, dy, dz = [t * ti for t in tw]
    xx, yy, zz = dx * dx, dy * dy, dz * dz
    basis = [
        -sh_one * dy, sh_one * dz, -sh_one * dx,
        sh_two[0] * dx * dy, sh_two[1] * dy * dz, sh_two[2] * (2.0 * zz - xx - yy), sh_two[3] * dx * dz, sh_two[4] * (xx - yy),
        sh_three[0] * dy * (3.0 * xx - yy), sh_three[1] * dx * dy * dz, sh_three[2] * dy * (4.0 * zz - xx - yy),
        sh_three[3] * dz * (2.0 * zz - 3.0 * xx - 3.0 * yy), sh_three[4] * dx * (4.0 * zz - xx - yy),
        sh_three[5] * dz * (xx - yy), sh_three[6] * dx * (xx - 3.0 * yy),
    ]
    cols = []
    for c in range(3):
        acc = sh_zero * rows[11 + c] + 0.5
        for k in range(15):
            acc = acc + basis[k] * rows[14 + 3 * k + c]
        cols.append(acc)
    shape = sx.shape
    return [sx, sy, fa, fb, fc, jnp.broadcast_to(lo, shape)] + cols


def camera_columns(cam_ref):
    return [cam_ref[:, j:j + 1] for j in range(16)]


def slot_map(ids_ref, order_ref, count_ref):
    rowi = lax.broadcasted_iota(jnp.int32, (16, 128), 0)
    lane = lax.broadcasted_iota(jnp.int32, (16, 128), 1)
    owner = jnp.full((16, 128), -1, jnp.int32)
    for k in range(16):
        o = order_ref[0, 0, k]
        own = jnp.where(o < count_ref[0, 0], ids_ref[0, 0, o] >> 1, -1)
        owner = jnp.where(rowi == k, own, owner)
    return (owner == lane).astype(f32), jnp.where(owner[:, 0:1] < 0, -1e4, 0.0)


def exchange(me, send, recv, send_sem, recv_sem, n):
    def start(i, _):
        t = lax.rem(me + i, NT)
        pltpu.make_async_remote_copy(send.at[t, pl.ds(0, n)], recv.at[me, pl.ds(0, n)], send_sem.at[t], recv_sem.at[me], device_id={"tile": t}, device_id_type=MESH).start()
        return 0
    lax.fori_loop(1, NT, start, 0)


def finish(me, send, recv, send_sem, recv_sem, n):
    def wait(i, _):
        t = lax.rem(me + i, NT)
        d = pltpu.make_async_remote_copy(send.at[t, pl.ds(0, n)], recv.at[t, pl.ds(0, n)], send_sem.at[t], recv_sem.at[t], device_id={"tile": t}, device_id_type=MESH)
        d.wait_recv()
        d.wait_send()
        return 0
    lax.fori_loop(1, NT, wait, 0)


def spread_kernel(gauss_ref, cam_ref, cid_ref, ids_ref, order_ref, count_ref, feat_ref, bias_ref, col_ref, req, reqs, fbuf, send, recv, s1, r1, s2, r2):
    me = lax.axis_index("tile")
    barrier = pltpu.get_barrier_semaphore()

    def greet(i, _):
        pl.semaphore_signal(barrier, inc=1, device_id={"tile": lax.rem(me + i, NT)}, device_id_type=MESH)
        return 0
    lax.fori_loop(1, NT, greet, 0)
    lane = lax.broadcasted_iota(jnp.int32, (1, 128), 1)
    ask = jnp.full((1, 128), cid_ref[0, 0], jnp.int32)
    for k in range(16):
        b = ids_ref[0, 0, k]
        ask = ask + jnp.where(lane == (b >> 1), (b & 1) * 16, 0)
    for t in range(NT):
        req[t] = ask
    reqs[me] = ask
    pl.semaphore_wait(barrier, NT - 1)
    exchange(me, req, reqs, s1, r1, 1)
    cam = camera_columns(cam_ref)
    for b in range(2):
        rows = [gauss_ref[0, b, i:i + 1, :] for i in range(59)]
        out = features(rows, cam)
        for f in range(NF):
            fbuf[b * 16:(b + 1) * 16, f * 128:(f + 1) * 128] = out[f]
    onehot, bias = slot_map(ids_ref, order_ref, count_ref)
    bias_ref[...] = bias
    finish(me, req, reqs, s1, r1, 1)
    asked = jnp.concatenate([reqs[t] for t in range(NT)], 0)
    lane32 = lax.broadcasted_iota(jnp.int32, (NT, 128), 1)
    col = jnp.sum(jnp.where(lane32 == me, asked, 0).astype(f32), 1, keepdims=True).astype(jnp.int32)
    col_ref[...] = jnp.broadcast_to(col, (NT, 128))
    sel = (col == lax.broadcasted_iota(jnp.int32, (NT, NT), 1)).astype(f32)
    x = jnp.dot(sel, fbuf[...], precision=HI, preferred_element_type=f32)
    for f in range(NF):
        for t in range(NT):
            send[t, f:f + 1, :] = x[t:t + 1, f * 128:(f + 1) * 128]
    recv[me] = send[me]
    exchange(me, send, recv, s2, r2, NF)
    finish(me, send, recv, s2, r2, NF)
    for f in range(NF):
        fbuf[:, f * 128:(f + 1) * 128] = jnp.concatenate([recv[t, f:f + 1, :] for t in range(NT)], 0)
    y = jnp.dot(onehot[:, :NT], fbuf[...], precision=HI, preferred_element_type=f32)
    for f in range(NF):
        feat_ref[f] = y[:, f * 128:(f + 1) * 128]


def render_kernel(f_ref, t_ref, b_ref, o_ref, alpha, wts, gbuf, wbuf, lhs, csp, tb, cb, bend, rbuf, grhs, a0, a1, a2):
    feats = [f_ref[i] for i in range(NF)]
    targ = [jnp.concatenate([t_ref[0, 0, c:c + 1, y * 128:(y + 1) * 128] for y in range(8)], 0) for c in range(3)]
    ybase = (8 * lax.rem(lax.axis_index("tile"), 4)).astype(f32)
    outs = render_body(ybase, feats, targ, b_ref[...], alpha, wts, gbuf, wbuf, lhs, csp, tb, cb, bend, rbuf, grhs, (a0, a1, a2))
    for i in range(NF):
        o_ref[i] = outs[i]


def update_kernel(gauss_ref, cons_ref, dual_ref, step_ref, cam_ref, inter_ref, ids_ref, order_ref, count_ref, gf_ref, col_ref, upd_ref, newd_ref,
                  fbuf, send, recv, grad, vals, near, s2, r2, s3, r3):
    me = lax.axis_index("tile")
    grp = lax.axis_index("scene")
    last = lax.axis_size("scene") - 1
    near[...] = jnp.zeros_like(near)
    barrier = pltpu.get_barrier_semaphore()

    def greet(i, _):
        pl.semaphore_signal(barrier, inc=1, device_id={"tile": lax.rem(me + i, NT)}, device_id_type=MESH)
        return 0
    lax.fori_loop(1, NT, greet, 0)

    @pl.when(grp < last)
    def _():
        pl.semaphore_signal(barrier, inc=1, device_id={"scene": grp + 1}, device_id_type=MESH)

    @pl.when(grp > 0)
    def _():
        pl.semaphore_signal(barrier, inc=1, device_id={"scene": grp - 1}, device_id_type=MESH)
    onehot, _ = slot_map(ids_ref, order_ref, count_ref)
    g16 = jnp.concatenate([gf_ref[f] for f in range(NF)], 1)
    x = lax.dot_general(onehot, g16, (((0,), (0,)), ((), ())), precision=HI, preferred_element_type=f32)
    for f in range(NF):
        for t in range(NT):
            send[t, f:f + 1, :] = x[t:t + 1, f * 128:(f + 1) * 128]
    recv[me] = send[me]
    pl.semaphore_wait(barrier, NT - 1 + jnp.where(grp < last, 1, 0) + jnp.where(grp > 0, 1, 0))
    exchange(me, send, recv, s2, r2, NF)
    sel = (col_ref[:, :NT] == lax.broadcasted_iota(jnp.int32, (NT, NT), 1)).astype(f32)
    finish(me, send, recv, s2, r2, NF)
    for f in range(NF):
        fbuf[:, f * 128:(f + 1) * 128] = jnp.concatenate([recv[t, f:f + 1, :] for t in range(NT)], 0)
    df = lax.dot_general(sel, fbuf[...], (((0,), (0,)), ((), ())), precision=HI, preferred_element_type=f32)
    cam = camera_columns(cam_ref)
    li = lax.broadcasted_iota(jnp.int32, (59, 59), 0)
    lj = lax.broadcasted_iota(jnp.int32, (59, 59), 1)
    step = jnp.sum(jnp.where(li == lj, step_ref[...], 0.0), 1, keepdims=True)
    idx = jnp.concatenate([inter_ref[0, 0, 0:1, :], inter_ref[0, 0, 1:2, :]], 1)
    picks = []
    v = None
    for b in range(2):
        rows = [gauss_ref[0, b, i:i + 1, :] for i in range(59)]
        _, pull = jax.vjp(lambda r: features(r, cam), rows)
        (grows,) = pull([df[b * 16:(b + 1) * 16, f * 128:(f + 1) * 128] for f in range(NF)])
        for i in range(59):
            grad[b, i:i + 1, :] = grows[i]
        gb, db = gauss_ref[0, b], dual_ref[0, b]
        upd = gb - step * (grad[b] + penalty_weight * (gb - cons_ref[0, b] + db))
        upd_ref[0, b] = upd
        pick = (lax.broadcasted_iota(jnp.int32, (128, 128), 0) + b * 128 == idx).astype(f32)
        picks.append(pick)
        p = jnp.dot(upd + db, pick, precision=HI, preferred_element_type=f32)
        v = p if v is None else v + p
    vals[...] = v

    def up():
        return pltpu.make_async_remote_copy(vals, near.at[0], s3.at[0], r3.at[0], device_id={"scene": lax.rem(grp + 1, last + 1)}, device_id_type=MESH)

    def down():
        return pltpu.make_async_remote_copy(vals, near.at[1], s3.at[1], r3.at[1], device_id={"scene": lax.rem(grp + last, last + 1)}, device_id_type=MESH)

    @pl.when(grp < last)
    def _():
        up().start()

    @pl.when(grp > 0)
    def _():
        down().start()

    @pl.when(grp > 0)
    def _():
        up().wait_recv()
        down().wait_send()

    @pl.when(grp < last)
    def _():
        down().wait_recv()
        up().wait_send()
    lane = lax.broadcasted_iota(jnp.int32, (59, 128), 1)
    below = pltpu.roll(near[0], 64, 1)
    above = pltpu.roll(near[1], 64, 1)
    up_d = jnp.where(grp < last, v - above, 0.0)
    down_d = jnp.where(grp > 0, v - below, 0.0)
    diff = 0.5 * jnp.where(lane < 64, up_d, down_d)
    for b in range(2):
        newd_ref[0, b] = lax.dot_general(diff, picks[b], (((1,), (1,)), ((), ())), precision=HI, preferred_element_type=f32)


VM = pl.BlockSpec(memory_space=pltpu.VMEM)
SM = pl.BlockSpec(memory_space=pltpu.SMEM)
DMA = pltpu.SemaphoreType.DMA


def on_device(gaussians, consensus, duals, step_sizes, cameras, camera_ids, block_lists, depth_order, block_counts, targets, intersection):
    def sd(shape, t=f32):
        return jax.ShapeDtypeStruct(shape, t)
    feat, bias, col = pl.pallas_call(
        spread_kernel, name="spread",
        out_shape=(sd((NF, 16, 128)), sd((16, 1)), sd((NT, 128), jnp.int32)),
        in_specs=[VM, VM, SM, SM, SM, SM], out_specs=(VM, VM, VM),
        scratch_shapes=[
            pltpu.VMEM((NT, 1, 128), jnp.int32), pltpu.VMEM((NT, 1, 128), jnp.int32), pltpu.VMEM((NT, NF * 128), f32),
            pltpu.VMEM((NT, ROWS, 128), f32), pltpu.VMEM((NT, ROWS, 128), f32),
            DMA((NT,)), DMA((NT,)), DMA((NT,)), DMA((NT,)),
        ],
        compiler_params=pltpu.CompilerParams(collective_id=0, has_side_effects=True),
    )(gaussians, cameras, camera_ids, block_lists, depth_order, block_counts)
    gf = pl.pallas_call(
        render_kernel, name="render", out_shape=sd((NF, 16, 128)),
        in_specs=[VM, VM, VM], out_specs=VM, scratch_shapes=RENDER_SCRATCH,
        compiler_params=pltpu.CompilerParams(vmem_limit_bytes=60 * 1024 * 1024),
    )(feat, targets, bias)
    return pl.pallas_call(
        update_kernel, name="update",
        out_shape=(sd((1, 2, 59, 128)), sd((1, 2, 59, 128))),
        in_specs=[VM, VM, VM, VM, VM, VM, SM, SM, SM, VM, VM], out_specs=(VM, VM),
        scratch_shapes=[
            pltpu.VMEM((NT, NF * 128), f32), pltpu.VMEM((NT, ROWS, 128), f32), pltpu.VMEM((NT, ROWS, 128), f32),
            pltpu.VMEM((2, 59, 128), f32), pltpu.VMEM((59, 128), f32), pltpu.VMEM((2, 59, 128), f32),
            DMA((NT,)), DMA((NT,)), DMA((2,)), DMA((2,)),
        ],
        compiler_params=pltpu.CompilerParams(collective_id=1, has_side_effects=True),
    )(gaussians, consensus, duals, step_sizes.reshape(1, 59), cameras, intersection, block_lists, depth_order, block_counts, gf, col)


def solution(mesh):
    t4, t3, t2 = P("scene", "tile", None, None), P("scene", "tile", None), P("scene", "tile")
    return jax.shard_map(
        on_device, mesh=mesh,
        in_specs=(t4, t4, t4, P(), P(), t2, t3, t3, t2, t4, t4),
        out_specs=(t4, t4), check_vma=False,
    )
```

```python
import functools

import jax
import jax.numpy as jnp
from jax import lax
from jax.experimental import pallas as pl
from jax.experimental.pallas import tpu as pltpu
from jax.sharding import PartitionSpec as P

HI = lax.Precision.HIGHEST
f32, bf16 = jnp.float32, jnp.bfloat16
MESH = pl.DeviceIdType.MESH
S = 132
SB = 8 * S
NI = 4
LN2 = 0.6931471805599453

def part2(v):
    a = v.astype(bf16)
    return a, (v - a.astype(f32)).astype(bf16)

def part3(v):
    a = v.astype(bf16).astype(f32)
    r = v - a
    b = r.astype(bf16).astype(f32)
    return a, b, (r - b).astype(bf16).astype(f32)

def render_body(ybase, feats, targ, bias, alpha, wts, gbuf, lhs, csp, tb, cb, bend, grhs, acc):
    sx, sy, fa, fb, fc, lo, k0, k1, k2 = feats
    sxc = sx - 64.0
    syc = sy - (ybase + 4.0)
    lob = lo + bias
    zero32 = jnp.zeros((32, 128), f32)
    pa = part3(fa)
    lhs_a = jnp.concatenate(list(pa) + list(pa) + [zero32], 0).T.astype(bf16)
    for y in range(8):
        dy = (y - 4.0) - syc
        c1 = fb * dy - 2.0 * fa * sxc
        c0 = (fa * sxc - fb * dy) * sxc + fc * dy * dy + lob
        m = jnp.concatenate(list(part3(c0)) + list(part3(c1)) + [zero32], 0)
        lhs[y * 128:(y + 1) * 128, 0:128] = m.T.astype(bf16)
        lhs[y * 128:(y + 1) * 128, 128:256] = lhs_a
    colt = jnp.concatenate([k0, k1, k2, jnp.zeros((80, 128), f32)], 0).T
    for c in range(3):
        for b in range(16):
            csp[c, b * 128:(b + 1) * 128, :] = jnp.broadcast_to(colt[:, c * 16 + b:c * 16 + b + 1], (128, 128))
    kr = lax.broadcasted_iota(jnp.int32, (256, 256), 0)
    ln = lax.broadcasted_iota(jnp.int32, (256, 256), 1)
    xi = ((ln & 127) - 64).astype(f32)
    x2 = xi * xi
    x2h = x2.astype(bf16).astype(f32)
    x2l = x2 - x2h
    basis = jnp.where(kr < 48, 1.0, jnp.where(kr < 96, xi, jnp.where(kr < 128, 0.0, jnp.where(kr < 176, x2h, jnp.where(kr < 224, x2l, 0.0)))))
    grhs[...] = basis
    def alpha_pair(p, _):
        rhs = jnp.where((kr & 15) == 2 * p + (ln >> 7), grhs[...], 0.0).astype(bf16)
        for y in range(8):
            e = jnp.dot(lhs[y * 128:(y + 1) * 128, :], rhs, preferred_element_type=f32)
            a = jnp.minimum(0.99, jnp.exp2(e))
            alpha[pl.ds(pl.multiple_of(2 * p * SB, 8) + y * S, 128), :] = a[:, :128]
            alpha[pl.ds(pl.multiple_of((2 * p + 1) * SB, 8) + y * S, 128), :] = a[:, 128:]
        return 0
    lax.fori_loop(0, 8, alpha_pair, 0, unroll=2)
    one = jnp.ones((8, 128), f32)
    zero = jnp.zeros((8, 128), f32)
    U = 8
    for q0 in range(0, 16, NI):
        def fwd(i, carry):
            st = [list(t) for t in carry]
            for u in range(U):
                g = i * U + u
                for j in range(NI):
                    b = q0 + j
                    a = alpha[pl.ds(b * SB + g, 8, stride=S), :]
                    t, s0, s1, s2 = st[j]
                    w = a * t
                    t = t * (1.0 - a)
                    row = b * 128 + g
                    s0 = s0 + w * csp[0, pl.ds(row, 8, stride=0), :]
                    s1 = s1 + w * csp[1, pl.ds(row, 8, stride=0), :]
                    s2 = s2 + w * csp[2, pl.ds(row, 8, stride=0), :]
                    wts[pl.ds(b * SB + g, 8, stride=S), :] = w
                    st[j] = [t, s0, s1, s2]
            return tuple(tuple(t) for t in st)
        out = lax.fori_loop(0, 128 // U, fwd, tuple((one, zero, zero, zero) for _ in range(NI)))
        for j in range(NI):
            tb[q0 + j] = out[j][0]
            for c in range(3):
                cb[c, q0 + j] = out[j][1 + c]
    t = one
    prods = [tb[b] for b in range(16)]
    cs = [zero, zero, zero]
    for b in range(16):
        tb[b] = t
        for c in range(3):
            cs[c] = cs[c] + t * cb[c, b]
        t = t * prods[b]
    r = [cs[c] - targ[c] for c in range(3)]
    e = zero
    for b in range(15, -1, -1):
        bend[b] = e
        e = prods[b] * e + (cb[0, b] * r[0] + cb[1, b] * r[1] + cb[2, b] * r[2])
    for q0 in range(0, 16, NI):
        rs = [[tb[q0 + j] * r[c] for c in range(3)] for j in range(NI)]
        def bwd(i, carry):
            st = list(carry)
            g0 = (128 // U - 1 - i) * U
            for u in range(U - 1, -1, -1):
                g = g0 + u
                for j in range(NI):
                    b = q0 + j
                    a = alpha[pl.ds(b * SB + g, 8, stride=S), :]
                    w = wts[pl.ds(b * SB + g, 8, stride=S), :]
                    row = b * 128 + g
                    q = (rs[j][0] * csp[0, pl.ds(row, 8, stride=0), :] + rs[j][1] * csp[1, pl.ds(row, 8, stride=0), :]) + rs[j][2] * csp[2, pl.ds(row, 8, stride=0), :]
                    d = q - st[j]
                    gbuf[pl.ds(b * SB + g, 8, stride=S), :] = jnp.where(a < 0.99, w * d, 0.0)
                    st[j] = st[j] + a * d
            return tuple(st)
        lax.fori_loop(0, 128 // U, bwd, tuple(tb[q0 + j] * bend[q0 + j] for j in range(NI)))
    xf = (lax.broadcasted_iota(jnp.int32, (16, 128), 1) - 64).astype(f32)
    kk = lax.broadcasted_iota(jnp.int32, (16, 128), 0)
    xx = xf * xf
    xxh = xx.astype(bf16).astype(f32)
    mt, phi, rb = acc
    for y in range(8):
        yv = y - 4.0
        p = jnp.where(kk == 0, 1.0, jnp.where(kk == 1, xf, jnp.where(kk == 2, yv, jnp.where(kk == 3, xxh, jnp.where(kk == 4, xx - xxh, jnp.where(kk == 5, xf * yv, jnp.where(kk == 6, yv * yv, 0.0)))))))
        p = p.astype(bf16)
        phi[:, y * 256:y * 256 + 128] = p
        phi[:, y * 256 + 128:y * 256 + 256] = p
        q = jnp.zeros((16, 128), f32)
        for c in range(3):
            v = r[c][y:y + 1, :]
            h = v.astype(bf16).astype(f32)
            q = jnp.where(kk == 8 + c, h, jnp.where(kk == 11 + c, v - h, q))
        q = q.astype(bf16)
        rb[:, y * 256:y * 256 + 128] = q
        rb[:, y * 256 + 128:y * 256 + 256] = q
    nt = (((1,), (1,)), ((), ()))
    def red(b, _):
        o = jnp.zeros((16, 128), f32)
        tbb = tb[b]
        for y in range(8):
            base = pl.multiple_of(b * SB, 8) + y * S
            o = o + lax.dot_general(phi[:, y * 256:(y + 1) * 256], jnp.concatenate(part2(gbuf[pl.ds(base, 128), :]), 1), nt, preferred_element_type=f32)
            o = o + lax.dot_general(rb[:, y * 256:(y + 1) * 256], jnp.concatenate(part2(wts[pl.ds(base, 128), :] * tbb[y:y + 1, :]), 1), nt, preferred_element_type=f32)
        mt[b] = o
        return 0
    lax.fori_loop(0, 16, red, 0)
    rowb = lax.broadcasted_iota(jnp.int32, (16, 128), 0)
    def pick(k):
        v = jnp.zeros((16, 128), f32)
        for b in range(16):
            v = jnp.where(rowb == b, mt[b][k:k + 1, :], v)
        return v
    M = [pick(k) for k in range(14)]
    M0 = M[0] * LN2
    Mx = M[1] * LN2
    My = M[2] * LN2
    Mxx = (M[3] + M[4]) * LN2
    Mxy = M[5] * LN2
    Myy = M[6] * LN2
    ux = Mx - sxc * M0
    uy = My - syc * M0
    d_a = Mxx - sxc * (Mx + ux)
    d_b = Mxy - syc * Mx - sxc * uy
    d_c = Myy - syc * (My + uy)
    d_sx = -(2.0 * fa * ux + fb * uy)
    d_sy = -(fb * ux + 2.0 * fc * uy)
    return [d_sx, d_sy, d_a, d_b, d_c, M0, M[8] + M[11], M[9] + M[12], M[10] + M[13]]

RENDER_SCRATCH = [
    pltpu.VMEM((16 * SB, 128), f32), pltpu.VMEM((16 * SB, 128), f32), pltpu.VMEM((16 * SB, 128), f32),
    pltpu.VMEM((1024, 256), bf16), pltpu.VMEM((3, 2048, 128), f32),
    pltpu.VMEM((16, 8, 128), f32), pltpu.VMEM((3, 16, 8, 128), f32), pltpu.VMEM((16, 8, 128), f32),
    pltpu.VMEM((256, 256), f32),
    pltpu.VMEM((16, 16, 128), f32), pltpu.VMEM((16, 2048), bf16), pltpu.VMEM((16, 2048), bf16),
]

LOG2E = 1.4426950408889634
blur_floor = 0.3
penalty_weight = 0.5
sh_zero = 0.28209479177387814
sh_one = 0.4886025119029199
sh_two = (1.0925484305920792, -1.0925484305920792, 0.31539156525252005, -1.0925484305920792, 0.5462742152960396)
sh_three = (-0.5900435899266435, 2.890611442640554, -0.4570457994644658, 0.3731763325901154, -0.4570457994644658, 1.445305721320277, -0.5900435899266435)
NT = 32
NF = 9
ROWS = 16


def features(rows, cam):
    rot = [[cam[3 * i + j] for j in range(3)] for i in range(3)]
    shift = cam[9:12]
    fx, fy, cx, cy = cam[12:16]
    m = rows[0:3]
    e = [rot[i][0] * m[0] + rot[i][1] * m[1] + rot[i][2] * m[2] + shift[i] for i in range(3)]
    inv = 1.0 / e[2]
    px = e[0] * inv
    py = e[1] * inv
    sx = fx * px + cx
    sy = fy * py + cy
    qn = rows[6] * rows[6] + rows[7] * rows[7] + rows[8] * rows[8] + rows[9] * rows[9]
    qi = 1.0 / jnp.sqrt(qn)
    w, x, y, z = [rows[6 + i] * qi for i in range(4)]
    rq = [
        [1.0 - 2.0 * (y * y + z * z), 2.0 * (x * y - w * z), 2.0 * (x * z + w * y)],
        [2.0 * (x * y + w * z), 1.0 - 2.0 * (x * x + z * z), 2.0 * (y * z - w * x)],
        [2.0 * (x * z - w * y), 2.0 * (y * z + w * x), 1.0 - 2.0 * (x * x + y * y)],
    ]
    sc = [jnp.exp(rows[3 + k]) for k in range(3)]
    mm = [[rq[j][k] * sc[k] for k in range(3)] for j in range(3)]
    ww = [[rot[i][0] * mm[0][k] + rot[i][1] * mm[1][k] + rot[i][2] * mm[2][k] for k in range(3)] for i in range(3)]
    ax, ay = fx * inv, fy * inv
    r1 = [ax * (ww[0][k] - px * ww[2][k]) for k in range(3)]
    r2 = [ay * (ww[1][k] - py * ww[2][k]) for k in range(3)]
    cxx = r1[0] * r1[0] + r1[1] * r1[1] + r1[2] * r1[2] + blur_floor
    cxy = r1[0] * r2[0] + r1[1] * r2[1] + r1[2] * r2[2]
    cyy = r2[0] * r2[0] + r2[1] * r2[1] + r2[2] * r2[2] + blur_floor
    idet = 1.0 / (cxx * cyy - cxy * cxy)
    fa = (-0.5 * LOG2E) * (cyy * idet)
    fb = LOG2E * (cxy * idet)
    fc = (-0.5 * LOG2E) * (cxx * idet)
    lo = (-LOG2E) * jnp.log(1.0 + jnp.exp(-rows[10]))
    eye = [-(rot[0][i] * shift[0] + rot[1][i] * shift[1] + rot[2][i] * shift[2]) for i in range(3)]
    tw = [m[i] - eye[i] for i in range(3)]
    ti = 1.0 / jnp.sqrt(tw[0] * tw[0] + tw[1] * tw[1] + tw[2] * tw[2])
    dx, dy, dz = [t * ti for t in tw]
    xx, yy, zz = dx * dx, dy * dy, dz * dz
    basis = [
        -sh_one * dy, sh_one * dz, -sh_one * dx,
        sh_two[0] * dx * dy, sh_two[1] * dy * dz, sh_two[2] * (2.0 * zz - xx - yy), sh_two[3] * dx * dz, sh_two[4] * (xx - yy),
        sh_three[0] * dy * (3.0 * xx - yy), sh_three[1] * dx * dy * dz, sh_three[2] * dy * (4.0 * zz - xx - yy),
        sh_three[3] * dz * (2.0 * zz - 3.0 * xx - 3.0 * yy), sh_three[4] * dx * (4.0 * zz - xx - yy),
        sh_three[5] * dz * (xx - yy), sh_three[6] * dx * (xx - 3.0 * yy),
    ]
    cols = []
    for c in range(3):
        acc = sh_zero * rows[11 + c] + 0.5
        for k in range(15):
            acc = acc + basis[k] * rows[14 + 3 * k + c]
        cols.append(acc)
    shape = sx.shape
    return [sx, sy, fa, fb, fc, jnp.broadcast_to(lo, shape)] + cols


def camera_columns(cam_ref):
    return [cam_ref[:, j:j + 1] for j in range(16)]


def slot_map(ids_ref, order_ref, count_ref):
    rowi = lax.broadcasted_iota(jnp.int32, (16, 128), 0)
    lane = lax.broadcasted_iota(jnp.int32, (16, 128), 1)
    owner = jnp.full((16, 128), -1, jnp.int32)
    for k in range(16):
        o = order_ref[0, 0, k]
        own = jnp.where(o < count_ref[0, 0], ids_ref[0, 0, o] >> 1, -1)
        owner = jnp.where(rowi == k, own, owner)
    return (owner == lane).astype(f32), jnp.where(owner[:, 0:1] < 0, -1e4, 0.0)


def exchange(me, send, recv, send_sem, recv_sem, n):
    def start(i, _):
        t = lax.rem(me + i, NT)
        pltpu.make_async_remote_copy(send.at[t, pl.ds(0, n)], recv.at[me, pl.ds(0, n)], send_sem.at[t], recv_sem.at[me], device_id={"tile": t}, device_id_type=MESH).start()
        return 0
    lax.fori_loop(1, NT, start, 0)


def finish(me, send, recv, send_sem, recv_sem, n):
    def wait(i, _):
        t = lax.rem(me + i, NT)
        d = pltpu.make_async_remote_copy(send.at[t, pl.ds(0, n)], recv.at[t, pl.ds(0, n)], send_sem.at[t], recv_sem.at[t], device_id={"tile": t}, device_id_type=MESH)
        d.wait_recv()
        d.wait_send()
        return 0
    lax.fori_loop(1, NT, wait, 0)


def spread_kernel(gauss_ref, cam_ref, cid_ref, ids_ref, order_ref, count_ref, feat_ref, bias_ref, col_ref, req, reqs, fbuf, send, recv, s1, r1, s2, r2):
    me = lax.axis_index("tile")
    barrier = pltpu.get_barrier_semaphore()

    def greet(i, _):
        pl.semaphore_signal(barrier, inc=1, device_id={"tile": lax.rem(me + i, NT)}, device_id_type=MESH)
        return 0
    lax.fori_loop(1, NT, greet, 0)
    lane = lax.broadcasted_iota(jnp.int32, (1, 128), 1)
    ask = jnp.full((1, 128), cid_ref[0, 0], jnp.int32)
    for k in range(16):
        b = ids_ref[0, 0, k]
        ask = ask + jnp.where(lane == (b >> 1), (b & 1) * 16, 0)
    for t in range(NT):
        req[t] = ask
    reqs[me] = ask
    pl.semaphore_wait(barrier, NT - 1)
    exchange(me, req, reqs, s1, r1, 1)
    cam = camera_columns(cam_ref)
    for b in range(2):
        rows = [gauss_ref[0, i, b:b + 1, :] for i in range(59)]
        out = features(rows, cam)
        for f in range(NF):
            fbuf[b * 16:(b + 1) * 16, f * 128:(f + 1) * 128] = out[f]
    onehot, bias = slot_map(ids_ref, order_ref, count_ref)
    bias_ref[...] = bias
    finish(me, req, reqs, s1, r1, 1)
    asked = jnp.concatenate([reqs[t] for t in range(NT)], 0)
    lane32 = lax.broadcasted_iota(jnp.int32, (NT, 128), 1)
    col = jnp.sum(jnp.where(lane32 == me, asked, 0).astype(f32), 1, keepdims=True).astype(jnp.int32)
    col_ref[...] = jnp.broadcast_to(col, (NT, 128))
    sel = (col == lax.broadcasted_iota(jnp.int32, (NT, NT), 1)).astype(f32)
    x = jnp.dot(sel, fbuf[...], precision=HI, preferred_element_type=f32)
    for f in range(NF):
        for t in range(NT):
            send[t, f:f + 1, :] = x[t:t + 1, f * 128:(f + 1) * 128]
    recv[me] = send[me]
    exchange(me, send, recv, s2, r2, NF)
    finish(me, send, recv, s2, r2, NF)
    for f in range(NF):
        fbuf[:, f * 128:(f + 1) * 128] = jnp.concatenate([recv[t, f:f + 1, :] for t in range(NT)], 0)
    y = jnp.dot(onehot[:, :NT], fbuf[...], precision=HI, preferred_element_type=f32)
    for f in range(NF):
        feat_ref[f] = y[:, f * 128:(f + 1) * 128]


def render_kernel(f_ref, t_ref, b_ref, o_ref, alpha, wts, gbuf, lhs, csp, tb, cb, bend, grhs, a0, a1, a2):
    feats = [f_ref[i] for i in range(NF)]
    targ = [jnp.concatenate([t_ref[0, c, 0:1, y * 128:(y + 1) * 128] for y in range(8)], 0) for c in range(3)]
    ybase = (8 * lax.rem(lax.axis_index("tile"), 4)).astype(f32)
    outs = render_body(ybase, feats, targ, b_ref[...], alpha, wts, gbuf, lhs, csp, tb, cb, bend, grhs, (a0, a1, a2))
    for i in range(NF):
        o_ref[i] = outs[i]


def update_kernel(gauss_ref, cons_ref, dual_ref, step_ref, cam_ref, inter_ref, ids_ref, order_ref, count_ref, gf_ref, col_ref, upd_ref, newd_ref,
                  fbuf, send, recv, grad, vals, near, s2, r2, s3, r3):
    me = lax.axis_index("tile")
    grp = lax.axis_index("scene")
    last = lax.axis_size("scene") - 1
    near[...] = jnp.zeros_like(near)
    barrier = pltpu.get_barrier_semaphore()

    def greet(i, _):
        pl.semaphore_signal(barrier, inc=1, device_id={"tile": lax.rem(me + i, NT)}, device_id_type=MESH)
        return 0
    lax.fori_loop(1, NT, greet, 0)

    @pl.when(grp < last)
    def _():
        pl.semaphore_signal(barrier, inc=1, device_id={"scene": grp + 1}, device_id_type=MESH)

    @pl.when(grp > 0)
    def _():
        pl.semaphore_signal(barrier, inc=1, device_id={"scene": grp - 1}, device_id_type=MESH)
    onehot, _ = slot_map(ids_ref, order_ref, count_ref)
    g16 = jnp.concatenate([gf_ref[f] for f in range(NF)], 1)
    x = lax.dot_general(onehot, g16, (((0,), (0,)), ((), ())), precision=HI, preferred_element_type=f32)
    for f in range(NF):
        for t in range(NT):
            send[t, f:f + 1, :] = x[t:t + 1, f * 128:(f + 1) * 128]
    recv[me] = send[me]
    pl.semaphore_wait(barrier, NT - 1 + jnp.where(grp < last, 1, 0) + jnp.where(grp > 0, 1, 0))
    exchange(me, send, recv, s2, r2, NF)
    sel = (col_ref[:, :NT] == lax.broadcasted_iota(jnp.int32, (NT, NT), 1)).astype(f32)
    finish(me, send, recv, s2, r2, NF)
    for f in range(NF):
        fbuf[:, f * 128:(f + 1) * 128] = jnp.concatenate([recv[t, f:f + 1, :] for t in range(NT)], 0)
    df = lax.dot_general(sel, fbuf[...], (((0,), (0,)), ((), ())), precision=HI, preferred_element_type=f32)
    cam = camera_columns(cam_ref)
    idx = jnp.concatenate([inter_ref[0, 0, 0:1, :], inter_ref[0, 0, 1:2, :]], 1)
    for b in range(2):
        rows = [gauss_ref[0, i, b:b + 1, :] for i in range(59)]
        _, pull = jax.vjp(lambda r: features(r, cam), rows)
        (grows,) = pull([df[b * 16:(b + 1) * 16, f * 128:(f + 1) * 128] for f in range(NF)])
        for i in range(59):
            d = dual_ref[0, i, b:b + 1, :]
            u = rows[i] - step_ref[i] * (grows[i] + penalty_weight * (rows[i] - cons_ref[0, i, b:b + 1, :] + d))
            upd_ref[0, i, b:b + 1, :] = u
            grad[b, i:i + 1, :] = u + d
    picks = [(lax.broadcasted_iota(jnp.int32, (128, 128), 0) + b * 128 == idx).astype(f32) for b in range(2)]
    v = sum(jnp.dot(grad[b], picks[b], precision=HI, preferred_element_type=f32) for b in range(2))
    vals[...] = v

    def up():
        return pltpu.make_async_remote_copy(vals, near.at[0], s3.at[0], r3.at[0], device_id={"scene": lax.rem(grp + 1, last + 1)}, device_id_type=MESH)

    def down():
        return pltpu.make_async_remote_copy(vals, near.at[1], s3.at[1], r3.at[1], device_id={"scene": lax.rem(grp + last, last + 1)}, device_id_type=MESH)

    @pl.when(grp < last)
    def _():
        up().start()

    @pl.when(grp > 0)
    def _():
        down().start()

    @pl.when(grp > 0)
    def _():
        up().wait_recv()
        down().wait_send()

    @pl.when(grp < last)
    def _():
        down().wait_recv()
        up().wait_send()
    lane = lax.broadcasted_iota(jnp.int32, (59, 128), 1)
    below = pltpu.roll(near[0], 64, 1)
    above = pltpu.roll(near[1], 64, 1)
    up_d = jnp.where(grp < last, v - above, 0.0)
    down_d = jnp.where(grp > 0, v - below, 0.0)
    diff = 0.5 * jnp.where(lane < 64, up_d, down_d)
    for b in range(2):
        nd = lax.dot_general(diff, picks[b], (((1,), (1,)), ((), ())), precision=HI, preferred_element_type=f32)
        for i in range(59):
            newd_ref[0, i, b:b + 1, :] = nd[i:i + 1, :]


VM = pl.BlockSpec(memory_space=pltpu.VMEM)
SM = pl.BlockSpec(memory_space=pltpu.SMEM)
DMA = pltpu.SemaphoreType.DMA


def on_device(gaussians, consensus, duals, step_sizes, cameras, camera_ids, block_lists, depth_order, block_counts, targets, intersection):
    def sd(shape, t=f32):
        return jax.ShapeDtypeStruct(shape, t)
    gaussians, consensus, duals, targets = [a.transpose(0, 2, 1, 3) for a in (gaussians, consensus, duals, targets)]
    feat, bias, col = pl.pallas_call(
        spread_kernel, name="spread",
        out_shape=(sd((NF, 16, 128)), sd((16, 1)), sd((NT, 128), jnp.int32)),
        in_specs=[VM, VM, SM, SM, SM, SM], out_specs=(VM, VM, VM),
        scratch_shapes=[
            pltpu.VMEM((NT, 1, 128), jnp.int32), pltpu.VMEM((NT, 1, 128), jnp.int32), pltpu.VMEM((NT, NF * 128), f32),
            pltpu.VMEM((NT, ROWS, 128), f32), pltpu.VMEM((NT, ROWS, 128), f32),
            DMA((NT,)), DMA((NT,)), DMA((NT,)), DMA((NT,)),
        ],
        compiler_params=pltpu.CompilerParams(collective_id=0, has_side_effects=True),
    )(gaussians, cameras, camera_ids, block_lists, depth_order, block_counts)
    gf = pl.pallas_call(
        render_kernel, name="render", out_shape=sd((NF, 16, 128)),
        in_specs=[VM, VM, VM], out_specs=VM, scratch_shapes=RENDER_SCRATCH,
        compiler_params=pltpu.CompilerParams(vmem_limit_bytes=60 * 1024 * 1024),
    )(feat, targets, bias)
    out = pl.pallas_call(
        update_kernel, name="update",
        out_shape=(sd((1, 59, 2, 128)), sd((1, 59, 2, 128))),
        in_specs=[VM, VM, VM, SM, VM, VM, SM, SM, SM, VM, VM], out_specs=(VM, VM),
        scratch_shapes=[
            pltpu.VMEM((NT, NF * 128), f32), pltpu.VMEM((NT, ROWS, 128), f32), pltpu.VMEM((NT, ROWS, 128), f32),
            pltpu.VMEM((2, 59, 128), f32), pltpu.VMEM((59, 128), f32), pltpu.VMEM((2, 59, 128), f32),
            DMA((NT,)), DMA((NT,)), DMA((2,)), DMA((2,)),
        ],
        compiler_params=pltpu.CompilerParams(collective_id=1, has_side_effects=True),
    )(gaussians, consensus, duals, step_sizes, cameras, intersection, block_lists, depth_order, block_counts, gf, col)
    return tuple(a.transpose(0, 2, 1, 3) for a in out)


def solution(mesh):
    t4, t3, t2 = P("scene", "tile", None, None), P("scene", "tile", None), P("scene", "tile")
    return jax.shard_map(
        on_device, mesh=mesh,
        in_specs=(t4, t4, t4, P(), P(), t2, t3, t3, t2, t4, t4),
        out_specs=(t4, t4), check_vma=False,
    )
```

```python
import functools

import jax
import jax.numpy as jnp
from jax import lax
from jax.experimental import pallas as pl
from jax.experimental.pallas import tpu as pltpu
from jax.sharding import PartitionSpec as P

HI = lax.Precision.HIGHEST
f32, bf16 = jnp.float32, jnp.bfloat16
MESH = pl.DeviceIdType.MESH
S = 132
SB = 8 * S
NI = 4
LN2 = 0.6931471805599453

def part2(v):
    a = v.astype(bf16)
    return a, (v - a.astype(f32)).astype(bf16)

def part3(v):
    a = v.astype(bf16).astype(f32)
    r = v - a
    b = r.astype(bf16).astype(f32)
    return a, b, (r - b).astype(bf16).astype(f32)

def render_body(ybase, feats, targ, bias, alpha, wts, gbuf, lhs, csp, tb, cb, bend, grhs, acc):
    sx, sy, fa, fb, fc, lo, k0, k1, k2 = feats
    sxc = sx - 64.0
    syc = sy - (ybase + 4.0)
    lob = lo + bias
    zero32 = jnp.zeros((32, 128), f32)
    pa = part3(fa)
    lhs_a = jnp.concatenate(list(pa) + list(pa) + [zero32], 0).T.astype(bf16)
    for y in range(8):
        dy = (y - 4.0) - syc
        c1 = fb * dy - 2.0 * fa * sxc
        c0 = (fa * sxc - fb * dy) * sxc + fc * dy * dy + lob
        m = jnp.concatenate(list(part3(c0)) + list(part3(c1)) + [zero32], 0)
        lhs[y * 128:(y + 1) * 128, 0:128] = m.T.astype(bf16)
        lhs[y * 128:(y + 1) * 128, 128:256] = lhs_a
    colt = jnp.concatenate([k0, k1, k2, jnp.zeros((80, 128), f32)], 0).T
    for c in range(3):
        for b in range(16):
            csp[c, b * 128:(b + 1) * 128, :] = jnp.broadcast_to(colt[:, c * 16 + b:c * 16 + b + 1], (128, 128))
    kr = lax.broadcasted_iota(jnp.int32, (256, 256), 0)
    ln = lax.broadcasted_iota(jnp.int32, (256, 256), 1)
    xi = ((ln & 127) - 64).astype(f32)
    x2 = xi * xi
    x2h = x2.astype(bf16).astype(f32)
    x2l = x2 - x2h
    basis = jnp.where(kr < 48, 1.0, jnp.where(kr < 96, xi, jnp.where(kr < 128, 0.0, jnp.where(kr < 176, x2h, jnp.where(kr < 224, x2l, 0.0)))))
    grhs[...] = basis
    def alpha_pair(p, _):
        rhs = jnp.where((kr & 15) == 2 * p + (ln >> 7), grhs[...], 0.0).astype(bf16)
        for y in range(8):
            e = jnp.dot(lhs[y * 128:(y + 1) * 128, :], rhs, preferred_element_type=f32)
            a = jnp.minimum(0.99, jnp.exp2(e))
            alpha[pl.ds(pl.multiple_of(2 * p * SB, 8) + y * S, 128), :] = a[:, :128]
            alpha[pl.ds(pl.multiple_of((2 * p + 1) * SB, 8) + y * S, 128), :] = a[:, 128:]
        return 0
    lax.fori_loop(0, 8, alpha_pair, 0, unroll=2)
    one = jnp.ones((8, 128), f32)
    zero = jnp.zeros((8, 128), f32)
    U = 8
    for q0 in range(0, 16, NI):
        def fwd(i, carry):
            st = [list(t) for t in carry]
            for u in range(U):
                g = i * U + u
                for j in range(NI):
                    b = q0 + j
                    a = alpha[pl.ds(b * SB + g, 8, stride=S), :]
                    t, s0, s1, s2 = st[j]
                    w = a * t
                    t = t * (1.0 - a)
                    row = b * 128 + g
                    s0 = s0 + w * csp[0, pl.ds(row, 8, stride=0), :]
                    s1 = s1 + w * csp[1, pl.ds(row, 8, stride=0), :]
                    s2 = s2 + w * csp[2, pl.ds(row, 8, stride=0), :]
                    wts[pl.ds(b * SB + g, 8, stride=S), :] = w
                    st[j] = [t, s0, s1, s2]
            return tuple(tuple(t) for t in st)
        out = lax.fori_loop(0, 128 // U, fwd, tuple((one, zero, zero, zero) for _ in range(NI)))
        for j in range(NI):
            tb[q0 + j] = out[j][0]
            for c in range(3):
                cb[c, q0 + j] = out[j][1 + c]
    t = one
    prods = [tb[b] for b in range(16)]
    cs = [zero, zero, zero]
    for b in range(16):
        tb[b] = t
        for c in range(3):
            cs[c] = cs[c] + t * cb[c, b]
        t = t * prods[b]
    r = [cs[c] - targ[c] for c in range(3)]
    e = zero
    for b in range(15, -1, -1):
        bend[b] = e
        e = prods[b] * e + (cb[0, b] * r[0] + cb[1, b] * r[1] + cb[2, b] * r[2])
    for q0 in range(0, 16, NI):
        rs = [[tb[q0 + j] * r[c] for c in range(3)] for j in range(NI)]
        def bwd(i, carry):
            st = list(carry)
            g0 = (128 // U - 1 - i) * U
            for u in range(U - 1, -1, -1):
                g = g0 + u
                for j in range(NI):
                    b = q0 + j
                    a = alpha[pl.ds(b * SB + g, 8, stride=S), :]
                    w = wts[pl.ds(b * SB + g, 8, stride=S), :]
                    row = b * 128 + g
                    q = (rs[j][0] * csp[0, pl.ds(row, 8, stride=0), :] + rs[j][1] * csp[1, pl.ds(row, 8, stride=0), :]) + rs[j][2] * csp[2, pl.ds(row, 8, stride=0), :]
                    d = q - st[j]
                    gbuf[pl.ds(b * SB + g, 8, stride=S), :] = jnp.where(a < 0.99, w * d, 0.0)
                    st[j] = st[j] + a * d
            return tuple(st)
        lax.fori_loop(0, 128 // U, bwd, tuple(tb[q0 + j] * bend[q0 + j] for j in range(NI)))
    xf = (lax.broadcasted_iota(jnp.int32, (16, 128), 1) - 64).astype(f32)
    kk = lax.broadcasted_iota(jnp.int32, (16, 128), 0)
    xx = xf * xf
    xxh = xx.astype(bf16).astype(f32)
    mt, phi, rb = acc
    for y in range(8):
        yv = y - 4.0
        p = jnp.where(kk == 0, 1.0, jnp.where(kk == 1, xf, jnp.where(kk == 2, yv, jnp.where(kk == 3, xxh, jnp.where(kk == 4, xx - xxh, jnp.where(kk == 5, xf * yv, jnp.where(kk == 6, yv * yv, 0.0)))))))
        p = p.astype(bf16)
        phi[:, y * 256:y * 256 + 128] = p
        phi[:, y * 256 + 128:y * 256 + 256] = p
        q = jnp.zeros((16, 128), f32)
        for c in range(3):
            v = r[c][y:y + 1, :]
            h = v.astype(bf16).astype(f32)
            q = jnp.where(kk == 8 + c, h, jnp.where(kk == 11 + c, v - h, q))
        q = q.astype(bf16)
        rb[:, y * 256:y * 256 + 128] = q
        rb[:, y * 256 + 128:y * 256 + 256] = q
    nt = (((1,), (1,)), ((), ()))
    def red(b, _):
        o = jnp.zeros((16, 128), f32)
        tbb = tb[b]
        for y in range(8):
            base = pl.multiple_of(b * SB, 8) + y * S
            o = o + lax.dot_general(phi[:, y * 256:(y + 1) * 256], jnp.concatenate(part2(gbuf[pl.ds(base, 128), :]), 1), nt, preferred_element_type=f32)
            o = o + lax.dot_general(rb[:, y * 256:(y + 1) * 256], jnp.concatenate(part2(wts[pl.ds(base, 128), :] * tbb[y:y + 1, :]), 1), nt, preferred_element_type=f32)
        mt[b] = o
        return 0
    lax.fori_loop(0, 16, red, 0)
    rowb = lax.broadcasted_iota(jnp.int32, (16, 128), 0)
    def pick(k):
        v = jnp.zeros((16, 128), f32)
        for b in range(16):
            v = jnp.where(rowb == b, mt[b][k:k + 1, :], v)
        return v
    M = [pick(k) for k in range(14)]
    M0 = M[0] * LN2
    Mx = M[1] * LN2
    My = M[2] * LN2
    Mxx = (M[3] + M[4]) * LN2
    Mxy = M[5] * LN2
    Myy = M[6] * LN2
    ux = Mx - sxc * M0
    uy = My - syc * M0
    d_a = Mxx - sxc * (Mx + ux)
    d_b = Mxy - syc * Mx - sxc * uy
    d_c = Myy - syc * (My + uy)
    d_sx = -(2.0 * fa * ux + fb * uy)
    d_sy = -(fb * ux + 2.0 * fc * uy)
    return [d_sx, d_sy, d_a, d_b, d_c, M0, M[8] + M[11], M[9] + M[12], M[10] + M[13]]

RENDER_SCRATCH = [
    pltpu.VMEM((16 * SB, 128), f32), pltpu.VMEM((16 * SB, 128), f32), pltpu.VMEM((16 * SB, 128), f32),
    pltpu.VMEM((1024, 256), bf16), pltpu.VMEM((3, 2048, 128), f32),
    pltpu.VMEM((16, 8, 128), f32), pltpu.VMEM((3, 16, 8, 128), f32), pltpu.VMEM((16, 8, 128), f32),
    pltpu.VMEM((256, 256), f32),
    pltpu.VMEM((16, 16, 128), f32), pltpu.VMEM((16, 2048), bf16), pltpu.VMEM((16, 2048), bf16),
]

LOG2E = 1.4426950408889634
blur_floor = 0.3
penalty_weight = 0.5
sh_zero = 0.28209479177387814
sh_one = 0.4886025119029199
sh_two = (1.0925484305920792, -1.0925484305920792, 0.31539156525252005, -1.0925484305920792, 0.5462742152960396)
sh_three = (-0.5900435899266435, 2.890611442640554, -0.4570457994644658, 0.3731763325901154, -0.4570457994644658, 1.445305721320277, -0.5900435899266435)
NT = 32
NF = 9
ROWS = 16


def features(rows, cam):
    rot = [[cam[3 * i + j] for j in range(3)] for i in range(3)]
    shift = cam[9:12]
    fx, fy, cx, cy = cam[12:16]
    m = rows[0:3]
    e = [rot[i][0] * m[0] + rot[i][1] * m[1] + rot[i][2] * m[2] + shift[i] for i in range(3)]
    inv = 1.0 / e[2]
    px = e[0] * inv
    py = e[1] * inv
    sx = fx * px + cx
    sy = fy * py + cy
    qn = rows[6] * rows[6] + rows[7] * rows[7] + rows[8] * rows[8] + rows[9] * rows[9]
    qi = 1.0 / jnp.sqrt(qn)
    w, x, y, z = [rows[6 + i] * qi for i in range(4)]
    rq = [
        [1.0 - 2.0 * (y * y + z * z), 2.0 * (x * y - w * z), 2.0 * (x * z + w * y)],
        [2.0 * (x * y + w * z), 1.0 - 2.0 * (x * x + z * z), 2.0 * (y * z - w * x)],
        [2.0 * (x * z - w * y), 2.0 * (y * z + w * x), 1.0 - 2.0 * (x * x + y * y)],
    ]
    sc = [jnp.exp(rows[3 + k]) for k in range(3)]
    mm = [[rq[j][k] * sc[k] for k in range(3)] for j in range(3)]
    ww = [[rot[i][0] * mm[0][k] + rot[i][1] * mm[1][k] + rot[i][2] * mm[2][k] for k in range(3)] for i in range(3)]
    ax, ay = fx * inv, fy * inv
    r1 = [ax * (ww[0][k] - px * ww[2][k]) for k in range(3)]
    r2 = [ay * (ww[1][k] - py * ww[2][k]) for k in range(3)]
    cxx = r1[0] * r1[0] + r1[1] * r1[1] + r1[2] * r1[2] + blur_floor
    cxy = r1[0] * r2[0] + r1[1] * r2[1] + r1[2] * r2[2]
    cyy = r2[0] * r2[0] + r2[1] * r2[1] + r2[2] * r2[2] + blur_floor
    idet = 1.0 / (cxx * cyy - cxy * cxy)
    fa = (-0.5 * LOG2E) * (cyy * idet)
    fb = LOG2E * (cxy * idet)
    fc = (-0.5 * LOG2E) * (cxx * idet)
    lo = (-LOG2E) * jnp.log(1.0 + jnp.exp(-rows[10]))
    eye = [-(rot[0][i] * shift[0] + rot[1][i] * shift[1] + rot[2][i] * shift[2]) for i in range(3)]
    tw = [m[i] - eye[i] for i in range(3)]
    ti = 1.0 / jnp.sqrt(tw[0] * tw[0] + tw[1] * tw[1] + tw[2] * tw[2])
    dx, dy, dz = [t * ti for t in tw]
    xx, yy, zz = dx * dx, dy * dy, dz * dz
    basis = [
        -sh_one * dy, sh_one * dz, -sh_one * dx,
        sh_two[0] * dx * dy, sh_two[1] * dy * dz, sh_two[2] * (2.0 * zz - xx - yy), sh_two[3] * dx * dz, sh_two[4] * (xx - yy),
        sh_three[0] * dy * (3.0 * xx - yy), sh_three[1] * dx * dy * dz, sh_three[2] * dy * (4.0 * zz - xx - yy),
        sh_three[3] * dz * (2.0 * zz - 3.0 * xx - 3.0 * yy), sh_three[4] * dx * (4.0 * zz - xx - yy),
        sh_three[5] * dz * (xx - yy), sh_three[6] * dx * (xx - 3.0 * yy),
    ]
    cols = []
    for c in range(3):
        acc = sh_zero * rows[11 + c] + 0.5
        for k in range(15):
            acc = acc + basis[k] * rows[14 + 3 * k + c]
        cols.append(acc)
    shape = sx.shape
    return [sx, sy, fa, fb, fc, jnp.broadcast_to(lo, shape)] + cols


def camera_columns(cam_ref):
    return [cam_ref[:, j:j + 1] for j in range(16)]


def slot_map(ids_ref, order_ref, count_ref):
    rowi = lax.broadcasted_iota(jnp.int32, (16, 128), 0)
    lane = lax.broadcasted_iota(jnp.int32, (16, 128), 1)
    owner = jnp.full((16, 128), -1, jnp.int32)
    for k in range(16):
        o = order_ref[0, 0, k]
        own = jnp.where(o < count_ref[0, 0], ids_ref[0, 0, o] >> 1, -1)
        owner = jnp.where(rowi == k, own, owner)
    return (owner == lane).astype(f32), jnp.where(owner[:, 0:1] < 0, -1e4, 0.0)


def exchange(me, send, recv, send_sem, recv_sem, n):
    def start(i, _):
        t = lax.rem(me + i, NT)
        pltpu.make_async_remote_copy(send.at[t, pl.ds(0, n)], recv.at[me, pl.ds(0, n)], send_sem.at[t], recv_sem.at[me], device_id={"tile": t}, device_id_type=MESH).start()
        return 0
    lax.fori_loop(1, NT, start, 0)


def finish(me, send, recv, send_sem, recv_sem, n):
    def wait(i, _):
        t = lax.rem(me + i, NT)
        d = pltpu.make_async_remote_copy(send.at[t, pl.ds(0, n)], recv.at[t, pl.ds(0, n)], send_sem.at[t], recv_sem.at[t], device_id={"tile": t}, device_id_type=MESH)
        d.wait_recv()
        d.wait_send()
        return 0
    lax.fori_loop(1, NT, wait, 0)


def gather_rows(recv, fbuf):
    for f in range(NF):
        fbuf[:, f * 128:(f + 1) * 128] = jnp.concatenate([recv[t, f:f + 1, :] for t in range(NT)], 0)
    return fbuf[...]


def place_rows(x, send):
    for f in range(NF):
        for t in range(NT):
            send[t, f:f + 1, :] = x[t:t + 1, f * 128:(f + 1) * 128]


def step_kernel(gauss_hbm, cons_hbm, dual_hbm, targ_hbm, step_ref, cam_ref, inter_ref, cid_ref, ids_ref, order_ref, count_ref, upd_ref, newd_ref,
                gauss_ref, cons_ref, dual_ref, t_ref, local_sem,
                req, reqs, fbuf, send, recv, gsend, grecv, grad, vals, near, s1, r1, s2, r2, s3, r3, s4, r4,
                alpha, wts, gbuf, lhs, csp, tb, cb, bend, grhs, a0, a1, a2):
    me = lax.axis_index("tile")
    grp = lax.axis_index("scene")
    last = lax.axis_size("scene") - 1
    loads = [pltpu.make_async_copy(x, y, local_sem.at[i]) for i, (x, y) in enumerate(((gauss_hbm, gauss_ref), (cons_hbm, cons_ref), (dual_hbm, dual_ref), (targ_hbm, t_ref)))]
    for l in loads:
        l.start()
    near[...] = jnp.zeros_like(near)
    barrier = pltpu.get_barrier_semaphore()

    def greet(i, _):
        pl.semaphore_signal(barrier, inc=1, device_id={"tile": lax.rem(me + i, NT)}, device_id_type=MESH)
        return 0
    lax.fori_loop(1, NT, greet, 0)

    @pl.when(grp < last)
    def _():
        pl.semaphore_signal(barrier, inc=1, device_id={"scene": grp + 1}, device_id_type=MESH)

    @pl.when(grp > 0)
    def _():
        pl.semaphore_signal(barrier, inc=1, device_id={"scene": grp - 1}, device_id_type=MESH)
    lane = lax.broadcasted_iota(jnp.int32, (1, 128), 1)
    ask = jnp.full((1, 128), cid_ref[0, 0], jnp.int32)
    for k in range(16):
        b = ids_ref[0, 0, k]
        ask = ask + jnp.where(lane == (b >> 1), (b & 1) * 16, 0)
    for t in range(NT):
        req[t] = ask
    reqs[me] = ask
    loads[0].wait()
    cam = camera_columns(cam_ref)
    for b in range(2):
        out = features([gauss_ref[0, i, b:b + 1, :] for i in range(59)], cam)
        for f in range(NF):
            fbuf[b * 16:(b + 1) * 16, f * 128:(f + 1) * 128] = out[f]
    pl.semaphore_wait(barrier, NT - 1 + jnp.where(grp < last, 1, 0) + jnp.where(grp > 0, 1, 0))
    exchange(me, req, reqs, s1, r1, 1)
    onehot, bias = slot_map(ids_ref, order_ref, count_ref)
    for l in loads[1:]:
        l.wait()
    finish(me, req, reqs, s1, r1, 1)
    asked = jnp.concatenate([reqs[t] for t in range(NT)], 0)
    lane32 = lax.broadcasted_iota(jnp.int32, (NT, 128), 1)
    col = jnp.sum(jnp.where(lane32 == me, asked, 0).astype(f32), 1, keepdims=True).astype(jnp.int32)
    sel = (col == lax.broadcasted_iota(jnp.int32, (NT, NT), 1)).astype(f32)
    place_rows(jnp.dot(sel, fbuf[...], precision=HI, preferred_element_type=f32), send)
    recv[me] = send[me]
    exchange(me, send, recv, s2, r2, NF)
    finish(me, send, recv, s2, r2, NF)
    y = jnp.dot(onehot[:, :NT], gather_rows(recv, fbuf), precision=HI, preferred_element_type=f32)
    targ = [jnp.concatenate([t_ref[0, c, 0:1, y0 * 128:(y0 + 1) * 128] for y0 in range(8)], 0) for c in range(3)]
    ybase = (8 * lax.rem(me, 4)).astype(f32)
    outs = render_body(ybase, [y[:, f * 128:(f + 1) * 128] for f in range(NF)], targ, bias, alpha, wts, gbuf, lhs, csp, tb, cb, bend, grhs, (a0, a1, a2))
    place_rows(lax.dot_general(onehot, jnp.concatenate(outs, 1), (((0,), (0,)), ((), ())), precision=HI, preferred_element_type=f32), gsend)
    grecv[me] = gsend[me]
    exchange(me, gsend, grecv, s3, r3, NF)
    finish(me, gsend, grecv, s3, r3, NF)
    df = lax.dot_general(sel, gather_rows(grecv, fbuf), (((0,), (0,)), ((), ())), precision=HI, preferred_element_type=f32)
    idx = jnp.concatenate([inter_ref[0, 0, 0:1, :], inter_ref[0, 0, 1:2, :]], 1)
    for b in range(2):
        rows = [gauss_ref[0, i, b:b + 1, :] for i in range(59)]
        _, pull = jax.vjp(lambda r: features(r, cam), rows)
        (grows,) = pull([df[b * 16:(b + 1) * 16, f * 128:(f + 1) * 128] for f in range(NF)])
        for i in range(59):
            d = dual_ref[0, i, b:b + 1, :]
            u = rows[i] - step_ref[i] * (grows[i] + penalty_weight * (rows[i] - cons_ref[0, i, b:b + 1, :] + d))
            upd_ref[0, i, b:b + 1, :] = u
            grad[b, i:i + 1, :] = u + d
    picks = [(lax.broadcasted_iota(jnp.int32, (128, 128), 0) + b * 128 == idx).astype(f32) for b in range(2)]
    v = sum(jnp.dot(grad[b], picks[b], precision=HI, preferred_element_type=f32) for b in range(2))
    vals[...] = v

    def up():
        return pltpu.make_async_remote_copy(vals, near.at[0], s4.at[0], r4.at[0], device_id={"scene": lax.rem(grp + 1, last + 1)}, device_id_type=MESH)

    def down():
        return pltpu.make_async_remote_copy(vals, near.at[1], s4.at[1], r4.at[1], device_id={"scene": lax.rem(grp + last, last + 1)}, device_id_type=MESH)

    @pl.when(grp < last)
    def _():
        up().start()

    @pl.when(grp > 0)
    def _():
        down().start()

    @pl.when(grp > 0)
    def _():
        up().wait_recv()
        down().wait_send()

    @pl.when(grp < last)
    def _():
        down().wait_recv()
        up().wait_send()
    lane = lax.broadcasted_iota(jnp.int32, (59, 128), 1)
    below = pltpu.roll(near[0], 64, 1)
    above = pltpu.roll(near[1], 64, 1)
    up_d = jnp.where(grp < last, v - above, 0.0)
    down_d = jnp.where(grp > 0, v - below, 0.0)
    diff = 0.5 * jnp.where(lane < 64, up_d, down_d)
    for b in range(2):
        nd = lax.dot_general(diff, picks[b], (((1,), (1,)), ((), ())), precision=HI, preferred_element_type=f32)
        for i in range(59):
            newd_ref[0, i, b:b + 1, :] = nd[i:i + 1, :]


VM = pl.BlockSpec(memory_space=pltpu.VMEM)
SM = pl.BlockSpec(memory_space=pltpu.SMEM)
HB = pl.BlockSpec(memory_space=pl.ANY)
DMA = pltpu.SemaphoreType.DMA


def on_device(gaussians, consensus, duals, step_sizes, cameras, camera_ids, block_lists, depth_order, block_counts, targets, intersection):
    def sd(shape, t=f32):
        return jax.ShapeDtypeStruct(shape, t)
    gaussians, consensus, duals, targets = [a.transpose(0, 2, 1, 3) for a in (gaussians, consensus, duals, targets)]
    big = sd((1, 59, 2, 128))
    out = pl.pallas_call(
        step_kernel, name="step", out_shape=(big, big),
        in_specs=[HB, HB, HB, HB, SM, VM, VM, SM, SM, SM, SM], out_specs=(VM, VM),
        scratch_shapes=[
            pltpu.VMEM((1, 59, 2, 128), f32), pltpu.VMEM((1, 59, 2, 128), f32), pltpu.VMEM((1, 59, 2, 128), f32), pltpu.VMEM((1, 3, 1, 1024), f32), DMA((4,)),
            pltpu.VMEM((NT, 1, 128), jnp.int32), pltpu.VMEM((NT, 1, 128), jnp.int32), pltpu.VMEM((NT, NF * 128), f32),
            pltpu.VMEM((NT, ROWS, 128), f32), pltpu.VMEM((NT, ROWS, 128), f32), pltpu.VMEM((NT, ROWS, 128), f32), pltpu.VMEM((NT, ROWS, 128), f32),
            pltpu.VMEM((2, 59, 128), f32), pltpu.VMEM((59, 128), f32), pltpu.VMEM((2, 59, 128), f32),
            DMA((NT,)), DMA((NT,)), DMA((NT,)), DMA((NT,)), DMA((NT,)), DMA((NT,)), DMA((2,)), DMA((2,)),
        ] + RENDER_SCRATCH,
        compiler_params=pltpu.CompilerParams(collective_id=0, has_side_effects=True, vmem_limit_bytes=60 * 1024 * 1024),
    )(gaussians, consensus, duals, targets, step_sizes, cameras, intersection, camera_ids, block_lists, depth_order, block_counts)
    return tuple(a.transpose(0, 2, 1, 3) for a in out)


def solution(mesh):
    t4, t3, t2 = P("scene", "tile", None, None), P("scene", "tile", None), P("scene", "tile")
    return jax.shard_map(
        on_device, mesh=mesh,
        in_specs=(t4, t4, t4, P(), P(), t2, t3, t3, t2, t4, t4),
        out_specs=(t4, t4), check_vma=False,
    )
```

```python
import functools

import jax
import jax.numpy as jnp
from jax import lax
from jax.experimental import pallas as pl
from jax.experimental.pallas import tpu as pltpu
from jax.sharding import PartitionSpec as P

HI = lax.Precision.HIGHEST
f32, bf16 = jnp.float32, jnp.bfloat16
MESH = pl.DeviceIdType.MESH
S = 132
SB = 8 * S
NI = 4
LN2 = 0.6931471805599453

def part2(v):
    a = v.astype(bf16)
    return a, (v - a.astype(f32)).astype(bf16)

def part3(v):
    a = v.astype(bf16).astype(f32)
    r = v - a
    b = r.astype(bf16).astype(f32)
    return a, b, (r - b).astype(bf16).astype(f32)

def render_body(ybase, feats, targ, bias, alpha, wts, gbuf, lhs, csp, tb, cb, bend, grhs, acc, rq):
    sx, sy, fa, fb, fc, lo, k0, k1, k2 = feats
    sxc = sx - 64.0
    syc = sy - (ybase + 3.5)
    lob = lo + bias
    zero32 = jnp.zeros((32, 128), f32)
    pa = part3(fa)
    lhs_a = jnp.concatenate(list(pa) + list(pa) + [zero32], 0).T.astype(bf16)
    for y in range(8):
        dy = (y - 3.5) - syc
        c1 = fb * dy - 2.0 * fa * sxc
        c0 = (fa * sxc - fb * dy) * sxc + fc * dy * dy + lob
        m = jnp.concatenate(list(part3(c0)) + list(part3(c1)) + [zero32], 0)
        lhs[y * 128:(y + 1) * 128, 0:128] = m.T.astype(bf16)
        lhs[y * 128:(y + 1) * 128, 128:256] = lhs_a
    colt = jnp.concatenate([k0, k1, k2, jnp.zeros((80, 128), f32)], 0).T
    kr = lax.broadcasted_iota(jnp.int32, (256, 256), 0)
    ln = lax.broadcasted_iota(jnp.int32, (256, 256), 1)
    xi = ((ln & 127) - 64).astype(f32)
    x2 = xi * xi
    x2h = x2.astype(bf16).astype(f32)
    x2l = x2 - x2h
    basis = jnp.where(kr < 48, 1.0, jnp.where(kr < 96, xi, jnp.where(kr < 128, 0.0, jnp.where(kr < 176, x2h, jnp.where(kr < 224, x2l, 0.0)))))
    grhs[...] = basis
    for p in range(8):
        rhs = jnp.where((kr & 15) == 2 * p + (ln >> 7), grhs[...], 0.0).astype(bf16)
        for y in range(8):
            e = jnp.dot(lhs[y * 128:(y + 1) * 128, :], rhs, preferred_element_type=f32)
            a = jnp.minimum(0.99, jnp.exp2(e))
            alpha[2 * p * SB + y * S:2 * p * SB + y * S + 128, :] = a[:, :128]
            alpha[(2 * p + 1) * SB + y * S:(2 * p + 1) * SB + y * S + 128, :] = a[:, 128:]
        for b in (2 * p, 2 * p + 1):
            for c in range(3):
                csp[c, b * 128:(b + 1) * 128, :] = jnp.broadcast_to(colt[:, c * 16 + b:c * 16 + b + 1], (128, 128))
    one = jnp.ones((8, 128), f32)
    zero = jnp.zeros((8, 128), f32)
    U = 8
    for q0 in range(0, 16, NI):
        def fwd(i, carry):
            st = [list(t) for t in carry]
            for u in range(U):
                g = i * U + u
                for j in range(NI):
                    b = q0 + j
                    a = alpha[pl.ds(b * SB + g, 8, stride=S), :]
                    t, s0, s1, s2 = st[j]
                    w = a * t
                    t = t * (1.0 - a)
                    row = b * 128 + g
                    s0 = s0 + w * csp[0, pl.ds(row, 8, stride=0), :]
                    s1 = s1 + w * csp[1, pl.ds(row, 8, stride=0), :]
                    s2 = s2 + w * csp[2, pl.ds(row, 8, stride=0), :]
                    wts[pl.ds(b * SB + g, 8, stride=S), :] = w
                    st[j] = [t, s0, s1, s2]
            return tuple(tuple(t) for t in st)
        out = lax.fori_loop(0, 128 // U, fwd, tuple((one, zero, zero, zero) for _ in range(NI)))
        for j in range(NI):
            tb[q0 + j] = out[j][0]
            for c in range(3):
                cb[c, q0 + j] = out[j][1 + c]
    t = one
    prods = [tb[b] for b in range(16)]
    cs = [zero, zero, zero]
    for b in range(16):
        tb[b] = t
        for c in range(3):
            cs[c] = cs[c] + t * cb[c, b]
        t = t * prods[b]
    r = [cs[c] - targ[c] for c in range(3)]
    e = zero
    for b in range(15, -1, -1):
        bend[b] = e
        e = prods[b] * e + (cb[0, b] * r[0] + cb[1, b] * r[1] + cb[2, b] * r[2])
    for q0 in range(0, 16, NI):
        rs = [[tb[q0 + j] * r[c] for c in range(3)] for j in range(NI)]
        def bwd(i, carry):
            st = list(carry)
            g0 = (128 // U - 1 - i) * U
            for u in range(U - 1, -1, -1):
                g = g0 + u
                for j in range(NI):
                    b = q0 + j
                    a = alpha[pl.ds(b * SB + g, 8, stride=S), :]
                    w = wts[pl.ds(b * SB + g, 8, stride=S), :]
                    row = b * 128 + g
                    q = (rs[j][0] * csp[0, pl.ds(row, 8, stride=0), :] + rs[j][1] * csp[1, pl.ds(row, 8, stride=0), :]) + rs[j][2] * csp[2, pl.ds(row, 8, stride=0), :]
                    d = q - st[j]
                    gbuf[pl.ds(b * SB + g, 8, stride=S), :] = jnp.where(a < 0.99, w * d, 0.0)
                    st[j] = st[j] + a * d
            return tuple(st)
        lax.fori_loop(0, 128 // U, bwd, tuple(tb[q0 + j] * bend[q0 + j] for j in range(NI)))
    mt, phi, xs = acc
    xf = (lax.broadcasted_iota(jnp.int32, (16, 128), 1) - 64).astype(f32)
    kk = lax.broadcasted_iota(jnp.int32, (16, 128), 0)
    xx = xf * xf
    xxh = xx.astype(bf16).astype(f32)
    plans = ({0: 1.0, 1: xf, 2: xxh, 3: xx - xxh}, {4: 1.0, 5: xf}, {6: 1.0}, {7: 1.0}, {8: 1.0}, {9: 1.0})
    for i, plan in enumerate(plans):
        v = jnp.zeros((16, 128), f32)
        for k, w in plan.items():
            v = jnp.where(kk == k, w, v)
        phi[:, i * 256:i * 256 + 128] = v.astype(bf16)
        phi[:, i * 256 + 128:i * 256 + 256] = v.astype(bf16)
    nt = (((1,), (1,)), ((), ()))
    for c in range(3):
        rq[c] = r[c]
    xa, xb = xs
    def fill(b, dst):
        tbb = tb[b]
        base = b * SB if isinstance(b, int) else pl.multiple_of(b * SB, 8)
        rows = []
        for c in range(3):
            v = rq[c] * tbb
            rows.append([v[y:y + 1, :] for y in range(8)])
        for n in range(8):
            at = base + n * 16
            g = [gbuf[pl.ds(at + y * S, 16), :] for y in range(8)]
            sm = [g[4 + k] + g[3 - k] for k in range(4)]
            df = [g[4 + k] - g[3 - k] for k in range(4)]
            out = [(sm[0] + sm[1]) + (sm[2] + sm[3]),
                   (0.5 * df[0] + 1.5 * df[1]) + (2.5 * df[2] + 3.5 * df[3]),
                   (0.25 * sm[0] + 2.25 * sm[1]) + (6.25 * sm[2] + 12.25 * sm[3])]
            w = [wts[pl.ds(at + y * S, 16), :] for y in range(8)]
            for c in range(3):
                t = [w[y] * rows[c][y] for y in range(8)]
                out.append(((t[0] + t[1]) + (t[2] + t[3])) + ((t[4] + t[5]) + (t[6] + t[7])))
            for i in range(6):
                h, l = part2(out[i])
                dst[n * 16:(n + 1) * 16, i * 256:i * 256 + 128] = h
                dst[n * 16:(n + 1) * 16, i * 256 + 128:i * 256 + 256] = l
    def contract(b, src):
        mt[pl.ds(b * 17, 16), :] = lax.dot_general(phi[...], src[...], nt, preferred_element_type=f32)
    fill(0, xa)
    def red(i, _):
        contract(2 * i, xa)
        fill(2 * i + 1, xb)
        contract(2 * i + 1, xb)
        fill(2 * i + 2, xa)
        return 0
    lax.fori_loop(0, 7, red, 0)
    contract(14, xa)
    fill(15, xb)
    contract(15, xb)
    M = [jnp.concatenate([mt[pl.ds(k, 8, stride=17), :], mt[pl.ds(8 * 17 + k, 8, stride=17), :]], 0) for k in range(10)]
    M0 = M[0] * LN2
    Mx = M[1] * LN2
    Mxx = (M[2] + M[3]) * LN2
    My = M[4] * LN2
    Mxy = M[5] * LN2
    Myy = M[6] * LN2
    ux = Mx - sxc * M0
    uy = My - syc * M0
    d_a = Mxx - sxc * (Mx + ux)
    d_b = Mxy - syc * Mx - sxc * uy
    d_c = Myy - syc * (My + uy)
    d_sx = -(2.0 * fa * ux + fb * uy)
    d_sy = -(fb * ux + 2.0 * fc * uy)
    return [d_sx, d_sy, d_a, d_b, d_c, M0, M[7], M[8], M[9]]

RENDER_SCRATCH = [
    pltpu.VMEM((16 * SB, 128), f32), pltpu.VMEM((16 * SB, 128), f32), pltpu.VMEM((16 * SB, 128), f32),
    pltpu.VMEM((1024, 256), bf16), pltpu.VMEM((3, 2048, 128), f32),
    pltpu.VMEM((16, 8, 128), f32), pltpu.VMEM((3, 16, 8, 128), f32), pltpu.VMEM((16, 8, 128), f32),
    pltpu.VMEM((256, 256), f32),
    pltpu.VMEM((16 * 17 + 8, 128), f32), pltpu.VMEM((16, 1536), bf16), pltpu.VMEM((128, 1536), bf16), pltpu.VMEM((128, 1536), bf16), pltpu.VMEM((3, 8, 128), f32),
]

LOG2E = 1.4426950408889634
blur_floor = 0.3
penalty_weight = 0.5
sh_zero = 0.28209479177387814
sh_one = 0.4886025119029199
sh_two = (1.0925484305920792, -1.0925484305920792, 0.31539156525252005, -1.0925484305920792, 0.5462742152960396)
sh_three = (-0.5900435899266435, 2.890611442640554, -0.4570457994644658, 0.3731763325901154, -0.4570457994644658, 1.445305721320277, -0.5900435899266435)
NT = 32
NF = 9
VMEM_LIMIT = 40 * 1024 * 1024
ROWS = 16


def features(rows, cam):
    rot = [[cam[3 * i + j] for j in range(3)] for i in range(3)]
    shift = cam[9:12]
    fx, fy, cx, cy = cam[12:16]
    m = rows[0:3]
    e = [rot[i][0] * m[0] + rot[i][1] * m[1] + rot[i][2] * m[2] + shift[i] for i in range(3)]
    inv = 1.0 / e[2]
    px = e[0] * inv
    py = e[1] * inv
    sx = fx * px + cx
    sy = fy * py + cy
    qn = rows[6] * rows[6] + rows[7] * rows[7] + rows[8] * rows[8] + rows[9] * rows[9]
    qi = 1.0 / jnp.sqrt(qn)
    w, x, y, z = [rows[6 + i] * qi for i in range(4)]
    rq = [
        [1.0 - 2.0 * (y * y + z * z), 2.0 * (x * y - w * z), 2.0 * (x * z + w * y)],
        [2.0 * (x * y + w * z), 1.0 - 2.0 * (x * x + z * z), 2.0 * (y * z - w * x)],
        [2.0 * (x * z - w * y), 2.0 * (y * z + w * x), 1.0 - 2.0 * (x * x + y * y)],
    ]
    sc = [jnp.exp(rows[3 + k]) for k in range(3)]
    mm = [[rq[j][k] * sc[k] for k in range(3)] for j in range(3)]
    ww = [[rot[i][0] * mm[0][k] + rot[i][1] * mm[1][k] + rot[i][2] * mm[2][k] for k in range(3)] for i in range(3)]
    ax, ay = fx * inv, fy * inv
    r1 = [ax * (ww[0][k] - px * ww[2][k]) for k in range(3)]
    r2 = [ay * (ww[1][k] - py * ww[2][k]) for k in range(3)]
    cxx = r1[0] * r1[0] + r1[1] * r1[1] + r1[2] * r1[2] + blur_floor
    cxy = r1[0] * r2[0] + r1[1] * r2[1] + r1[2] * r2[2]
    cyy = r2[0] * r2[0] + r2[1] * r2[1] + r2[2] * r2[2] + blur_floor
    idet = 1.0 / (cxx * cyy - cxy * cxy)
    fa = (-0.5 * LOG2E) * (cyy * idet)
    fb = LOG2E * (cxy * idet)
    fc = (-0.5 * LOG2E) * (cxx * idet)
    lo = (-LOG2E) * jnp.log(1.0 + jnp.exp(-rows[10]))
    eye = [-(rot[0][i] * shift[0] + rot[1][i] * shift[1] + rot[2][i] * shift[2]) for i in range(3)]
    tw = [m[i] - eye[i] for i in range(3)]
    ti = 1.0 / jnp.sqrt(tw[0] * tw[0] + tw[1] * tw[1] + tw[2] * tw[2])
    dx, dy, dz = [t * ti for t in tw]
    xx, yy, zz = dx * dx, dy * dy, dz * dz
    basis = [
        -sh_one * dy, sh_one * dz, -sh_one * dx,
        sh_two[0] * dx * dy, sh_two[1] * dy * dz, sh_two[2] * (2.0 * zz - xx - yy), sh_two[3] * dx * dz, sh_two[4] * (xx - yy),
        sh_three[0] * dy * (3.0 * xx - yy), sh_three[1] * dx * dy * dz, sh_three[2] * dy * (4.0 * zz - xx - yy),
        sh_three[3] * dz * (2.0 * zz - 3.0 * xx - 3.0 * yy), sh_three[4] * dx * (4.0 * zz - xx - yy),
        sh_three[5] * dz * (xx - yy), sh_three[6] * dx * (xx - 3.0 * yy),
    ]
    cols = []
    for c in range(3):
        acc = sh_zero * rows[11 + c] + 0.5
        for k in range(15):
            acc = acc + basis[k] * rows[14 + 3 * k + c]
        cols.append(acc)
    shape = sx.shape
    return [sx, sy, fa, fb, fc, jnp.broadcast_to(lo, shape)] + cols


def camera_columns(cam_ref):
    return [cam_ref[:, j:j + 1] for j in range(16)]


def slot_map(ids_ref, order_ref, count_ref):
    rowi = lax.broadcasted_iota(jnp.int32, (16, 128), 0)
    lane = lax.broadcasted_iota(jnp.int32, (16, 128), 1)
    owner = jnp.full((16, 128), -1, jnp.int32)
    across = jnp.full((16, 128), -1, jnp.int32)
    for k in range(16):
        o = order_ref[0, 0, k]
        own = jnp.where(o < count_ref[0, 0], ids_ref[0, 0, o] >> 1, -1)
        owner = jnp.where(rowi == k, own, owner)
        across = jnp.where(lane == k, own, across)
    one = (owner == lane).astype(f32)[:, :NT]
    back = (jnp.broadcast_to(across[0:1, :16], (NT, 16)) == lax.broadcasted_iota(jnp.int32, (NT, 16), 0)).astype(f32)
    return one, back, jnp.where(owner[:, 0:1] < 0, -1e4, 0.0)


def slab(ref, t):
    return ref.at[pl.ds(pl.multiple_of(t * ROWS, ROWS), NF)]


def copy_to(me, t, send, recv, send_sem, recv_sem, row, wide):
    src, dst = (slab(send, t), slab(recv, row)) if wide else (send.at[t], recv.at[row])
    return pltpu.make_async_remote_copy(src, dst, send_sem.at[t], recv_sem.at[row], device_id={"tile": t}, device_id_type=MESH)


def exchange(me, send, recv, send_sem, recv_sem, wide=True):
    def start(i, _):
        copy_to(me, lax.rem(me + i, NT), send, recv, send_sem, recv_sem, me, wide).start()
        return 0
    lax.fori_loop(1, NT, start, 0)


def arrived(me, send, recv, send_sem, recv_sem, wide=True):
    def wait(i, _):
        t = lax.rem(me + i, NT)
        copy_to(me, t, send, recv, send_sem, recv_sem, t, wide).wait_recv()
        return 0
    lax.fori_loop(1, NT, wait, 0)


def sent(me, send, recv, send_sem, recv_sem, wide=True):
    def wait(i, _):
        t = lax.rem(me + i, NT)
        copy_to(me, t, send, recv, send_sem, recv_sem, t, wide).wait_send()
        return 0
    lax.fori_loop(1, NT, wait, 0)


def stack3(x):
    return jnp.concatenate(part3(x), 0).astype(bf16)


def thrice(onehot):
    return jnp.concatenate([onehot] * 3, 1).astype(bf16)


def gather_rows(recv):
    return jnp.concatenate([jnp.concatenate([recv[pl.ds(t * ROWS + f, 8, stride=ROWS), :] for t in range(0, NT, 8)], 0) for f in range(NF)], 1)


def place_rows(x, send):
    for f in range(NF):
        for t in range(0, NT, 8):
            send[pl.ds(t * ROWS + f, 8, stride=ROWS), :] = x[t:t + 8, f * 128:(f + 1) * 128]


def own_rows(me, send, recv):
    at = pl.ds(pl.multiple_of(me * ROWS, ROWS), ROWS)
    recv[at, :] = send[at, :]


def step_kernel(gauss_hbm, cons_hbm, dual_hbm, targ_hbm, step_ref, cam_ref, inter_ref, cid_ref, ids_ref, order_ref, count_ref, upd_ref, newd_ref,
                gauss_ref, cons_ref, dual_ref, t_ref, local_sem,
                req, reqs, fbuf, send, recv, gsend, grecv, grad, base, vals, near, s1, r1, s2, r2, s3, r3, s4, r4,
                alpha, wts, gbuf, lhs, csp, tb, cb, bend, grhs, a0, a1, a2, a3, rq):
    me = lax.axis_index("tile")
    grp = lax.axis_index("scene")
    last = lax.axis_size("scene") - 1
    loads = [pltpu.make_async_copy(x, y, local_sem.at[i]) for i, (x, y) in enumerate(((gauss_hbm, gauss_ref), (cons_hbm, cons_ref), (dual_hbm, dual_ref), (targ_hbm, t_ref)))]
    for l in loads:
        l.start()
    near[...] = jnp.zeros_like(near)
    barrier = pltpu.get_barrier_semaphore()

    def greet(i, _):
        pl.semaphore_signal(barrier, inc=1, device_id={"tile": lax.rem(me + i, NT)}, device_id_type=MESH)
        return 0
    lax.fori_loop(1, NT, greet, 0)

    @pl.when(grp < last)
    def _():
        pl.semaphore_signal(barrier, inc=1, device_id={"scene": grp + 1}, device_id_type=MESH)

    @pl.when(grp > 0)
    def _():
        pl.semaphore_signal(barrier, inc=1, device_id={"scene": grp - 1}, device_id_type=MESH)
    lane = lax.broadcasted_iota(jnp.int32, (1, 128), 1)
    ask = jnp.full((1, 128), cid_ref[0, 0], jnp.int32)
    for k in range(16):
        b = ids_ref[0, 0, k]
        ask = ask + jnp.where(lane == (b >> 1), (b & 1) * 16, 0)
    for t in range(NT):
        req[t] = ask
    reqs[me] = ask
    loads[0].wait()
    cam = camera_columns(cam_ref)
    outs = [features([gauss_ref[0, i, b:b + 1, :] for i in range(59)], cam) for b in range(2)]
    fbuf[...] = stack3(jnp.concatenate([jnp.concatenate(o, 1) for o in outs], 0))
    pl.semaphore_wait(barrier, NT - 1 + jnp.where(grp < last, 1, 0) + jnp.where(grp > 0, 1, 0))
    exchange(me, req, reqs, s1, r1, False)
    one, back, bias = slot_map(ids_ref, order_ref, count_ref)
    for l in loads[1:]:
        l.wait()
    arrived(me, req, reqs, s1, r1, False)
    asked = jnp.concatenate([reqs[t] for t in range(NT)], 0)
    lane32 = lax.broadcasted_iota(jnp.int32, (NT, 128), 1)
    col = jnp.sum(jnp.where(lane32 == me, asked, 0).astype(f32), 1, keepdims=True).astype(jnp.int32)
    sel = (col == lax.broadcasted_iota(jnp.int32, (NT, NT), 1)).astype(f32)
    place_rows(jnp.dot(thrice(sel), fbuf[...], preferred_element_type=f32), send)
    own_rows(me, send, recv)
    exchange(me, send, recv, s2, r2)
    one3 = thrice(one)
    arrived(me, send, recv, s2, r2)
    y = jnp.dot(one3, stack3(gather_rows(recv)), preferred_element_type=f32)
    targ = [jnp.concatenate([t_ref[0, c, 0:1, y0 * 128:(y0 + 1) * 128] for y0 in range(8)], 0) for c in range(3)]
    ybase = (8 * lax.rem(me, 4)).astype(f32)
    outs = render_body(ybase, [y[:, f * 128:(f + 1) * 128] for f in range(NF)], targ, bias, alpha, wts, gbuf, lhs, csp, tb, cb, bend, grhs, (a0, a1, (a2, a3)), rq)
    place_rows(jnp.dot(thrice(back), stack3(jnp.concatenate(outs, 1)), preferred_element_type=f32), gsend)
    own_rows(me, gsend, grecv)
    exchange(me, gsend, grecv, s3, r3)
    turned = jnp.concatenate([jnp.broadcast_to(col, (NT, 128)).astype(f32), jnp.zeros((96, 128), f32)], 0).T
    selt = thrice((turned[:NT, :NT].astype(jnp.int32) == lax.broadcasted_iota(jnp.int32, (NT, NT), 0)).astype(f32))
    idx = jnp.concatenate([inter_ref[0, 0, 0:1, :], inter_ref[0, 0, 1:2, :]], 1)
    picks = [(lax.broadcasted_iota(jnp.int32, (128, 128), 0) + b * 128 == idx).astype(f32) for b in range(2)]
    pulls = []
    for b in range(2):
        rows = [gauss_ref[0, i, b:b + 1, :] for i in range(59)]
        pulls.append(jax.vjp(lambda r: features(r, cam), rows)[1])
    for i in range(59):
        base[i] = gauss_ref[0, i] - (penalty_weight * step_ref[i]) * (gauss_ref[0, i] - cons_ref[0, i] + dual_ref[0, i])
    arrived(me, gsend, grecv, s3, r3)
    df = jnp.dot(selt, stack3(gather_rows(grecv)), preferred_element_type=f32)
    for b in range(2):
        (grows,) = pulls[b]([df[b * 16:(b + 1) * 16, f * 128:(f + 1) * 128] for f in range(NF)])
        for i in range(59):
            u = base[i, b:b + 1, :] - step_ref[i] * grows[i]
            upd_ref[0, i, b:b + 1, :] = u
            grad[b, i:i + 1, :] = u + dual_ref[0, i, b:b + 1, :]
    grad[:, 59:64, :] = jnp.zeros((2, 5, 128), f32)
    picks3 = [jnp.concatenate([p] * 3, 0).astype(bf16) for p in picks]
    v = sum(jnp.dot(jnp.concatenate(part3(grad[b]), 1).astype(bf16), picks3[b], preferred_element_type=f32) for b in range(2))
    lane = lax.broadcasted_iota(jnp.int32, (32, 128), 1)
    low, high = v[:32], v[32:]
    vals[0] = jnp.where(lane < 64, low, pltpu.roll(high, 64, 1))
    vals[1] = jnp.where(lane < 64, pltpu.roll(low, 64, 1), high)

    def up():
        return pltpu.make_async_remote_copy(vals.at[0], near.at[0], s4.at[0], r4.at[0], device_id={"scene": lax.rem(grp + 1, last + 1)}, device_id_type=MESH)

    def down():
        return pltpu.make_async_remote_copy(vals.at[1], near.at[1], s4.at[1], r4.at[1], device_id={"scene": lax.rem(grp + last, last + 1)}, device_id_type=MESH)

    @pl.when(grp < last)
    def _():
        up().start()

    @pl.when(grp > 0)
    def _():
        down().start()

    @pl.when(grp > 0)
    def _():
        up().wait_recv()
        down().wait_send()

    @pl.when(grp < last)
    def _():
        down().wait_recv()
        up().wait_send()
    from_above = jnp.where(grp < last, 0.5 * (vals[0] - near[1]), 0.0)
    from_below = jnp.where(grp > 0, 0.5 * (vals[1] - near[0]), 0.0)
    diff = jnp.concatenate([
        jnp.where(lane < 64, from_above, pltpu.roll(from_below, 64, 1)),
        jnp.where(lane < 64, pltpu.roll(from_above, 64, 1), from_below),
    ], 0)
    diff3 = jnp.concatenate(part3(diff), 1).astype(bf16)
    for b in range(2):
        p3 = jnp.concatenate([picks[b]] * 3, 1).astype(bf16)
        nd = lax.dot_general(diff3, p3, (((1,), (1,)), ((), ())), preferred_element_type=f32)
        for i in range(59):
            newd_ref[0, i, b:b + 1, :] = nd[i:i + 1, :]
    sent(me, req, reqs, s1, r1, False)
    sent(me, send, recv, s2, r2)
    sent(me, gsend, grecv, s3, r3)


VM = pl.BlockSpec(memory_space=pltpu.VMEM)
SM = pl.BlockSpec(memory_space=pltpu.SMEM)
HB = pl.BlockSpec(memory_space=pltpu.HBM)
DMA = pltpu.SemaphoreType.DMA


def on_device(gaussians, consensus, duals, step_sizes, cameras, camera_ids, block_lists, depth_order, block_counts, targets, intersection):
    def sd(shape, t=f32):
        return jax.ShapeDtypeStruct(shape, t)
    gaussians, consensus, duals, targets = [a.transpose(0, 2, 1, 3) for a in (gaussians, consensus, duals, targets)]
    big = sd((1, 59, 2, 128))
    out = pl.pallas_call(
        step_kernel, name="step", out_shape=(big, big),
        in_specs=[HB, HB, HB, HB, SM, VM, VM, SM, SM, SM, SM], out_specs=(VM, VM),
        scratch_shapes=[
            pltpu.VMEM((1, 59, 2, 128), f32), pltpu.VMEM((1, 59, 2, 128), f32), pltpu.VMEM((1, 59, 2, 128), f32), pltpu.VMEM((1, 3, 1, 1024), f32), DMA((4,)),
            pltpu.VMEM((NT, 1, 128), jnp.int32), pltpu.VMEM((NT, 1, 128), jnp.int32), pltpu.VMEM((3 * NT, NF * 128), bf16),
            pltpu.VMEM((NT * ROWS, 128), f32), pltpu.VMEM((NT * ROWS, 128), f32), pltpu.VMEM((NT * ROWS, 128), f32), pltpu.VMEM((NT * ROWS, 128), f32),
            pltpu.VMEM((2, 64, 128), f32), pltpu.VMEM((59, 2, 128), f32), pltpu.VMEM((2, 32, 128), f32), pltpu.VMEM((2, 32, 128), f32),
            DMA((NT,)), DMA((NT,)), DMA((NT,)), DMA((NT,)), DMA((NT,)), DMA((NT,)), DMA((2,)), DMA((2,)),
        ] + RENDER_SCRATCH,
        compiler_params=pltpu.CompilerParams(collective_id=0, has_side_effects=True, vmem_limit_bytes=VMEM_LIMIT),
    )(gaussians, consensus, duals, targets, step_sizes, cameras, intersection, camera_ids, block_lists, depth_order, block_counts)
    return tuple(a.transpose(0, 2, 1, 3) for a in out)


def solution(mesh):
    t4, t3, t2 = P("scene", "tile", None, None), P("scene", "tile", None), P("scene", "tile")
    return jax.shard_map(
        on_device, mesh=mesh,
        in_specs=(t4, t4, t4, P(), P(), t2, t3, t3, t2, t4, t4),
        out_specs=(t4, t4), check_vma=False,
    )
```

```python
import functools

import jax
import jax.numpy as jnp
from jax import lax
from jax.experimental import pallas as pl
from jax.experimental.pallas import tpu as pltpu
from jax.sharding import PartitionSpec as P

HI = lax.Precision.HIGHEST
f32, bf16 = jnp.float32, jnp.bfloat16
MESH = pl.DeviceIdType.MESH
S = 132
SB = 8 * S
NI = 4
LN2 = 0.6931471805599453

def part2(v):
    a = v.astype(bf16)
    return a, (v - a.astype(f32)).astype(bf16)

def part3(v):
    a = v.astype(bf16).astype(f32)
    r = v - a
    b = r.astype(bf16).astype(f32)
    return a, b, (r - b).astype(bf16).astype(f32)

def render_body(ybase, feats, targ, bias, alpha, wts, gbuf, lhs, csp, tb, cb, bend, grhs, acc, rq):
    sx, sy, fa, fb, fc, lo, k0, k1, k2 = feats
    sxc = sx - 64.0
    syc = sy - (ybase + 3.5)
    lob = lo + bias
    zero32 = jnp.zeros((32, 128), f32)
    pa = part3(fa)
    lhs_a = jnp.concatenate(list(pa) + list(pa) + [zero32], 0).T.astype(bf16)
    for y in range(8):
        dy = (y - 3.5) - syc
        c1 = fb * dy - 2.0 * fa * sxc
        c0 = (fa * sxc - fb * dy) * sxc + fc * dy * dy + lob
        m = jnp.concatenate(list(part3(c0)) + list(part3(c1)) + [zero32], 0)
        lhs[y * 128:(y + 1) * 128, 0:128] = m.T.astype(bf16)
        lhs[y * 128:(y + 1) * 128, 128:256] = lhs_a
    colt = jnp.concatenate([k0, k1, k2, jnp.zeros((80, 128), f32)], 0).T
    kr = lax.broadcasted_iota(jnp.int32, (256, 256), 0)
    ln = lax.broadcasted_iota(jnp.int32, (256, 256), 1)
    xi = ((ln & 127) - 64).astype(f32)
    x2 = xi * xi
    x2h = x2.astype(bf16).astype(f32)
    x2l = x2 - x2h
    basis = jnp.where(kr < 48, 1.0, jnp.where(kr < 96, xi, jnp.where(kr < 128, 0.0, jnp.where(kr < 176, x2h, jnp.where(kr < 224, x2l, 0.0)))))
    grhs[...] = basis
    for p in range(8):
        rhs = jnp.where((kr & 15) == 2 * p + (ln >> 7), grhs[...], 0.0).astype(bf16)
        for y in range(8):
            e = jnp.dot(lhs[y * 128:(y + 1) * 128, :], rhs, preferred_element_type=f32)
            a = jnp.minimum(0.99, jnp.exp2(e))
            alpha[2 * p * SB + y * S:2 * p * SB + y * S + 128, :] = a[:, :128]
            alpha[(2 * p + 1) * SB + y * S:(2 * p + 1) * SB + y * S + 128, :] = a[:, 128:]
        for b in (2 * p, 2 * p + 1):
            for c in range(3):
                csp[c, b * 128:(b + 1) * 128, :] = jnp.broadcast_to(colt[:, c * 16 + b:c * 16 + b + 1], (128, 128))
    one = jnp.ones((8, 128), f32)
    zero = jnp.zeros((8, 128), f32)
    U = 8
    for q0 in range(0, 16, NI):
        def fwd(i, carry):
            st = [list(t) for t in carry]
            for u in range(U):
                g = i * U + u
                for j in range(NI):
                    b = q0 + j
                    a = alpha[pl.ds(b * SB + g, 8, stride=S), :]
                    t, s0, s1, s2 = st[j]
                    w = a * t
                    t = t * (1.0 - a)
                    row = b * 128 + g
                    s0 = s0 + w * csp[0, pl.ds(row, 8, stride=0), :]
                    s1 = s1 + w * csp[1, pl.ds(row, 8, stride=0), :]
                    s2 = s2 + w * csp[2, pl.ds(row, 8, stride=0), :]
                    wts[pl.ds(b * SB + g, 8, stride=S), :] = w
                    st[j] = [t, s0, s1, s2]
            return tuple(tuple(t) for t in st)
        out = lax.fori_loop(0, 128 // U, fwd, tuple((one, zero, zero, zero) for _ in range(NI)))
        for j in range(NI):
            tb[q0 + j] = out[j][0]
            for c in range(3):
                cb[c, q0 + j] = out[j][1 + c]
    t = one
    prods = [tb[b] for b in range(16)]
    cs = [zero, zero, zero]
    for b in range(16):
        tb[b] = t
        for c in range(3):
            cs[c] = cs[c] + t * cb[c, b]
        t = t * prods[b]
    r = [cs[c] - targ[c] for c in range(3)]
    e = zero
    for b in range(15, -1, -1):
        bend[b] = e
        e = prods[b] * e + (cb[0, b] * r[0] + cb[1, b] * r[1] + cb[2, b] * r[2])
    for q0 in range(0, 16, NI):
        rs = [[tb[q0 + j] * r[c] for c in range(3)] for j in range(NI)]
        def bwd(i, carry):
            st = list(carry)
            g0 = (128 // U - 1 - i) * U
            for u in range(U - 1, -1, -1):
                g = g0 + u
                for j in range(NI):
                    b = q0 + j
                    a = alpha[pl.ds(b * SB + g, 8, stride=S), :]
                    w = wts[pl.ds(b * SB + g, 8, stride=S), :]
                    row = b * 128 + g
                    q = (rs[j][0] * csp[0, pl.ds(row, 8, stride=0), :] + rs[j][1] * csp[1, pl.ds(row, 8, stride=0), :]) + rs[j][2] * csp[2, pl.ds(row, 8, stride=0), :]
                    d = q - st[j]
                    gbuf[pl.ds(b * SB + g, 8, stride=S), :] = jnp.where(a < 0.99, w * d, 0.0)
                    st[j] = st[j] + a * d
            return tuple(st)
        lax.fori_loop(0, 128 // U, bwd, tuple(tb[q0 + j] * bend[q0 + j] for j in range(NI)))
    mt, phi, xs = acc
    xf = (lax.broadcasted_iota(jnp.int32, (16, 128), 1) - 64).astype(f32)
    kk = lax.broadcasted_iota(jnp.int32, (16, 128), 0)
    xx = xf * xf
    xxh = xx.astype(bf16).astype(f32)
    plans = ({0: 1.0, 1: xf, 2: xxh, 3: xx - xxh}, {4: 1.0, 5: xf}, {6: 1.0}, {7: 1.0}, {8: 1.0}, {9: 1.0})
    for i, plan in enumerate(plans):
        v = jnp.zeros((16, 128), f32)
        for k, w in plan.items():
            v = jnp.where(kk == k, w, v)
        phi[:, i * 256:i * 256 + 128] = v.astype(bf16)
        phi[:, i * 256 + 128:i * 256 + 256] = v.astype(bf16)
    nt = (((1,), (1,)), ((), ()))
    for c in range(3):
        rq[c] = r[c]
    xa, xb = xs
    def fill(b, dst):
        tbb = tb[b]
        base = b * SB if isinstance(b, int) else pl.multiple_of(b * SB, 8)
        rows = []
        for c in range(3):
            v = rq[c] * tbb
            rows.append([v[y:y + 1, :] for y in range(8)])
        for n in range(8):
            at = base + n * 16
            g = [gbuf[pl.ds(at + y * S, 16), :] for y in range(8)]
            sm = [g[4 + k] + g[3 - k] for k in range(4)]
            df = [g[4 + k] - g[3 - k] for k in range(4)]
            out = [(sm[0] + sm[1]) + (sm[2] + sm[3]),
                   (0.5 * df[0] + 1.5 * df[1]) + (2.5 * df[2] + 3.5 * df[3]),
                   (0.25 * sm[0] + 2.25 * sm[1]) + (6.25 * sm[2] + 12.25 * sm[3])]
            w = [wts[pl.ds(at + y * S, 16), :] for y in range(8)]
            for c in range(3):
                t = [w[y] * rows[c][y] for y in range(8)]
                out.append(((t[0] + t[1]) + (t[2] + t[3])) + ((t[4] + t[5]) + (t[6] + t[7])))
            for i in range(6):
                h, l = part2(out[i])
                dst[n * 16:(n + 1) * 16, i * 256:i * 256 + 128] = h
                dst[n * 16:(n + 1) * 16, i * 256 + 128:i * 256 + 256] = l
    def contract(b, src):
        mt[pl.ds(b * 17, 16), :] = lax.dot_general(phi[...], src[...], nt, preferred_element_type=f32)
    fill(0, xa)
    def red(i, _):
        contract(2 * i, xa)
        fill(2 * i + 1, xb)
        contract(2 * i + 1, xb)
        fill(2 * i + 2, xa)
        return 0
    lax.fori_loop(0, 7, red, 0)
    contract(14, xa)
    fill(15, xb)
    contract(15, xb)
    M = [jnp.concatenate([mt[pl.ds(k, 8, stride=17), :], mt[pl.ds(8 * 17 + k, 8, stride=17), :]], 0) for k in range(10)]
    M0 = M[0] * LN2
    Mx = M[1] * LN2
    Mxx = (M[2] + M[3]) * LN2
    My = M[4] * LN2
    Mxy = M[5] * LN2
    Myy = M[6] * LN2
    ux = Mx - sxc * M0
    uy = My - syc * M0
    d_a = Mxx - sxc * (Mx + ux)
    d_b = Mxy - syc * Mx - sxc * uy
    d_c = Myy - syc * (My + uy)
    d_sx = -(2.0 * fa * ux + fb * uy)
    d_sy = -(fb * ux + 2.0 * fc * uy)
    return [d_sx, d_sy, d_a, d_b, d_c, M0, M[7], M[8], M[9]]

RENDER_SCRATCH = [
    pltpu.VMEM((16 * SB, 128), f32), pltpu.VMEM((16 * SB, 128), f32), pltpu.VMEM((16 * SB, 128), f32),
    pltpu.VMEM((1024, 256), bf16), pltpu.VMEM((3, 2048, 128), f32),
    pltpu.VMEM((16, 8, 128), f32), pltpu.VMEM((3, 16, 8, 128), f32), pltpu.VMEM((16, 8, 128), f32),
    pltpu.VMEM((256, 256), f32),
    pltpu.VMEM((16 * 17 + 8, 128), f32), pltpu.VMEM((16, 1536), bf16), pltpu.VMEM((128, 1536), bf16), pltpu.VMEM((128, 1536), bf16), pltpu.VMEM((3, 8, 128), f32),
]

LOG2E = 1.4426950408889634
blur_floor = 0.3
penalty_weight = 0.5
sh_zero = 0.28209479177387814
sh_one = 0.4886025119029199
sh_two = (1.0925484305920792, -1.0925484305920792, 0.31539156525252005, -1.0925484305920792, 0.5462742152960396)
sh_three = (-0.5900435899266435, 2.890611442640554, -0.4570457994644658, 0.3731763325901154, -0.4570457994644658, 1.445305721320277, -0.5900435899266435)
NT = 32
NF = 9
VMEM_LIMIT = 40 * 1024 * 1024
ROWS = 16


def features(rows, cam):
    rot = [[cam[3 * i + j] for j in range(3)] for i in range(3)]
    shift = cam[9:12]
    fx, fy, cx, cy = cam[12:16]
    m = rows[0:3]
    e = [rot[i][0] * m[0] + rot[i][1] * m[1] + rot[i][2] * m[2] + shift[i] for i in range(3)]
    inv = 1.0 / e[2]
    px = e[0] * inv
    py = e[1] * inv
    sx = fx * px + cx
    sy = fy * py + cy
    qn = rows[6] * rows[6] + rows[7] * rows[7] + rows[8] * rows[8] + rows[9] * rows[9]
    qi = 1.0 / jnp.sqrt(qn)
    w, x, y, z = [rows[6 + i] * qi for i in range(4)]
    rq = [
        [1.0 - 2.0 * (y * y + z * z), 2.0 * (x * y - w * z), 2.0 * (x * z + w * y)],
        [2.0 * (x * y + w * z), 1.0 - 2.0 * (x * x + z * z), 2.0 * (y * z - w * x)],
        [2.0 * (x * z - w * y), 2.0 * (y * z + w * x), 1.0 - 2.0 * (x * x + y * y)],
    ]
    sc = [jnp.exp(rows[3 + k]) for k in range(3)]
    mm = [[rq[j][k] * sc[k] for k in range(3)] for j in range(3)]
    ww = [[rot[i][0] * mm[0][k] + rot[i][1] * mm[1][k] + rot[i][2] * mm[2][k] for k in range(3)] for i in range(3)]
    ax, ay = fx * inv, fy * inv
    r1 = [ax * (ww[0][k] - px * ww[2][k]) for k in range(3)]
    r2 = [ay * (ww[1][k] - py * ww[2][k]) for k in range(3)]
    cxx = r1[0] * r1[0] + r1[1] * r1[1] + r1[2] * r1[2] + blur_floor
    cxy = r1[0] * r2[0] + r1[1] * r2[1] + r1[2] * r2[2]
    cyy = r2[0] * r2[0] + r2[1] * r2[1] + r2[2] * r2[2] + blur_floor
    idet = 1.0 / (cxx * cyy - cxy * cxy)
    fa = (-0.5 * LOG2E) * (cyy * idet)
    fb = LOG2E * (cxy * idet)
    fc = (-0.5 * LOG2E) * (cxx * idet)
    lo = (-LOG2E) * jnp.log(1.0 + jnp.exp(-rows[10]))
    eye = [-(rot[0][i] * shift[0] + rot[1][i] * shift[1] + rot[2][i] * shift[2]) for i in range(3)]
    tw = [m[i] - eye[i] for i in range(3)]
    ti = 1.0 / jnp.sqrt(tw[0] * tw[0] + tw[1] * tw[1] + tw[2] * tw[2])
    dx, dy, dz = [t * ti for t in tw]
    xx, yy, zz = dx * dx, dy * dy, dz * dz
    basis = [
        -sh_one * dy, sh_one * dz, -sh_one * dx,
        sh_two[0] * dx * dy, sh_two[1] * dy * dz, sh_two[2] * (2.0 * zz - xx - yy), sh_two[3] * dx * dz, sh_two[4] * (xx - yy),
        sh_three[0] * dy * (3.0 * xx - yy), sh_three[1] * dx * dy * dz, sh_three[2] * dy * (4.0 * zz - xx - yy),
        sh_three[3] * dz * (2.0 * zz - 3.0 * xx - 3.0 * yy), sh_three[4] * dx * (4.0 * zz - xx - yy),
        sh_three[5] * dz * (xx - yy), sh_three[6] * dx * (xx - 3.0 * yy),
    ]
    cols = []
    for c in range(3):
        acc = sh_zero * rows[11 + c] + 0.5
        for k in range(15):
            acc = acc + basis[k] * rows[14 + 3 * k + c]
        cols.append(acc)
    shape = sx.shape
    return [sx, sy, fa, fb, fc, jnp.broadcast_to(lo, shape)] + cols


def camera_columns(cam_ref):
    return [cam_ref[:, j:j + 1] for j in range(16)]


def slot_map(ids_ref, order_ref, count_ref):
    rowi = lax.broadcasted_iota(jnp.int32, (16, 128), 0)
    lane = lax.broadcasted_iota(jnp.int32, (16, 128), 1)
    owner = jnp.full((16, 128), -1, jnp.int32)
    across = jnp.full((16, 128), -1, jnp.int32)
    for k in range(16):
        o = order_ref[0, 0, k]
        own = jnp.where(o < count_ref[0, 0], ids_ref[0, 0, o] >> 1, -1)
        owner = jnp.where(rowi == k, own, owner)
        across = jnp.where(lane == k, own, across)
    one = (owner == lane).astype(f32)[:, :NT]
    back = (jnp.broadcast_to(across[0:1, :16], (NT, 16)) == lax.broadcasted_iota(jnp.int32, (NT, 16), 0)).astype(f32)
    return one, back, jnp.where(owner[:, 0:1] < 0, -1e4, 0.0)


def slab(ref, t):
    return ref.at[pl.ds(pl.multiple_of(t * ROWS, ROWS), NF)]


STEPS = sorted([(z, y, x) for z in range(2) for y in range(4) for x in range(4)][1:], key=lambda s: -(s[0] + min(s[1], 4 - s[1]) + min(s[2], 4 - s[2])))


def others(me):
    zs = [16 * lax.rem(lax.div(me, 16) + d, 2) for d in range(2)]
    ys = [4 * lax.rem(lax.div(me, 4) + d, 4) for d in range(4)]
    xs = [lax.rem(me + d, 4) for d in range(4)]
    return [zs[z] + ys[y] + xs[x] for z, y, x in STEPS]


def exchange(me, peers, send, recv, sems, wide=True):
    for t in peers:
        src, dst = (slab(send, t), slab(recv, me)) if wide else (send.at[0], recv.at[me])
        pltpu.make_async_remote_copy(src, dst, sems.at[0], sems.at[1], device_id={"tile": t}, device_id_type=MESH).start()


def passed(buf, sem, wide=True):
    whole = buf.at[pl.ds(0, (NT - 1) * (NF if wide else 1))]
    pltpu.make_async_copy(whole, whole, sem).wait()


def stack3(x):
    return jnp.concatenate(part3(x), 0).astype(bf16)


def thrice(onehot):
    return jnp.concatenate([onehot] * 3, 1).astype(bf16)


def gather_rows(recv):
    return jnp.concatenate([jnp.concatenate([recv[pl.ds(t * ROWS + f, 8, stride=ROWS), :] for t in range(0, NT, 8)], 0) for f in range(NF)], 1)


def place_rows(x, send):
    for f in range(NF):
        for t in range(0, NT, 8):
            send[pl.ds(t * ROWS + f, 8, stride=ROWS), :] = x[t:t + 8, f * 128:(f + 1) * 128]


def own_rows(me, send, recv):
    at = pl.ds(pl.multiple_of(me * ROWS, ROWS), ROWS)
    recv[at, :] = send[at, :]


def step_kernel(gauss_hbm, cons_hbm, dual_hbm, targ_hbm, step_hbm, cam_hbm, inter_hbm, ids_hbm, order_hbm, cid_ref, count_ref, upd_ref, newd_ref,
                gauss_ref, cons_ref, dual_ref, t_ref, step_ref, cam_ref, inter_ref, ids_ref, order_ref, local_sem,
                req, reqs, fbuf, send, recv, gsend, grecv, grad, base, vals, near, e1, e2, e3, s4, r4,
                alpha, wts, gbuf, lhs, csp, tb, cb, bend, grhs, a0, a1, a2, a3, rq):
    me = lax.axis_index("tile")
    grp = lax.axis_index("scene")
    last = lax.axis_size("scene") - 1
    loads = [pltpu.make_async_copy(x, y, local_sem.at[i]) for i, (x, y) in enumerate((
        (ids_hbm, ids_ref), (order_hbm, order_ref), (cam_hbm, cam_ref), (gauss_hbm, gauss_ref),
        (cons_hbm, cons_ref), (dual_hbm, dual_ref), (targ_hbm, t_ref), (step_hbm, step_ref), (inter_hbm, inter_ref)))]
    for l in loads:
        l.start()
    near[...] = jnp.zeros_like(near)
    barrier = pltpu.get_barrier_semaphore()

    peers = others(me)
    for t in peers:
        pl.semaphore_signal(barrier, inc=1, device_id={"tile": t}, device_id_type=MESH)

    @pl.when(grp < last)
    def _():
        pl.semaphore_signal(barrier, inc=1, device_id={"scene": grp + 1}, device_id_type=MESH)

    @pl.when(grp > 0)
    def _():
        pl.semaphore_signal(barrier, inc=1, device_id={"scene": grp - 1}, device_id_type=MESH)
    loads[0].wait()
    lane = lax.broadcasted_iota(jnp.int32, (1, 128), 1)
    ask = jnp.full((1, 128), cid_ref[0, 0], jnp.int32)
    for k in range(16):
        b = ids_ref[0, 0, k]
        ask = ask + jnp.where(lane == (b >> 1), (b & 1) * 16, 0)
    req[0] = ask
    reqs[me] = ask
    loads[2].wait()
    loads[3].wait()
    cam = camera_columns(cam_ref)
    outs = [features([gauss_ref[0, i, b:b + 1, :] for i in range(59)], cam) for b in range(2)]
    fbuf[...] = stack3(jnp.concatenate([jnp.concatenate(o, 1) for o in outs], 0))
    pl.semaphore_wait(barrier, NT - 1 + jnp.where(grp < last, 1, 0) + jnp.where(grp > 0, 1, 0))
    exchange(me, peers, req, reqs, e1, False)
    loads[1].wait()
    one, back, bias = slot_map(ids_ref, order_ref, count_ref)
    for l in loads[4:]:
        l.wait()
    passed(reqs, e1.at[1], False)
    asked = jnp.concatenate([reqs[t] for t in range(NT)], 0)
    lane32 = lax.broadcasted_iota(jnp.int32, (NT, 128), 1)
    col = jnp.sum(jnp.where(lane32 == me, asked, 0).astype(f32), 1, keepdims=True).astype(jnp.int32)
    sel = (col == lax.broadcasted_iota(jnp.int32, (NT, NT), 1)).astype(f32)
    place_rows(jnp.dot(thrice(sel), fbuf[...], preferred_element_type=f32), send)
    own_rows(me, send, recv)
    exchange(me, peers, send, recv, e2)
    one3 = thrice(one)
    passed(recv, e2.at[1])
    y = jnp.dot(one3, stack3(gather_rows(recv)), preferred_element_type=f32)
    targ = [jnp.concatenate([t_ref[0, c, 0:1, y0 * 128:(y0 + 1) * 128] for y0 in range(8)], 0) for c in range(3)]
    ybase = (8 * lax.rem(me, 4)).astype(f32)
    outs = render_body(ybase, [y[:, f * 128:(f + 1) * 128] for f in range(NF)], targ, bias, alpha, wts, gbuf, lhs, csp, tb, cb, bend, grhs, (a0, a1, (a2, a3)), rq)
    place_rows(jnp.dot(thrice(back), stack3(jnp.concatenate(outs, 1)), preferred_element_type=f32), gsend)
    own_rows(me, gsend, grecv)
    exchange(me, peers, gsend, grecv, e3)
    turned = jnp.concatenate([jnp.broadcast_to(col, (NT, 128)).astype(f32), jnp.zeros((96, 128), f32)], 0).T
    selt = thrice((turned[:NT, :NT].astype(jnp.int32) == lax.broadcasted_iota(jnp.int32, (NT, NT), 0)).astype(f32))
    idx = jnp.concatenate([inter_ref[0, 0, 0:1, :], inter_ref[0, 0, 1:2, :]], 1)
    picks = [(lax.broadcasted_iota(jnp.int32, (128, 128), 0) + b * 128 == idx).astype(f32) for b in range(2)]
    pulls = []
    for b in range(2):
        rows = [gauss_ref[0, i, b:b + 1, :] for i in range(59)]
        pulls.append(jax.vjp(lambda r: features(r, cam), rows)[1])
    for i in range(59):
        base[i] = gauss_ref[0, i] - (penalty_weight * step_ref[i]) * (gauss_ref[0, i] - cons_ref[0, i] + dual_ref[0, i])
    passed(grecv, e3.at[1])
    df = jnp.dot(selt, stack3(gather_rows(grecv)), preferred_element_type=f32)
    for b in range(2):
        (grows,) = pulls[b]([df[b * 16:(b + 1) * 16, f * 128:(f + 1) * 128] for f in range(NF)])
        for i in range(59):
            u = base[i, b:b + 1, :] - step_ref[i] * grows[i]
            upd_ref[0, i, b:b + 1, :] = u
            grad[b, i:i + 1, :] = u + dual_ref[0, i, b:b + 1, :]
    grad[:, 59:64, :] = jnp.zeros((2, 5, 128), f32)
    picks3 = [jnp.concatenate([p] * 3, 0).astype(bf16) for p in picks]
    v = sum(jnp.dot(jnp.concatenate(part3(grad[b]), 1).astype(bf16), picks3[b], preferred_element_type=f32) for b in range(2))
    lane = lax.broadcasted_iota(jnp.int32, (32, 128), 1)
    low, high = v[:32], v[32:]
    vals[0] = jnp.where(lane < 64, low, pltpu.roll(high, 64, 1))
    vals[1] = jnp.where(lane < 64, pltpu.roll(low, 64, 1), high)

    def up():
        return pltpu.make_async_remote_copy(vals.at[0], near.at[0], s4.at[0], r4.at[0], device_id={"scene": lax.rem(grp + 1, last + 1)}, device_id_type=MESH)

    def down():
        return pltpu.make_async_remote_copy(vals.at[1], near.at[1], s4.at[1], r4.at[1], device_id={"scene": lax.rem(grp + last, last + 1)}, device_id_type=MESH)

    @pl.when(grp < last)
    def _():
        up().start()

    @pl.when(grp > 0)
    def _():
        down().start()

    @pl.when(grp > 0)
    def _():
        up().wait_recv()
        down().wait_send()

    @pl.when(grp < last)
    def _():
        down().wait_recv()
        up().wait_send()
    from_above = jnp.where(grp < last, 0.5 * (vals[0] - near[1]), 0.0)
    from_below = jnp.where(grp > 0, 0.5 * (vals[1] - near[0]), 0.0)
    diff = jnp.concatenate([
        jnp.where(lane < 64, from_above, pltpu.roll(from_below, 64, 1)),
        jnp.where(lane < 64, pltpu.roll(from_above, 64, 1), from_below),
    ], 0)
    diff3 = jnp.concatenate(part3(diff), 1).astype(bf16)
    for b in range(2):
        p3 = jnp.concatenate([picks[b]] * 3, 1).astype(bf16)
        nd = lax.dot_general(diff3, p3, (((1,), (1,)), ((), ())), preferred_element_type=f32)
        for i in range(59):
            newd_ref[0, i, b:b + 1, :] = nd[i:i + 1, :]
    passed(reqs, e1.at[0], False)
    passed(send, e2.at[0])
    passed(gsend, e3.at[0])


VM = pl.BlockSpec(memory_space=pltpu.VMEM)
SM = pl.BlockSpec(memory_space=pltpu.SMEM)
HB = pl.BlockSpec(memory_space=pltpu.HBM)
DMA = pltpu.SemaphoreType.DMA


def on_device(gaussians, consensus, duals, step_sizes, cameras, camera_ids, block_lists, depth_order, block_counts, targets, intersection):
    def sd(shape, t=f32):
        return jax.ShapeDtypeStruct(shape, t)
    gaussians, consensus, duals, targets = [a.transpose(0, 2, 1, 3) for a in (gaussians, consensus, duals, targets)]
    big = sd((1, 59, 2, 128))
    gaussians, consensus, duals, targets, cameras, intersection, step_sizes, block_lists, depth_order = [
        pltpu.with_memory_space_constraint(a, pltpu.HBM)
        for a in (gaussians, consensus, duals, targets, cameras, intersection, step_sizes, block_lists, depth_order)
    ]
    out = pl.pallas_call(
        step_kernel, name="step", out_shape=(big, big),
        in_specs=[HB] * 9 + [SM, SM], out_specs=(VM, VM),
        scratch_shapes=[
            pltpu.VMEM((1, 59, 2, 128), f32), pltpu.VMEM((1, 59, 2, 128), f32), pltpu.VMEM((1, 59, 2, 128), f32), pltpu.VMEM((1, 3, 1, 1024), f32),
            pltpu.SMEM((59,), f32), pltpu.VMEM((16, 16), f32), pltpu.VMEM((1, 1, 2, 64), jnp.int32), pltpu.SMEM((1, 1, 16), jnp.int32), pltpu.SMEM((1, 1, 16), jnp.int32), DMA((9,)),
            pltpu.VMEM((1, 1, 128), jnp.int32), pltpu.VMEM((NT, 1, 128), jnp.int32), pltpu.VMEM((3 * NT, NF * 128), bf16),
            pltpu.VMEM((NT * ROWS, 128), f32), pltpu.VMEM((NT * ROWS, 128), f32), pltpu.VMEM((NT * ROWS, 128), f32), pltpu.VMEM((NT * ROWS, 128), f32),
            pltpu.VMEM((2, 64, 128), f32), pltpu.VMEM((59, 2, 128), f32), pltpu.VMEM((2, 32, 128), f32), pltpu.VMEM((2, 32, 128), f32),
            DMA((2,)), DMA((2,)), DMA((2,)), DMA((2,)), DMA((2,)),
        ] + RENDER_SCRATCH,
        compiler_params=pltpu.CompilerParams(collective_id=0, has_side_effects=True, vmem_limit_bytes=VMEM_LIMIT),
    )(gaussians, consensus, duals, targets, step_sizes, cameras, intersection, block_lists, depth_order, camera_ids, block_counts)
    return tuple(a.transpose(0, 2, 1, 3) for a in out)


def solution(mesh):
    t4, t3, t2 = P("scene", "tile", None, None), P("scene", "tile", None), P("scene", "tile")
    return jax.shard_map(
        on_device, mesh=mesh,
        in_specs=(t4, t4, t4, P(), P(), t2, t3, t3, t2, t4, t4),
        out_specs=(t4, t4), check_vma=False,
    )
```

```python
import functools

import jax
import jax.numpy as jnp
from jax import lax
from jax.experimental import pallas as pl
from jax.experimental.pallas import tpu as pltpu
from jax.sharding import PartitionSpec as P

HI = lax.Precision.HIGHEST
f32, bf16 = jnp.float32, jnp.bfloat16
MESH = pl.DeviceIdType.MESH
S = 132
SB = 8 * S
NI = 4
LN2 = 0.6931471805599453

def part2(v):
    a = v.astype(bf16)
    return a, (v - a.astype(f32)).astype(bf16)

def part3(v):
    a = v.astype(bf16).astype(f32)
    r = v - a
    b = r.astype(bf16).astype(f32)
    return a, b, (r - b).astype(bf16).astype(f32)

def render_body(ybase, feats, targ, bias, alpha, wts, gbuf, lhs, csp, tb, cb, bend, grhs, acc, rq):
    sx, sy, fa, fb, fc, lo, k0, k1, k2 = feats
    sxc = sx - 64.0
    syc = sy - (ybase + 3.5)
    lob = lo + bias
    zero32 = jnp.zeros((32, 128), f32)
    pa = part3(fa)
    lhs_a = jnp.concatenate(list(pa) + list(pa) + [zero32], 0).T.astype(bf16)
    for y in range(8):
        dy = (y - 3.5) - syc
        c1 = fb * dy - 2.0 * fa * sxc
        c0 = (fa * sxc - fb * dy) * sxc + fc * dy * dy + lob
        m = jnp.concatenate(list(part3(c0)) + list(part3(c1)) + [zero32], 0)
        lhs[y * 128:(y + 1) * 128, 0:128] = m.T.astype(bf16)
        lhs[y * 128:(y + 1) * 128, 128:256] = lhs_a
    colt = jnp.concatenate([k0, k1, k2, jnp.zeros((80, 128), f32)], 0).T
    kr = lax.broadcasted_iota(jnp.int32, (256, 256), 0)
    ln = lax.broadcasted_iota(jnp.int32, (256, 256), 1)
    xi = ((ln & 127) - 64).astype(f32)
    x2 = xi * xi
    x2h = x2.astype(bf16).astype(f32)
    x2l = x2 - x2h
    basis = jnp.where(kr < 48, 1.0, jnp.where(kr < 96, xi, jnp.where(kr < 128, 0.0, jnp.where(kr < 176, x2h, jnp.where(kr < 224, x2l, 0.0)))))
    grhs[...] = basis
    for p in range(8):
        rhs = jnp.where((kr & 15) == 2 * p + (ln >> 7), grhs[...], 0.0).astype(bf16)
        for y in range(8):
            e = jnp.dot(lhs[y * 128:(y + 1) * 128, :], rhs, preferred_element_type=f32)
            a = jnp.minimum(0.99, jnp.exp2(e))
            alpha[2 * p * SB + y * S:2 * p * SB + y * S + 128, :] = a[:, :128]
            alpha[(2 * p + 1) * SB + y * S:(2 * p + 1) * SB + y * S + 128, :] = a[:, 128:]
        for b in (2 * p, 2 * p + 1):
            for c in range(3):
                csp[c, b * 128:(b + 1) * 128, :] = jnp.broadcast_to(colt[:, c * 16 + b:c * 16 + b + 1], (128, 128))
    one = jnp.ones((8, 128), f32)
    zero = jnp.zeros((8, 128), f32)
    U = 32
    for q0 in range(0, 16, NI):
        def fwd(i, carry):
            st = [list(t) for t in carry]
            for u in range(U):
                g = i * U + u
                for j in range(NI):
                    b = q0 + j
                    a = alpha[pl.ds(b * SB + g, 8, stride=S), :]
                    t, s0, s1, s2 = st[j]
                    w = a * t
                    t = t * (1.0 - a)
                    row = b * 128 + g
                    s0 = s0 + w * csp[0, pl.ds(row, 8, stride=0), :]
                    s1 = s1 + w * csp[1, pl.ds(row, 8, stride=0), :]
                    s2 = s2 + w * csp[2, pl.ds(row, 8, stride=0), :]
                    wts[pl.ds(b * SB + g, 8, stride=S), :] = w
                    st[j] = [t, s0, s1, s2]
            return tuple(tuple(t) for t in st)
        out = lax.fori_loop(0, 128 // U, fwd, tuple((one, zero, zero, zero) for _ in range(NI)))
        for j in range(NI):
            tb[q0 + j] = out[j][0]
            for c in range(3):
                cb[c, q0 + j] = out[j][1 + c]
    t = one
    prods = [tb[b] for b in range(16)]
    cs = [zero, zero, zero]
    for b in range(16):
        tb[b] = t
        for c in range(3):
            cs[c] = cs[c] + t * cb[c, b]
        t = t * prods[b]
    r = [cs[c] - targ[c] for c in range(3)]
    e = zero
    for b in range(15, -1, -1):
        bend[b] = e
        e = prods[b] * e + (cb[0, b] * r[0] + cb[1, b] * r[1] + cb[2, b] * r[2])
    for q0 in range(0, 16, NI):
        rs = [[tb[q0 + j] * r[c] for c in range(3)] for j in range(NI)]
        def bwd(i, carry):
            st = list(carry)
            g0 = (128 // U - 1 - i) * U
            for u in range(U - 1, -1, -1):
                g = g0 + u
                for j in range(NI):
                    b = q0 + j
                    a = alpha[pl.ds(b * SB + g, 8, stride=S), :]
                    w = wts[pl.ds(b * SB + g, 8, stride=S), :]
                    row = b * 128 + g
                    q = (rs[j][0] * csp[0, pl.ds(row, 8, stride=0), :] + rs[j][1] * csp[1, pl.ds(row, 8, stride=0), :]) + rs[j][2] * csp[2, pl.ds(row, 8, stride=0), :]
                    d = q - st[j]
                    gbuf[pl.ds(b * SB + g, 8, stride=S), :] = jnp.where(a < 0.99, w * d, 0.0)
                    st[j] = st[j] + a * d
            return tuple(st)
        lax.fori_loop(0, 128 // U, bwd, tuple(tb[q0 + j] * bend[q0 + j] for j in range(NI)))
    mt, phi, xs = acc
    xf = (lax.broadcasted_iota(jnp.int32, (16, 128), 1) - 64).astype(f32)
    kk = lax.broadcasted_iota(jnp.int32, (16, 128), 0)
    xx = xf * xf
    xxh = xx.astype(bf16).astype(f32)
    plans = ({0: 1.0, 1: xf, 2: xxh, 3: xx - xxh}, {4: 1.0, 5: xf}, {6: 1.0}, {7: 1.0}, {8: 1.0}, {9: 1.0})
    for i, plan in enumerate(plans):
        v = jnp.zeros((16, 128), f32)
        for k, w in plan.items():
            v = jnp.where(kk == k, w, v)
        phi[:, i * 256:i * 256 + 128] = v.astype(bf16)
        phi[:, i * 256 + 128:i * 256 + 256] = v.astype(bf16)
    nt = (((1,), (1,)), ((), ()))
    for c in range(3):
        rq[c] = r[c]
    xa, xb = xs
    def fill(b, dst):
        tbb = tb[b]
        base = b * SB if isinstance(b, int) else pl.multiple_of(b * SB, 8)
        rows = []
        for c in range(3):
            v = rq[c] * tbb
            rows.append([v[y:y + 1, :] for y in range(8)])
        for n in range(8):
            at = base + n * 16
            g = [gbuf[pl.ds(at + y * S, 16), :] for y in range(8)]
            sm = [g[4 + k] + g[3 - k] for k in range(4)]
            df = [g[4 + k] - g[3 - k] for k in range(4)]
            out = [(sm[0] + sm[1]) + (sm[2] + sm[3]),
                   (0.5 * df[0] + 1.5 * df[1]) + (2.5 * df[2] + 3.5 * df[3]),
                   (0.25 * sm[0] + 2.25 * sm[1]) + (6.25 * sm[2] + 12.25 * sm[3])]
            w = [wts[pl.ds(at + y * S, 16), :] for y in range(8)]
            for c in range(3):
                t = [w[y] * rows[c][y] for y in range(8)]
                out.append(((t[0] + t[1]) + (t[2] + t[3])) + ((t[4] + t[5]) + (t[6] + t[7])))
            for i in range(6):
                h, l = part2(out[i])
                dst[n * 16:(n + 1) * 16, i * 256:i * 256 + 128] = h
                dst[n * 16:(n + 1) * 16, i * 256 + 128:i * 256 + 256] = l
    def contract(b, src):
        mt[pl.ds(b * 17, 16), :] = lax.dot_general(phi[...], src[...], nt, preferred_element_type=f32)
    fill(0, xa)
    def red(i, _):
        contract(2 * i, xa)
        fill(2 * i + 1, xb)
        contract(2 * i + 1, xb)
        fill(2 * i + 2, xa)
        return 0
    lax.fori_loop(0, 7, red, 0)
    contract(14, xa)
    fill(15, xb)
    contract(15, xb)
    M = [jnp.concatenate([mt[pl.ds(k, 8, stride=17), :], mt[pl.ds(8 * 17 + k, 8, stride=17), :]], 0) for k in range(10)]
    M0 = M[0] * LN2
    Mx = M[1] * LN2
    Mxx = (M[2] + M[3]) * LN2
    My = M[4] * LN2
    Mxy = M[5] * LN2
    Myy = M[6] * LN2
    ux = Mx - sxc * M0
    uy = My - syc * M0
    d_a = Mxx - sxc * (Mx + ux)
    d_b = Mxy - syc * Mx - sxc * uy
    d_c = Myy - syc * (My + uy)
    d_sx = -(2.0 * fa * ux + fb * uy)
    d_sy = -(fb * ux + 2.0 * fc * uy)
    return [d_sx, d_sy, d_a, d_b, d_c, M0, M[7], M[8], M[9]]

RENDER_SCRATCH = [
    pltpu.VMEM((16 * SB, 128), f32), pltpu.VMEM((16 * SB, 128), f32), pltpu.VMEM((16 * SB, 128), f32),
    pltpu.VMEM((1024, 256), bf16), pltpu.VMEM((3, 2048, 128), f32),
    pltpu.VMEM((16, 8, 128), f32), pltpu.VMEM((3, 16, 8, 128), f32), pltpu.VMEM((16, 8, 128), f32),
    pltpu.VMEM((256, 256), f32),
    pltpu.VMEM((16 * 17 + 8, 128), f32), pltpu.VMEM((16, 1536), bf16), pltpu.VMEM((128, 1536), bf16), pltpu.VMEM((128, 1536), bf16), pltpu.VMEM((3, 8, 128), f32),
]

LOG2E = 1.4426950408889634
blur_floor = 0.3
penalty_weight = 0.5
sh_zero = 0.28209479177387814
sh_one = 0.4886025119029199
sh_two = (1.0925484305920792, -1.0925484305920792, 0.31539156525252005, -1.0925484305920792, 0.5462742152960396)
sh_three = (-0.5900435899266435, 2.890611442640554, -0.4570457994644658, 0.3731763325901154, -0.4570457994644658, 1.445305721320277, -0.5900435899266435)
NT = 32
NF = 9
VMEM_LIMIT = 40 * 1024 * 1024
ROWS = 16


def features(rows, cam):
    rot = [[cam[3 * i + j] for j in range(3)] for i in range(3)]
    shift = cam[9:12]
    fx, fy, cx, cy = cam[12:16]
    m = rows[0:3]
    e = [rot[i][0] * m[0] + rot[i][1] * m[1] + rot[i][2] * m[2] + shift[i] for i in range(3)]
    inv = 1.0 / e[2]
    px = e[0] * inv
    py = e[1] * inv
    sx = fx * px + cx
    sy = fy * py + cy
    qn = rows[6] * rows[6] + rows[7] * rows[7] + rows[8] * rows[8] + rows[9] * rows[9]
    qi = 1.0 / jnp.sqrt(qn)
    w, x, y, z = [rows[6 + i] * qi for i in range(4)]
    rq = [
        [1.0 - 2.0 * (y * y + z * z), 2.0 * (x * y - w * z), 2.0 * (x * z + w * y)],
        [2.0 * (x * y + w * z), 1.0 - 2.0 * (x * x + z * z), 2.0 * (y * z - w * x)],
        [2.0 * (x * z - w * y), 2.0 * (y * z + w * x), 1.0 - 2.0 * (x * x + y * y)],
    ]
    sc = [jnp.exp(rows[3 + k]) for k in range(3)]
    mm = [[rq[j][k] * sc[k] for k in range(3)] for j in range(3)]
    ww = [[rot[i][0] * mm[0][k] + rot[i][1] * mm[1][k] + rot[i][2] * mm[2][k] for k in range(3)] for i in range(3)]
    ax, ay = fx * inv, fy * inv
    r1 = [ax * (ww[0][k] - px * ww[2][k]) for k in range(3)]
    r2 = [ay * (ww[1][k] - py * ww[2][k]) for k in range(3)]
    cxx = r1[0] * r1[0] + r1[1] * r1[1] + r1[2] * r1[2] + blur_floor
    cxy = r1[0] * r2[0] + r1[1] * r2[1] + r1[2] * r2[2]
    cyy = r2[0] * r2[0] + r2[1] * r2[1] + r2[2] * r2[2] + blur_floor
    idet = 1.0 / (cxx * cyy - cxy * cxy)
    fa = (-0.5 * LOG2E) * (cyy * idet)
    fb = LOG2E * (cxy * idet)
    fc = (-0.5 * LOG2E) * (cxx * idet)
    lo = (-LOG2E) * jnp.log(1.0 + jnp.exp(-rows[10]))
    eye = [-(rot[0][i] * shift[0] + rot[1][i] * shift[1] + rot[2][i] * shift[2]) for i in range(3)]
    tw = [m[i] - eye[i] for i in range(3)]
    ti = 1.0 / jnp.sqrt(tw[0] * tw[0] + tw[1] * tw[1] + tw[2] * tw[2])
    dx, dy, dz = [t * ti for t in tw]
    xx, yy, zz = dx * dx, dy * dy, dz * dz
    basis = [
        -sh_one * dy, sh_one * dz, -sh_one * dx,
        sh_two[0] * dx * dy, sh_two[1] * dy * dz, sh_two[2] * (2.0 * zz - xx - yy), sh_two[3] * dx * dz, sh_two[4] * (xx - yy),
        sh_three[0] * dy * (3.0 * xx - yy), sh_three[1] * dx * dy * dz, sh_three[2] * dy * (4.0 * zz - xx - yy),
        sh_three[3] * dz * (2.0 * zz - 3.0 * xx - 3.0 * yy), sh_three[4] * dx * (4.0 * zz - xx - yy),
        sh_three[5] * dz * (xx - yy), sh_three[6] * dx * (xx - 3.0 * yy),
    ]
    cols = []
    for c in range(3):
        acc = sh_zero * rows[11 + c] + 0.5
        for k in range(15):
            acc = acc + basis[k] * rows[14 + 3 * k + c]
        cols.append(acc)
    shape = sx.shape
    return [sx, sy, fa, fb, fc, jnp.broadcast_to(lo, shape)] + cols


def camera_columns(cam_ref):
    return [cam_ref[:, j:j + 1] for j in range(16)]


def slot_map(ids_ref, order_ref, count_ref):
    rowi = lax.broadcasted_iota(jnp.int32, (16, 128), 0)
    lane = lax.broadcasted_iota(jnp.int32, (16, 128), 1)
    owner = jnp.full((16, 128), -1, jnp.int32)
    across = jnp.full((16, 128), -1, jnp.int32)
    for k in range(16):
        o = order_ref[0, 0, k]
        own = jnp.where(o < count_ref[0, 0], ids_ref[0, 0, o] >> 1, -1)
        owner = jnp.where(rowi == k, own, owner)
        across = jnp.where(lane == k, own, across)
    one = (owner == lane).astype(f32)[:, :NT]
    back = (jnp.broadcast_to(across[0:1, :16], (NT, 16)) == lax.broadcasted_iota(jnp.int32, (NT, 16), 0)).astype(f32)
    return one, back, jnp.where(owner[:, 0:1] < 0, -1e4, 0.0)


def slab(ref, t):
    return ref.at[pl.ds(pl.multiple_of(t * ROWS, ROWS), NF)]


STEPS = sorted([(z, y, x) for z in range(2) for y in range(4) for x in range(4)][1:], key=lambda s: -(s[0] + min(s[1], 4 - s[1]) + min(s[2], 4 - s[2])))


def others(me):
    zs = [16 * lax.rem(lax.div(me, 16) + d, 2) for d in range(2)]
    ys = [4 * lax.rem(lax.div(me, 4) + d, 4) for d in range(4)]
    xs = [lax.rem(me + d, 4) for d in range(4)]
    return [zs[z] + ys[y] + xs[x] for z, y, x in STEPS]


def exchange(me, peers, send, recv, sems, wide=True):
    for t in peers:
        src, dst = (slab(send, t), slab(recv, me)) if wide else (send.at[0], recv.at[me])
        pltpu.make_async_remote_copy(src, dst, sems.at[0], sems.at[1], device_id={"tile": t}, device_id_type=MESH).start()


def passed(buf, sem, wide=True):
    whole = buf.at[pl.ds(0, (NT - 1) * (NF if wide else 1))]
    pltpu.make_async_copy(whole, whole, sem).wait()


def stack3(x):
    return jnp.concatenate(part3(x), 0).astype(bf16)


def thrice(onehot):
    return jnp.concatenate([onehot] * 3, 1).astype(bf16)


def gather_rows(recv):
    return jnp.concatenate([jnp.concatenate([recv[pl.ds(t * ROWS + f, 8, stride=ROWS), :] for t in range(0, NT, 8)], 0) for f in range(NF)], 1)


def place_rows(x, send):
    for f in range(NF):
        for t in range(0, NT, 8):
            send[pl.ds(t * ROWS + f, 8, stride=ROWS), :] = x[t:t + 8, f * 128:(f + 1) * 128]


def own_rows(me, send, recv):
    at = pl.ds(pl.multiple_of(me * ROWS, ROWS), ROWS)
    recv[at, :] = send[at, :]


def step_kernel(gauss_hbm, cons_hbm, dual_hbm, targ_hbm, step_hbm, cam_hbm, inter_hbm, ids_hbm, order_hbm, cid_ref, count_ref, upd_ref, newd_ref,
                gauss_ref, cons_ref, dual_ref, t_ref, step_ref, cam_ref, inter_ref, ids_ref, order_ref, local_sem,
                req, reqs, fbuf, send, recv, gsend, grecv, grad, base, vals, near, e1, e2, e3, s4, r4,
                alpha, wts, gbuf, lhs, csp, tb, cb, bend, grhs, a0, a1, a2, a3, rq):
    me = lax.axis_index("tile")
    grp = lax.axis_index("scene")
    last = lax.axis_size("scene") - 1
    loads = [pltpu.make_async_copy(x, y, local_sem.at[i]) for i, (x, y) in enumerate((
        (ids_hbm, ids_ref), (order_hbm, order_ref), (cam_hbm, cam_ref), (gauss_hbm, gauss_ref),
        (cons_hbm, cons_ref), (dual_hbm, dual_ref), (targ_hbm, t_ref), (step_hbm, step_ref), (inter_hbm, inter_ref)))]
    for l in loads:
        l.start()
    near[...] = jnp.zeros_like(near)
    barrier = pltpu.get_barrier_semaphore()

    peers = others(me)
    for t in peers:
        pl.semaphore_signal(barrier, inc=1, device_id={"tile": t}, device_id_type=MESH)

    @pl.when(grp < last)
    def _():
        pl.semaphore_signal(barrier, inc=1, device_id={"scene": grp + 1}, device_id_type=MESH)

    @pl.when(grp > 0)
    def _():
        pl.semaphore_signal(barrier, inc=1, device_id={"scene": grp - 1}, device_id_type=MESH)
    loads[0].wait()
    lane = lax.broadcasted_iota(jnp.int32, (1, 128), 1)
    ask = jnp.full((1, 128), cid_ref[0, 0], jnp.int32)
    for k in range(16):
        b = ids_ref[0, 0, k]
        ask = ask + jnp.where(lane == (b >> 1), (b & 1) * 16, 0)
    req[0] = ask
    reqs[me] = ask
    loads[2].wait()
    loads[3].wait()
    cam = camera_columns(cam_ref)
    outs = [features([gauss_ref[0, i, b:b + 1, :] for i in range(59)], cam) for b in range(2)]
    fbuf[...] = stack3(jnp.concatenate([jnp.concatenate(o, 1) for o in outs], 0))
    pl.semaphore_wait(barrier, NT - 1 + jnp.where(grp < last, 1, 0) + jnp.where(grp > 0, 1, 0))
    exchange(me, peers, req, reqs, e1, False)
    loads[1].wait()
    one, back, bias = slot_map(ids_ref, order_ref, count_ref)
    for l in loads[4:]:
        l.wait()
    passed(reqs, e1.at[1], False)
    asked = jnp.concatenate([reqs[t] for t in range(NT)], 0)
    lane32 = lax.broadcasted_iota(jnp.int32, (NT, 128), 1)
    col = jnp.sum(jnp.where(lane32 == me, asked, 0).astype(f32), 1, keepdims=True).astype(jnp.int32)
    sel = (col == lax.broadcasted_iota(jnp.int32, (NT, NT), 1)).astype(f32)
    place_rows(jnp.dot(thrice(sel), fbuf[...], preferred_element_type=f32), send)
    own_rows(me, send, recv)
    exchange(me, peers, send, recv, e2)
    one3 = thrice(one)
    passed(recv, e2.at[1])
    y = jnp.dot(one3, stack3(gather_rows(recv)), preferred_element_type=f32)
    targ = [jnp.concatenate([t_ref[0, c, 0:1, y0 * 128:(y0 + 1) * 128] for y0 in range(8)], 0) for c in range(3)]
    ybase = (8 * lax.rem(me, 4)).astype(f32)
    outs = render_body(ybase, [y[:, f * 128:(f + 1) * 128] for f in range(NF)], targ, bias, alpha, wts, gbuf, lhs, csp, tb, cb, bend, grhs, (a0, a1, (a2, a3)), rq)
    place_rows(jnp.dot(thrice(back), stack3(jnp.concatenate(outs, 1)), preferred_element_type=f32), gsend)
    own_rows(me, gsend, grecv)
    exchange(me, peers, gsend, grecv, e3)
    turned = jnp.concatenate([jnp.broadcast_to(col, (NT, 128)).astype(f32), jnp.zeros((96, 128), f32)], 0).T
    selt = thrice((turned[:NT, :NT].astype(jnp.int32) == lax.broadcasted_iota(jnp.int32, (NT, NT), 0)).astype(f32))
    idx = jnp.concatenate([inter_ref[0, 0, 0:1, :], inter_ref[0, 0, 1:2, :]], 1)
    picks = [(lax.broadcasted_iota(jnp.int32, (128, 128), 0) + b * 128 == idx).astype(f32) for b in range(2)]
    pulls = []
    for b in range(2):
        rows = [gauss_ref[0, i, b:b + 1, :] for i in range(59)]
        pulls.append(jax.vjp(lambda r: features(r, cam), rows)[1])
    for i in range(59):
        base[i] = gauss_ref[0, i] - (penalty_weight * step_ref[i]) * (gauss_ref[0, i] - cons_ref[0, i] + dual_ref[0, i])
    passed(grecv, e3.at[1])
    df = jnp.dot(selt, stack3(gather_rows(grecv)), preferred_element_type=f32)
    for b in range(2):
        (grows,) = pulls[b]([df[b * 16:(b + 1) * 16, f * 128:(f + 1) * 128] for f in range(NF)])
        for i in range(59):
            u = base[i, b:b + 1, :] - step_ref[i] * grows[i]
            upd_ref[0, i, b:b + 1, :] = u
            grad[b, i:i + 1, :] = u + dual_ref[0, i, b:b + 1, :]
    grad[:, 59:64, :] = jnp.zeros((2, 5, 128), f32)
    picks3 = [jnp.concatenate([p] * 3, 0).astype(bf16) for p in picks]
    v = sum(jnp.dot(jnp.concatenate(part3(grad[b]), 1).astype(bf16), picks3[b], preferred_element_type=f32) for b in range(2))
    lane = lax.broadcasted_iota(jnp.int32, (32, 128), 1)
    low, high = v[:32], v[32:]
    vals[0] = jnp.where(lane < 64, low, pltpu.roll(high, 64, 1))
    vals[1] = jnp.where(lane < 64, pltpu.roll(low, 64, 1), high)

    def up():
        return pltpu.make_async_remote_copy(vals.at[0], near.at[0], s4.at[0], r4.at[0], device_id={"scene": lax.rem(grp + 1, last + 1)}, device_id_type=MESH)

    def down():
        return pltpu.make_async_remote_copy(vals.at[1], near.at[1], s4.at[1], r4.at[1], device_id={"scene": lax.rem(grp + last, last + 1)}, device_id_type=MESH)

    @pl.when(grp < last)
    def _():
        up().start()

    @pl.when(grp > 0)
    def _():
        down().start()

    @pl.when(grp > 0)
    def _():
        up().wait_recv()
        down().wait_send()

    @pl.when(grp < last)
    def _():
        down().wait_recv()
        up().wait_send()
    from_above = jnp.where(grp < last, 0.5 * (vals[0] - near[1]), 0.0)
    from_below = jnp.where(grp > 0, 0.5 * (vals[1] - near[0]), 0.0)
    diff = jnp.concatenate([
        jnp.where(lane < 64, from_above, pltpu.roll(from_below, 64, 1)),
        jnp.where(lane < 64, pltpu.roll(from_above, 64, 1), from_below),
    ], 0)
    diff3 = jnp.concatenate(part3(diff), 1).astype(bf16)
    for b in range(2):
        p3 = jnp.concatenate([picks[b]] * 3, 1).astype(bf16)
        nd = lax.dot_general(diff3, p3, (((1,), (1,)), ((), ())), preferred_element_type=f32)
        for i in range(59):
            newd_ref[0, i, b:b + 1, :] = nd[i:i + 1, :]
    passed(reqs, e1.at[0], False)
    passed(send, e2.at[0])
    passed(gsend, e3.at[0])


def deliver_kernel(a_ref, b_ref, a_out, b_out, sem):
    moves = [pltpu.make_async_copy(a_ref, a_out, sem.at[0]), pltpu.make_async_copy(b_ref, b_out, sem.at[1])]
    for m in moves:
        m.start()
    for m in moves:
        m.wait()


ANY = pl.BlockSpec(memory_space=pl.ANY)
VM = pl.BlockSpec(memory_space=pltpu.VMEM)
SM = pl.BlockSpec(memory_space=pltpu.SMEM)
HB = pl.BlockSpec(memory_space=pltpu.HBM)
DMA = pltpu.SemaphoreType.DMA


def on_device(gaussians, consensus, duals, step_sizes, cameras, camera_ids, block_lists, depth_order, block_counts, targets, intersection):
    def sd(shape, t=f32):
        return jax.ShapeDtypeStruct(shape, t)
    gaussians, consensus, duals, targets = [a.transpose(0, 2, 1, 3) for a in (gaussians, consensus, duals, targets)]
    big = sd((1, 59, 2, 128))
    gaussians, consensus, duals, targets, cameras, intersection, step_sizes, block_lists, depth_order = [
        pltpu.with_memory_space_constraint(a, pltpu.HBM)
        for a in (gaussians, consensus, duals, targets, cameras, intersection, step_sizes, block_lists, depth_order)
    ]
    out = pl.pallas_call(
        step_kernel, name="step", out_shape=(big, big),
        in_specs=[HB] * 9 + [SM, SM], out_specs=(VM, VM),
        scratch_shapes=[
            pltpu.VMEM((1, 59, 2, 128), f32), pltpu.VMEM((1, 59, 2, 128), f32), pltpu.VMEM((1, 59, 2, 128), f32), pltpu.VMEM((1, 3, 1, 1024), f32),
            pltpu.SMEM((59,), f32), pltpu.VMEM((16, 16), f32), pltpu.VMEM((1, 1, 2, 64), jnp.int32), pltpu.SMEM((1, 1, 16), jnp.int32), pltpu.SMEM((1, 1, 16), jnp.int32), DMA((9,)),
            pltpu.VMEM((1, 1, 128), jnp.int32), pltpu.VMEM((NT, 1, 128), jnp.int32), pltpu.VMEM((3 * NT, NF * 128), bf16),
            pltpu.VMEM((NT * ROWS, 128), f32), pltpu.VMEM((NT * ROWS, 128), f32), pltpu.VMEM((NT * ROWS, 128), f32), pltpu.VMEM((NT * ROWS, 128), f32),
            pltpu.VMEM((2, 64, 128), f32), pltpu.VMEM((59, 2, 128), f32), pltpu.VMEM((2, 32, 128), f32), pltpu.VMEM((2, 32, 128), f32),
            DMA((2,)), DMA((2,)), DMA((2,)), DMA((2,)), DMA((2,)),
        ] + RENDER_SCRATCH,
        compiler_params=pltpu.CompilerParams(collective_id=0, has_side_effects=True, vmem_limit_bytes=VMEM_LIMIT),
    )(gaussians, consensus, duals, targets, step_sizes, cameras, intersection, block_lists, depth_order, camera_ids, block_counts)
    out = pl.pallas_call(
        deliver_kernel, name="deliver", out_shape=(big, big),
        in_specs=[ANY, ANY], out_specs=(HB, HB), scratch_shapes=[DMA((2,))],
        compiler_params=pltpu.CompilerParams(vmem_limit_bytes=1 << 20),
    )(*out)
    return tuple(a.transpose(0, 2, 1, 3) for a in out)


def solution(mesh):
    t4, t3, t2 = P("scene", "tile", None, None), P("scene", "tile", None), P("scene", "tile")
    return jax.shard_map(
        on_device, mesh=mesh,
        in_specs=(t4, t4, t4, P(), P(), t2, t3, t3, t2, t4, t4),
        out_specs=(t4, t4), check_vma=False,
    )
```

```python
import functools

import jax
import jax.numpy as jnp
from jax import lax
from jax.experimental import pallas as pl
from jax.experimental.pallas import tpu as pltpu
from jax.sharding import PartitionSpec as P

HI = lax.Precision.HIGHEST
f32, bf16 = jnp.float32, jnp.bfloat16
MESH = pl.DeviceIdType.MESH
S = 132
SB = 8 * S
NI = 4
LN2 = 0.6931471805599453

def part2(v):
    a = v.astype(bf16)
    return a, (v - a.astype(f32)).astype(bf16)

def part3(v):
    a = v.astype(bf16).astype(f32)
    r = v - a
    b = r.astype(bf16).astype(f32)
    return a, b, (r - b).astype(bf16).astype(f32)

def render_body(ybase, feats, targ, bias, alpha, wts, gbuf, lhs, csp, tb, cb, bend, grhs, acc, rq, ct):
    sx, sy, fa, fb, fc, lo, k0, k1, k2 = feats
    sxc = sx - 64.0
    syc = sy - (ybase + 3.5)
    lob = lo + bias
    zero32 = jnp.zeros((32, 128), f32)
    pa = part3(fa)
    lhs_a = jnp.concatenate(list(pa) + list(pa) + [zero32], 0).T.astype(bf16)
    for y in range(8):
        dy = (y - 3.5) - syc
        c1 = fb * dy - 2.0 * fa * sxc
        c0 = (fa * sxc - fb * dy) * sxc + fc * dy * dy + lob
        m = jnp.concatenate(list(part3(c0)) + list(part3(c1)) + [zero32], 0)
        lhs[y * 128:(y + 1) * 128, 0:128] = m.T.astype(bf16)
        lhs[y * 128:(y + 1) * 128, 128:256] = lhs_a
    colt = jnp.concatenate([k0, k1, k2, jnp.zeros((80, 128), f32)], 0).T
    kr = lax.broadcasted_iota(jnp.int32, (256, 256), 0)
    ln = lax.broadcasted_iota(jnp.int32, (256, 256), 1)
    xi = ((ln & 127) - 64).astype(f32)
    x2 = xi * xi
    x2h = x2.astype(bf16).astype(f32)
    x2l = x2 - x2h
    basis = jnp.where(kr < 48, 1.0, jnp.where(kr < 96, xi, jnp.where(kr < 128, 0.0, jnp.where(kr < 176, x2h, jnp.where(kr < 224, x2l, 0.0)))))
    grhs[...] = basis
    for p in range(8):
        rhs = jnp.where((kr & 15) == 2 * p + (ln >> 7), grhs[...], 0.0).astype(bf16)
        for y in range(8):
            e = jnp.dot(lhs[y * 128:(y + 1) * 128, :], rhs, preferred_element_type=f32)
            a = jnp.minimum(0.99, jnp.exp2(e))
            alpha[2 * p * SB + y * S:2 * p * SB + y * S + 128, :] = a[:, :128]
            alpha[(2 * p + 1) * SB + y * S:(2 * p + 1) * SB + y * S + 128, :] = a[:, 128:]
    ct[...] = colt
    def colours(q0, at, n):
        part = ct[pl.ds(at, n), :]
        for j in range(NI):
            for c in range(3):
                csp[q0 // NI][c, pl.ds(j * 128 + at, n), :] = jnp.broadcast_to(part[:, c * 16 + q0 + j:c * 16 + q0 + j + 1], (n, 128))
    for q in range(0, 16, NI):
        colours(q, 0, 128)
    one = jnp.ones((8, 128), f32)
    zero = jnp.zeros((8, 128), f32)
    U = 32
    for q0 in range(0, 16, NI):
        def fwd(i, carry):
            st = [list(t) for t in carry]
            for u in range(U):
                g = i * U + u
                for j in range(NI):
                    b = q0 + j
                    a = alpha[pl.ds(b * SB + g, 8, stride=S), :]
                    t, s0, s1, s2 = st[j]
                    w = a * t
                    t = t - w
                    row = j * 128 + g
                    s0 = s0 + w * csp[q0 // NI][0, pl.ds(row, 8, stride=0), :]
                    s1 = s1 + w * csp[q0 // NI][1, pl.ds(row, 8, stride=0), :]
                    s2 = s2 + w * csp[q0 // NI][2, pl.ds(row, 8, stride=0), :]
                    wts[pl.ds(b * SB + g, 8, stride=S), :] = w
                    st[j] = [t, s0, s1, s2]
            return tuple(tuple(t) for t in st)
        out = lax.fori_loop(0, 128 // U, fwd, tuple((one, zero, zero, zero) for _ in range(NI)))
        for j in range(NI):
            tb[q0 + j] = out[j][0]
            for c in range(3):
                cb[c, q0 + j] = out[j][1 + c]
    t = one
    prods = [tb[b] for b in range(16)]
    cs = [zero, zero, zero]
    for b in range(16):
        tb[b] = t
        for c in range(3):
            cs[c] = cs[c] + t * cb[c, b]
        t = t * prods[b]
    r = [cs[c] - targ[c] for c in range(3)]
    e = zero
    for b in range(15, -1, -1):
        bend[b] = e
        e = prods[b] * e + (cb[0, b] * r[0] + cb[1, b] * r[1] + cb[2, b] * r[2])
    for q0 in range(0, 16, NI):
        rs = [[tb[q0 + j] * r[c] for c in range(3)] for j in range(NI)]
        def bwd(i, carry):
            st = list(carry)
            g0 = (128 // U - 1 - i) * U
            for u in range(U - 1, -1, -1):
                g = g0 + u
                for j in range(NI):
                    b = q0 + j
                    a = alpha[pl.ds(b * SB + g, 8, stride=S), :]
                    w = wts[pl.ds(b * SB + g, 8, stride=S), :]
                    row = j * 128 + g
                    q = (rs[j][0] * csp[q0 // NI][0, pl.ds(row, 8, stride=0), :] + rs[j][1] * csp[q0 // NI][1, pl.ds(row, 8, stride=0), :]) + rs[j][2] * csp[q0 // NI][2, pl.ds(row, 8, stride=0), :]
                    d = q - st[j]
                    gbuf[pl.ds(b * SB + g, 8, stride=S), :] = jnp.where(a < 0.99, w * d, 0.0)
                    st[j] = st[j] + a * d
            return tuple(st)
        lax.fori_loop(0, 128 // U, bwd, tuple(tb[q0 + j] * bend[q0 + j] for j in range(NI)))
    mt, phi, xs = acc
    xf = (lax.broadcasted_iota(jnp.int32, (16, 128), 1) - 64).astype(f32)
    kk = lax.broadcasted_iota(jnp.int32, (16, 128), 0)
    xx = xf * xf
    xxh = xx.astype(bf16).astype(f32)
    plans = ({0: 1.0, 1: xf, 2: xxh, 3: xx - xxh}, {4: 1.0, 5: xf}, {6: 1.0}, {7: 1.0}, {8: 1.0}, {9: 1.0})
    for i, plan in enumerate(plans):
        v = jnp.zeros((16, 128), f32)
        for k, w in plan.items():
            v = jnp.where(kk == k, w, v)
        phi[:, i * 256:i * 256 + 128] = v.astype(bf16)
        phi[:, i * 256 + 128:i * 256 + 256] = v.astype(bf16)
    nt = (((1,), (1,)), ((), ()))
    for c in range(3):
        rq[c] = r[c]
    xa, xb = xs
    def fill(b, dst):
        tbb = tb[b]
        base = b * SB if isinstance(b, int) else pl.multiple_of(b * SB, 8)
        rows = []
        for c in range(3):
            v = rq[c] * tbb
            rows.append([v[y:y + 1, :] for y in range(8)])
        for n in range(8):
            at = base + n * 16
            g = [gbuf[pl.ds(at + y * S, 16), :] for y in range(8)]
            sm = [g[4 + k] + g[3 - k] for k in range(4)]
            df = [g[4 + k] - g[3 - k] for k in range(4)]
            out = [(sm[0] + sm[1]) + (sm[2] + sm[3]),
                   (0.5 * df[0] + 1.5 * df[1]) + (2.5 * df[2] + 3.5 * df[3]),
                   (0.25 * sm[0] + 2.25 * sm[1]) + (6.25 * sm[2] + 12.25 * sm[3])]
            w = [wts[pl.ds(at + y * S, 16), :] for y in range(8)]
            for c in range(3):
                t = [w[y] * rows[c][y] for y in range(8)]
                out.append(((t[0] + t[1]) + (t[2] + t[3])) + ((t[4] + t[5]) + (t[6] + t[7])))
            for i in range(6):
                h, l = part2(out[i])
                dst[n * 16:(n + 1) * 16, i * 256:i * 256 + 128] = h
                dst[n * 16:(n + 1) * 16, i * 256 + 128:i * 256 + 256] = l
    def contract(b, src):
        mt[pl.ds(b * 17, 16), :] = lax.dot_general(phi[...], src[...], nt, preferred_element_type=f32)
    fill(0, xa)
    def red(i, _):
        contract(2 * i, xa)
        fill(2 * i + 1, xb)
        contract(2 * i + 1, xb)
        fill(2 * i + 2, xa)
        return 0
    lax.fori_loop(0, 7, red, 0)
    contract(14, xa)
    fill(15, xb)
    contract(15, xb)
    M = [jnp.concatenate([mt[pl.ds(k, 8, stride=17), :], mt[pl.ds(8 * 17 + k, 8, stride=17), :]], 0) for k in range(10)]
    M0 = M[0] * LN2
    Mx = M[1] * LN2
    Mxx = (M[2] + M[3]) * LN2
    My = M[4] * LN2
    Mxy = M[5] * LN2
    Myy = M[6] * LN2
    ux = Mx - sxc * M0
    uy = My - syc * M0
    d_a = Mxx - sxc * (Mx + ux)
    d_b = Mxy - syc * Mx - sxc * uy
    d_c = Myy - syc * (My + uy)
    d_sx = -(2.0 * fa * ux + fb * uy)
    d_sy = -(fb * ux + 2.0 * fc * uy)
    return [d_sx, d_sy, d_a, d_b, d_c, M0, M[7], M[8], M[9]]

RENDER_SCRATCH = [
    pltpu.VMEM((16 * SB, 128), f32), pltpu.VMEM((16 * SB, 128), f32), pltpu.VMEM((16 * SB, 128), f32),
    pltpu.VMEM((1024, 256), bf16), pltpu.VMEM((3, 520, 128), f32), pltpu.VMEM((3, 520, 128), f32), pltpu.VMEM((3, 520, 128), f32), pltpu.VMEM((3, 520, 128), f32),
    pltpu.VMEM((16, 8, 128), f32), pltpu.VMEM((3, 16, 8, 128), f32), pltpu.VMEM((16, 8, 128), f32),
    pltpu.VMEM((256, 256), f32),
    pltpu.VMEM((16 * 17 + 8, 128), f32), pltpu.VMEM((16, 1536), bf16), pltpu.VMEM((128, 1536), bf16), pltpu.VMEM((128, 1536), bf16), pltpu.VMEM((3, 8, 128), f32), pltpu.VMEM((128, 128), f32),
]

LOG2E = 1.4426950408889634
blur_floor = 0.3
penalty_weight = 0.5
sh_zero = 0.28209479177387814
sh_one = 0.4886025119029199
sh_two = (1.0925484305920792, -1.0925484305920792, 0.31539156525252005, -1.0925484305920792, 0.5462742152960396)
sh_three = (-0.5900435899266435, 2.890611442640554, -0.4570457994644658, 0.3731763325901154, -0.4570457994644658, 1.445305721320277, -0.5900435899266435)
NT = 32
NF = 9
VMEM_LIMIT = 40 * 1024 * 1024
ROWS = 24


def features(rows, cam):
    rot = [[cam[3 * i + j] for j in range(3)] for i in range(3)]
    shift = cam[9:12]
    fx, fy, cx, cy = cam[12:16]
    m = rows[0:3]
    e = [rot[i][0] * m[0] + rot[i][1] * m[1] + rot[i][2] * m[2] + shift[i] for i in range(3)]
    inv = 1.0 / e[2]
    px = e[0] * inv
    py = e[1] * inv
    sx = fx * px + cx
    sy = fy * py + cy
    qn = rows[6] * rows[6] + rows[7] * rows[7] + rows[8] * rows[8] + rows[9] * rows[9]
    qi = 1.0 / jnp.sqrt(qn)
    w, x, y, z = [rows[6 + i] * qi for i in range(4)]
    rq = [
        [1.0 - 2.0 * (y * y + z * z), 2.0 * (x * y - w * z), 2.0 * (x * z + w * y)],
        [2.0 * (x * y + w * z), 1.0 - 2.0 * (x * x + z * z), 2.0 * (y * z - w * x)],
        [2.0 * (x * z - w * y), 2.0 * (y * z + w * x), 1.0 - 2.0 * (x * x + y * y)],
    ]
    sc = [jnp.exp(rows[3 + k]) for k in range(3)]
    mm = [[rq[j][k] * sc[k] for k in range(3)] for j in range(3)]
    ww = [[rot[i][0] * mm[0][k] + rot[i][1] * mm[1][k] + rot[i][2] * mm[2][k] for k in range(3)] for i in range(3)]
    ax, ay = fx * inv, fy * inv
    r1 = [ax * (ww[0][k] - px * ww[2][k]) for k in range(3)]
    r2 = [ay * (ww[1][k] - py * ww[2][k]) for k in range(3)]
    cxx = r1[0] * r1[0] + r1[1] * r1[1] + r1[2] * r1[2] + blur_floor
    cxy = r1[0] * r2[0] + r1[1] * r2[1] + r1[2] * r2[2]
    cyy = r2[0] * r2[0] + r2[1] * r2[1] + r2[2] * r2[2] + blur_floor
    idet = 1.0 / (cxx * cyy - cxy * cxy)
    fa = (-0.5 * LOG2E) * (cyy * idet)
    fb = LOG2E * (cxy * idet)
    fc = (-0.5 * LOG2E) * (cxx * idet)
    lo = (-LOG2E) * jnp.log(1.0 + jnp.exp(-rows[10]))
    eye = [-(rot[0][i] * shift[0] + rot[1][i] * shift[1] + rot[2][i] * shift[2]) for i in range(3)]
    tw = [m[i] - eye[i] for i in range(3)]
    ti = 1.0 / jnp.sqrt(tw[0] * tw[0] + tw[1] * tw[1] + tw[2] * tw[2])
    dx, dy, dz = [t * ti for t in tw]
    xx, yy, zz = dx * dx, dy * dy, dz * dz
    basis = [
        -sh_one * dy, sh_one * dz, -sh_one * dx,
        sh_two[0] * dx * dy, sh_two[1] * dy * dz, sh_two[2] * (2.0 * zz - xx - yy), sh_two[3] * dx * dz, sh_two[4] * (xx - yy),
        sh_three[0] * dy * (3.0 * xx - yy), sh_three[1] * dx * dy * dz, sh_three[2] * dy * (4.0 * zz - xx - yy),
        sh_three[3] * dz * (2.0 * zz - 3.0 * xx - 3.0 * yy), sh_three[4] * dx * (4.0 * zz - xx - yy),
        sh_three[5] * dz * (xx - yy), sh_three[6] * dx * (xx - 3.0 * yy),
    ]
    cols = []
    for c in range(3):
        acc = sh_zero * rows[11 + c] + 0.5
        for k in range(15):
            acc = acc + basis[k] * rows[14 + 3 * k + c]
        cols.append(acc)
    shape = sx.shape
    return [sx, sy, fa, fb, fc, jnp.broadcast_to(lo, shape)] + cols


def camera_columns(cam_ref):
    return [cam_ref[:, j:j + 1] for j in range(16)]


def slot_map(ids_ref, order_ref, count_ref):
    rowi = lax.broadcasted_iota(jnp.int32, (16, 128), 0)
    lane = lax.broadcasted_iota(jnp.int32, (16, 128), 1)
    owner = jnp.full((16, 128), -1, jnp.int32)
    across = jnp.full((16, 128), -1, jnp.int32)
    for k in range(16):
        o = order_ref[0, 0, k]
        own = jnp.where(o < count_ref[0, 0], ids_ref[0, 0, o] >> 1, -1)
        owner = jnp.where(rowi == k, own, owner)
        across = jnp.where(lane == k, own, across)
    one = (owner == lane).astype(f32)[:, :NT]
    back = (jnp.broadcast_to(across[0:1, :16], (NT, 16)) == lax.broadcasted_iota(jnp.int32, (NT, 16), 0)).astype(f32)
    return one, back, jnp.where(owner[:, 0:1] < 0, -1e4, 0.0)


def slab(ref, t):
    return ref.at[pl.ds(pl.multiple_of(t * ROWS, ROWS), NF)]


STEPS = sorted([(z, y, x) for z in range(2) for y in range(4) for x in range(4)][1:], key=lambda s: -(s[0] + min(s[1], 4 - s[1]) + min(s[2], 4 - s[2])))


def others(me):
    zs = [16 * lax.rem(lax.div(me, 16) + d, 2) for d in range(2)]
    ys = [4 * lax.rem(lax.div(me, 4) + d, 4) for d in range(4)]
    xs = [lax.rem(me + d, 4) for d in range(4)]
    return [zs[z] + ys[y] + xs[x] for z, y, x in STEPS]


def lines(me):
    zs = [16 * lax.rem(lax.div(me, 16) + d, 2) for d in range(2)]
    ys = [4 * lax.rem(lax.div(me, 4) + d, 4) for d in range(4)]
    xs = [lax.rem(me + d, 4) for d in range(4)]
    along = [zs[0] + ys[0] + xs[d] for d in (2, 1, 3)]
    across = [zs[z] + ys[y] + xs[0] for z, y in ((1, 2), (1, 1), (1, 3), (0, 2), (0, 1), (0, 3), (1, 0))]
    return along, across, zs[0] + ys[0]


def exchange(me, peers, send, recv, sems):
    for t in peers:
        pltpu.make_async_remote_copy(slab(send, t), slab(recv, me), sems.at[0], sems.at[1], device_id={"tile": t}, device_id_type=MESH).start()


def passed(buf, sem, rows=(NT - 1) * NF):
    whole = buf.at[pl.ds(0, rows)]
    pltpu.make_async_copy(whole, whole, sem).wait()


def stack3(x):
    return jnp.concatenate(part3(x), 0).astype(bf16)


def thrice(onehot):
    return jnp.concatenate([onehot] * 3, 1).astype(bf16)


def gather_rows(recv):
    return jnp.concatenate([jnp.concatenate([recv[pl.ds(t * ROWS + f, 8, stride=ROWS), :] for t in range(0, NT, 8)], 0) for f in range(NF)], 1)


def place_rows(x, send):
    for f in range(NF):
        for t in range(0, NT, 8):
            send[pl.ds(t * ROWS + f, 8, stride=ROWS), :] = x[t:t + 8, f * 128:(f + 1) * 128]


def own_rows(me, send, recv):
    at = pl.ds(pl.multiple_of(me * ROWS, ROWS), ROWS)
    recv[at, :] = send[at, :]


def step_kernel(gauss_hbm, cons_hbm, dual_hbm, targ_hbm, step_hbm, cam_hbm, inter_hbm, ids_hbm, order_hbm, cid_ref, count_ref, upd_ref, newd_ref,
                gauss_ref, cons_ref, dual_ref, t_ref, step_ref, cam_ref, inter_ref, ids_ref, order_ref, local_sem,
                req, reqs, fbuf, send, recv, gsend, grecv, grad, base, vals, near, e0, e1, e2, e3, s4, r4,
                alpha, wts, gbuf, lhs, k0, k1, k2, k3, tb, cb, bend, grhs, a0, a1, a2, a3, rq, ct):
    me = lax.axis_index("tile")
    grp = lax.axis_index("scene")
    last = lax.axis_size("scene") - 1
    loads = [pltpu.make_async_copy(x, y, local_sem.at[i]) for i, (x, y) in enumerate((
        (ids_hbm, ids_ref), (order_hbm, order_ref), (cam_hbm, cam_ref), (gauss_hbm, gauss_ref),
        (cons_hbm, cons_ref), (dual_hbm, dual_ref), (targ_hbm, t_ref), (step_hbm, step_ref), (inter_hbm, inter_ref)))]
    for l in loads:
        l.start()
    near[...] = jnp.zeros_like(near)
    barrier = pltpu.get_barrier_semaphore()

    peers = others(me)
    along, across, line = lines(me)
    for t in across + along:
        pl.semaphore_signal(barrier, inc=1, device_id={"tile": t}, device_id_type=MESH)

    @pl.when(grp < last)
    def _():
        pl.semaphore_signal(barrier, inc=1, device_id={"scene": grp + 1}, device_id_type=MESH)

    @pl.when(grp > 0)
    def _():
        pl.semaphore_signal(barrier, inc=1, device_id={"scene": grp - 1}, device_id_type=MESH)
    loads[0].wait()
    lane = lax.broadcasted_iota(jnp.int32, (1, 128), 1)
    ask = jnp.full((1, 128), cid_ref[0, 0], jnp.int32)
    for k in range(16):
        b = ids_ref[0, 0, k]
        ask = ask + jnp.where(lane == (b >> 1), (b & 1) * 16, 0)
    req[0] = ask
    reqs[me] = ask
    loads[2].wait()
    loads[3].wait()
    cam = camera_columns(cam_ref)
    outs = [features([gauss_ref[0, i, b:b + 1, :] for i in range(59)], cam) for b in range(2)]
    fbuf[...] = stack3(jnp.concatenate([jnp.concatenate(o, 1) for o in outs], 0))
    pl.semaphore_wait(barrier, 10 + jnp.where(grp < last, 1, 0) + jnp.where(grp > 0, 1, 0))
    for t in along:
        pltpu.make_async_remote_copy(req.at[0], reqs.at[me], e0.at[0], e0.at[1], device_id={"tile": t}, device_id_type=MESH).start()
    passed(reqs, e0.at[1], 3)
    four = reqs.at[pl.ds(line, 4)]
    for t in across:
        pltpu.make_async_remote_copy(four, four, e1.at[0], e1.at[1], device_id={"tile": t}, device_id_type=MESH).start()
    loads[1].wait()
    one, back, bias = slot_map(ids_ref, order_ref, count_ref)
    for l in loads[4:]:
        l.wait()
    passed(reqs, e1.at[1], 28)
    asked = jnp.concatenate([reqs[t] for t in range(NT)], 0)
    lane32 = lax.broadcasted_iota(jnp.int32, (NT, 128), 1)
    col = jnp.sum(jnp.where(lane32 == me, asked, 0).astype(f32), 1, keepdims=True).astype(jnp.int32)
    sel = (col == lax.broadcasted_iota(jnp.int32, (NT, NT), 1)).astype(f32)
    place_rows(jnp.dot(thrice(sel), fbuf[...], preferred_element_type=f32), send)
    own_rows(me, send, recv)
    exchange(me, peers, send, recv, e2)
    one3 = thrice(one)
    passed(recv, e2.at[1])
    y = jnp.dot(one3, stack3(gather_rows(recv)), preferred_element_type=f32)
    targ = [jnp.concatenate([t_ref[0, c, 0:1, y0 * 128:(y0 + 1) * 128] for y0 in range(8)], 0) for c in range(3)]
    ybase = (8 * lax.rem(me, 4)).astype(f32)
    outs = render_body(ybase, [y[:, f * 128:(f + 1) * 128] for f in range(NF)], targ, bias, alpha, wts, gbuf, lhs, (k0, k1, k2, k3), tb, cb, bend, grhs, (a0, a1, (a2, a3)), rq, ct)
    place_rows(jnp.dot(thrice(back), stack3(jnp.concatenate(outs, 1)), preferred_element_type=f32), gsend)
    own_rows(me, gsend, grecv)
    exchange(me, peers, gsend, grecv, e3)
    turned = jnp.concatenate([jnp.broadcast_to(col, (NT, 128)).astype(f32), jnp.zeros((96, 128), f32)], 0).T
    selt = thrice((turned[:NT, :NT].astype(jnp.int32) == lax.broadcasted_iota(jnp.int32, (NT, NT), 0)).astype(f32))
    idx = jnp.concatenate([inter_ref[0, 0, 0:1, :], inter_ref[0, 0, 1:2, :]], 1)
    picks = [(lax.broadcasted_iota(jnp.int32, (128, 128), 0) + b * 128 == idx).astype(f32) for b in range(2)]
    pulls = []
    for b in range(2):
        rows = [gauss_ref[0, i, b:b + 1, :] for i in range(59)]
        pulls.append(jax.vjp(lambda r: features(r, cam), rows)[1])
    for i in range(59):
        base[i] = gauss_ref[0, i] - (penalty_weight * step_ref[i]) * (gauss_ref[0, i] - cons_ref[0, i] + dual_ref[0, i])
    passed(grecv, e3.at[1])
    df = jnp.dot(selt, stack3(gather_rows(grecv)), preferred_element_type=f32)
    for b in range(2):
        (grows,) = pulls[b]([df[b * 16:(b + 1) * 16, f * 128:(f + 1) * 128] for f in range(NF)])
        for i in range(59):
            u = base[i, b:b + 1, :] - step_ref[i] * grows[i]
            upd_ref[0, i, b:b + 1, :] = u
            grad[b, i:i + 1, :] = u + dual_ref[0, i, b:b + 1, :]
    grad[:, 59:64, :] = jnp.zeros((2, 5, 128), f32)
    picks3 = [jnp.concatenate([p] * 3, 0).astype(bf16) for p in picks]
    v = sum(jnp.dot(jnp.concatenate(part3(grad[b]), 1).astype(bf16), picks3[b], preferred_element_type=f32) for b in range(2))
    lane = lax.broadcasted_iota(jnp.int32, (32, 128), 1)
    low, high = v[:32], v[32:]
    vals[0] = jnp.where(lane < 64, low, pltpu.roll(high, 64, 1))
    vals[1] = jnp.where(lane < 64, pltpu.roll(low, 64, 1), high)

    def up():
        return pltpu.make_async_remote_copy(vals.at[0], near.at[0], s4.at[0], r4.at[0], device_id={"scene": lax.rem(grp + 1, last + 1)}, device_id_type=MESH)

    def down():
        return pltpu.make_async_remote_copy(vals.at[1], near.at[1], s4.at[1], r4.at[1], device_id={"scene": lax.rem(grp + last, last + 1)}, device_id_type=MESH)

    @pl.when(grp < last)
    def _():
        up().start()

    @pl.when(grp > 0)
    def _():
        down().start()

    @pl.when(grp > 0)
    def _():
        up().wait_recv()
        down().wait_send()

    @pl.when(grp < last)
    def _():
        down().wait_recv()
        up().wait_send()
    from_above = jnp.where(grp < last, 0.5 * (vals[0] - near[1]), 0.0)
    from_below = jnp.where(grp > 0, 0.5 * (vals[1] - near[0]), 0.0)
    diff = jnp.concatenate([
        jnp.where(lane < 64, from_above, pltpu.roll(from_below, 64, 1)),
        jnp.where(lane < 64, pltpu.roll(from_above, 64, 1), from_below),
    ], 0)
    diff3 = jnp.concatenate(part3(diff), 1).astype(bf16)
    for b in range(2):
        p3 = jnp.concatenate([picks[b]] * 3, 1).astype(bf16)
        nd = lax.dot_general(diff3, p3, (((1,), (1,)), ((), ())), preferred_element_type=f32)
        for i in range(59):
            newd_ref[0, i, b:b + 1, :] = nd[i:i + 1, :]
    passed(reqs, e0.at[0], 3)
    passed(reqs, e1.at[0], 28)
    passed(send, e2.at[0])
    passed(gsend, e3.at[0])


def deliver_kernel(a_ref, b_ref, a_out, b_out, sem):
    moves = [pltpu.make_async_copy(a_ref, a_out, sem.at[0]), pltpu.make_async_copy(b_ref, b_out, sem.at[1])]
    for m in moves:
        m.start()
    for m in moves:
        m.wait()


ANY = pl.BlockSpec(memory_space=pl.ANY)
VM = pl.BlockSpec(memory_space=pltpu.VMEM)
SM = pl.BlockSpec(memory_space=pltpu.SMEM)
HB = pl.BlockSpec(memory_space=pltpu.HBM)
DMA = pltpu.SemaphoreType.DMA


def on_device(gaussians, consensus, duals, step_sizes, cameras, camera_ids, block_lists, depth_order, block_counts, targets, intersection):
    def sd(shape, t=f32):
        return jax.ShapeDtypeStruct(shape, t)
    gaussians, consensus, duals, targets = [a.transpose(0, 2, 1, 3) for a in (gaussians, consensus, duals, targets)]
    big = sd((1, 59, 2, 128))
    gaussians, consensus, duals, targets, cameras, intersection, step_sizes, block_lists, depth_order = [
        pltpu.with_memory_space_constraint(a, pltpu.HBM)
        for a in (gaussians, consensus, duals, targets, cameras, intersection, step_sizes, block_lists, depth_order)
    ]
    out = pl.pallas_call(
        step_kernel, name="step", out_shape=(big, big),
        in_specs=[HB] * 9 + [SM, SM], out_specs=(VM, VM),
        scratch_shapes=[
            pltpu.VMEM((1, 59, 2, 128), f32), pltpu.VMEM((1, 59, 2, 128), f32), pltpu.VMEM((1, 59, 2, 128), f32), pltpu.VMEM((1, 3, 1, 1024), f32),
            pltpu.SMEM((59,), f32), pltpu.VMEM((16, 16), f32), pltpu.VMEM((1, 1, 2, 64), jnp.int32), pltpu.SMEM((1, 1, 16), jnp.int32), pltpu.SMEM((1, 1, 16), jnp.int32), DMA((9,)),
            pltpu.VMEM((1, 1, 128), jnp.int32), pltpu.VMEM((NT, 1, 128), jnp.int32), pltpu.VMEM((3 * NT, NF * 128), bf16),
            pltpu.VMEM((NT * ROWS, 128), f32), pltpu.VMEM((NT * ROWS, 128), f32), pltpu.VMEM((NT * ROWS, 128), f32), pltpu.VMEM((NT * ROWS, 128), f32),
            pltpu.VMEM((2, 64, 128), f32), pltpu.VMEM((59, 2, 128), f32), pltpu.VMEM((2, 32, 128), f32), pltpu.VMEM((2, 32, 128), f32),
            DMA((2,)), DMA((2,)), DMA((2,)), DMA((2,)), DMA((2,)), DMA((2,)),
        ] + RENDER_SCRATCH,
        compiler_params=pltpu.CompilerParams(collective_id=0, has_side_effects=True, vmem_limit_bytes=VMEM_LIMIT),
    )(gaussians, consensus, duals, targets, step_sizes, cameras, intersection, block_lists, depth_order, camera_ids, block_counts)
    out = pl.pallas_call(
        deliver_kernel, name="deliver", out_shape=(big, big),
        in_specs=[ANY, ANY], out_specs=(HB, HB), scratch_shapes=[DMA((2,))],
        compiler_params=pltpu.CompilerParams(vmem_limit_bytes=1 << 20),
    )(*out)
    return tuple(a.transpose(0, 2, 1, 3) for a in out)


def solution(mesh):
    t4, t3, t2 = P("scene", "tile", None, None), P("scene", "tile", None), P("scene", "tile")
    return jax.shard_map(
        on_device, mesh=mesh,
        in_specs=(t4, t4, t4, P(), P(), t2, t3, t3, t2, t4, t4),
        out_specs=(t4, t4), check_vma=False,
    )
```

```python
import functools

import jax
import jax.numpy as jnp
from jax import lax
from jax.experimental import pallas as pl
from jax.experimental.pallas import tpu as pltpu
from jax.sharding import PartitionSpec as P

HI = lax.Precision.HIGHEST
f32, bf16 = jnp.float32, jnp.bfloat16
MESH = pl.DeviceIdType.MESH
S = 132
SB = 8 * S
NI = 4
LN2 = 0.6931471805599453

def part2(v):
    a = v.astype(bf16)
    return a, (v - a.astype(f32)).astype(bf16)

def part3(v):
    a = v.astype(bf16).astype(f32)
    r = v - a
    b = r.astype(bf16).astype(f32)
    return a, b, (r - b).astype(bf16).astype(f32)

def render_body(ybase, feats, targ, bias, alpha, wts, gbuf, lhs, csp, tb, cb, bend, grhs, acc, rq, ct):
    sx, sy, fa, fb, fc, lo, k0, k1, k2 = feats
    sxc = sx - 64.0
    syc = sy - (ybase + 3.5)
    lob = lo + bias
    zero32 = jnp.zeros((32, 128), f32)
    pa = part3(fa)
    lhs_a = jnp.concatenate(list(pa) + list(pa) + [zero32], 0).T.astype(bf16)
    for y in range(8):
        dy = (y - 3.5) - syc
        c1 = fb * dy - 2.0 * fa * sxc
        c0 = (fa * sxc - fb * dy) * sxc + fc * dy * dy + lob
        m = jnp.concatenate(list(part3(c0)) + list(part3(c1)) + [zero32], 0)
        lhs[y * 128:(y + 1) * 128, 0:128] = m.T.astype(bf16)
        lhs[y * 128:(y + 1) * 128, 128:256] = lhs_a
    colt = jnp.concatenate([k0, k1, k2, jnp.zeros((80, 128), f32)], 0).T
    kr = lax.broadcasted_iota(jnp.int32, (256, 256), 0)
    ln = lax.broadcasted_iota(jnp.int32, (256, 256), 1)
    xi = ((ln & 127) - 64).astype(f32)
    x2 = xi * xi
    x2h = x2.astype(bf16).astype(f32)
    x2l = x2 - x2h
    basis = jnp.where(kr < 48, 1.0, jnp.where(kr < 96, xi, jnp.where(kr < 128, 0.0, jnp.where(kr < 176, x2h, jnp.where(kr < 224, x2l, 0.0)))))
    grhs[...] = basis
    for p in range(8):
        rhs = jnp.where((kr & 15) == 2 * p + (ln >> 7), grhs[...], 0.0).astype(bf16)
        for y in range(8):
            e = jnp.dot(lhs[y * 128:(y + 1) * 128, :], rhs, preferred_element_type=f32)
            a = jnp.minimum(0.99, jnp.exp2(e))
            alpha[2 * p * SB + y * S:2 * p * SB + y * S + 128, :] = a[:, :128]
            alpha[(2 * p + 1) * SB + y * S:(2 * p + 1) * SB + y * S + 128, :] = a[:, 128:]
    ct[...] = colt
    def colours(q0, at, n):
        part = ct[pl.ds(at, n), :]
        for j in range(NI):
            for c in range(3):
                csp[q0 // NI][c, pl.ds(j * 128 + at, n), :] = jnp.broadcast_to(part[:, c * 16 + q0 + j:c * 16 + q0 + j + 1], (n, 128))
    for q in range(0, 16, NI):
        colours(q, 0, 128)
    one = jnp.ones((8, 128), f32)
    zero = jnp.zeros((8, 128), f32)
    U = 32
    for q0 in range(0, 16, NI):
        def fwd(i, carry):
            st = [list(t) for t in carry]
            for u in range(U):
                g = i * U + u
                for j in range(NI):
                    b = q0 + j
                    a = alpha[pl.ds(b * SB + g, 8, stride=S), :]
                    t, s0, s1, s2 = st[j]
                    w = a * t
                    t = t - w
                    row = j * 128 + g
                    s0 = s0 + w * csp[q0 // NI][0, pl.ds(row, 8, stride=0), :]
                    s1 = s1 + w * csp[q0 // NI][1, pl.ds(row, 8, stride=0), :]
                    s2 = s2 + w * csp[q0 // NI][2, pl.ds(row, 8, stride=0), :]
                    wts[pl.ds(b * SB + g, 8, stride=S), :] = w
                    st[j] = [t, s0, s1, s2]
            return tuple(tuple(t) for t in st)
        out = lax.fori_loop(0, 128 // U, fwd, tuple((one, zero, zero, zero) for _ in range(NI)))
        for j in range(NI):
            tb[q0 + j] = out[j][0]
            for c in range(3):
                cb[c, q0 + j] = out[j][1 + c]
    t = one
    prods = [tb[b] for b in range(16)]
    cs = [zero, zero, zero]
    for b in range(16):
        tb[b] = t
        for c in range(3):
            cs[c] = cs[c] + t * cb[c, b]
        t = t * prods[b]
    r = [cs[c] - targ[c] for c in range(3)]
    e = zero
    for b in range(15, -1, -1):
        bend[b] = e
        e = prods[b] * e + (cb[0, b] * r[0] + cb[1, b] * r[1] + cb[2, b] * r[2])
    for q0 in range(0, 16, NI):
        rs = [[tb[q0 + j] * r[c] for c in range(3)] for j in range(NI)]
        def bwd(i, carry):
            st = list(carry)
            g0 = (128 // U - 1 - i) * U
            for u in range(U - 1, -1, -1):
                g = g0 + u
                for j in range(NI):
                    b = q0 + j
                    a = alpha[pl.ds(b * SB + g, 8, stride=S), :]
                    w = wts[pl.ds(b * SB + g, 8, stride=S), :]
                    row = j * 128 + g
                    q = (rs[j][0] * csp[q0 // NI][0, pl.ds(row, 8, stride=0), :] + rs[j][1] * csp[q0 // NI][1, pl.ds(row, 8, stride=0), :]) + rs[j][2] * csp[q0 // NI][2, pl.ds(row, 8, stride=0), :]
                    d = q - st[j]
                    gbuf[pl.ds(b * SB + g, 8, stride=S), :] = jnp.where(a < 0.99, w * d, 0.0)
                    st[j] = st[j] + a * d
            return tuple(st)
        lax.fori_loop(0, 128 // U, bwd, tuple(tb[q0 + j] * bend[q0 + j] for j in range(NI)))
    mt, phi, xs = acc
    xf = (lax.broadcasted_iota(jnp.int32, (16, 128), 1) - 64).astype(f32)
    kk = lax.broadcasted_iota(jnp.int32, (16, 128), 0)
    xx = xf * xf
    xxh = xx.astype(bf16).astype(f32)
    plans = ({0: 1.0, 1: xf, 2: xxh, 3: xx - xxh}, {4: 1.0, 5: xf}, {6: 1.0}, {7: 1.0}, {8: 1.0}, {9: 1.0})
    for i, plan in enumerate(plans):
        v = jnp.zeros((16, 128), f32)
        for k, w in plan.items():
            v = jnp.where(kk == k, w, v)
        phi[:, i * 256:i * 256 + 128] = v.astype(bf16)
        phi[:, i * 256 + 128:i * 256 + 256] = v.astype(bf16)
    nt = (((1,), (1,)), ((), ()))
    for c in range(3):
        rq[c] = r[c]
    xa, xb = xs
    def fill(b, dst):
        tbb = tb[b]
        base = b * SB if isinstance(b, int) else pl.multiple_of(b * SB, 8)
        rows = []
        for c in range(3):
            v = rq[c] * tbb
            rows.append([v[y:y + 1, :] for y in range(8)])
        for n in range(8):
            at = base + n * 16
            g = [gbuf[pl.ds(at + y * S, 16), :] for y in range(8)]
            sm = [g[4 + k] + g[3 - k] for k in range(4)]
            df = [g[4 + k] - g[3 - k] for k in range(4)]
            out = [(sm[0] + sm[1]) + (sm[2] + sm[3]),
                   (0.5 * df[0] + 1.5 * df[1]) + (2.5 * df[2] + 3.5 * df[3]),
                   (0.25 * sm[0] + 2.25 * sm[1]) + (6.25 * sm[2] + 12.25 * sm[3])]
            w = [wts[pl.ds(at + y * S, 16), :] for y in range(8)]
            for c in range(3):
                t = [w[y] * rows[c][y] for y in range(8)]
                out.append(((t[0] + t[1]) + (t[2] + t[3])) + ((t[4] + t[5]) + (t[6] + t[7])))
            for i in range(6):
                h, l = part2(out[i])
                dst[n * 16:(n + 1) * 16, i * 256:i * 256 + 128] = h
                dst[n * 16:(n + 1) * 16, i * 256 + 128:i * 256 + 256] = l
    def contract(b, src):
        mt[pl.ds(b * 17, 16), :] = lax.dot_general(phi[...], src[...], nt, preferred_element_type=f32)
    fill(0, xa)
    def red(i, _):
        contract(2 * i, xa)
        fill(2 * i + 1, xb)
        contract(2 * i + 1, xb)
        fill(2 * i + 2, xa)
        return 0
    lax.fori_loop(0, 7, red, 0)
    contract(14, xa)
    fill(15, xb)
    contract(15, xb)
    M = [jnp.concatenate([mt[pl.ds(k, 8, stride=17), :], mt[pl.ds(8 * 17 + k, 8, stride=17), :]], 0) for k in range(10)]
    M0 = M[0] * LN2
    Mx = M[1] * LN2
    Mxx = (M[2] + M[3]) * LN2
    My = M[4] * LN2
    Mxy = M[5] * LN2
    Myy = M[6] * LN2
    ux = Mx - sxc * M0
    uy = My - syc * M0
    d_a = Mxx - sxc * (Mx + ux)
    d_b = Mxy - syc * Mx - sxc * uy
    d_c = Myy - syc * (My + uy)
    d_sx = -(2.0 * fa * ux + fb * uy)
    d_sy = -(fb * ux + 2.0 * fc * uy)
    return [d_sx, d_sy, d_a, d_b, d_c, M0, M[7], M[8], M[9]]

RENDER_SCRATCH = [
    pltpu.VMEM((16 * SB, 128), f32), pltpu.VMEM((16 * SB, 128), f32), pltpu.VMEM((16 * SB, 128), f32),
    pltpu.VMEM((1024, 256), bf16), pltpu.VMEM((3, 520, 128), f32), pltpu.VMEM((3, 520, 128), f32), pltpu.VMEM((3, 520, 128), f32), pltpu.VMEM((3, 520, 128), f32),
    pltpu.VMEM((16, 8, 128), f32), pltpu.VMEM((3, 16, 8, 128), f32), pltpu.VMEM((16, 8, 128), f32),
    pltpu.VMEM((256, 256), f32),
    pltpu.VMEM((16 * 17 + 8, 128), f32), pltpu.VMEM((16, 1536), bf16), pltpu.VMEM((128, 1536), bf16), pltpu.VMEM((128, 1536), bf16), pltpu.VMEM((3, 8, 128), f32), pltpu.VMEM((128, 128), f32),
]

LOG2E = 1.4426950408889634
blur_floor = 0.3
penalty_weight = 0.5
sh_zero = 0.28209479177387814
sh_one = 0.4886025119029199
sh_two = (1.0925484305920792, -1.0925484305920792, 0.31539156525252005, -1.0925484305920792, 0.5462742152960396)
sh_three = (-0.5900435899266435, 2.890611442640554, -0.4570457994644658, 0.3731763325901154, -0.4570457994644658, 1.445305721320277, -0.5900435899266435)
NT = 32
NF = 9
VMEM_LIMIT = 40 * 1024 * 1024
ROWS = 24


def features(rows, cam):
    rot = [[cam[3 * i + j] for j in range(3)] for i in range(3)]
    shift = cam[9:12]
    fx, fy, cx, cy = cam[12:16]
    m = rows[0:3]
    e = [rot[i][0] * m[0] + rot[i][1] * m[1] + rot[i][2] * m[2] + shift[i] for i in range(3)]
    inv = 1.0 / e[2]
    px = e[0] * inv
    py = e[1] * inv
    sx = fx * px + cx
    sy = fy * py + cy
    qn = rows[6] * rows[6] + rows[7] * rows[7] + rows[8] * rows[8] + rows[9] * rows[9]
    qi = 1.0 / jnp.sqrt(qn)
    w, x, y, z = [rows[6 + i] * qi for i in range(4)]
    rq = [
        [1.0 - 2.0 * (y * y + z * z), 2.0 * (x * y - w * z), 2.0 * (x * z + w * y)],
        [2.0 * (x * y + w * z), 1.0 - 2.0 * (x * x + z * z), 2.0 * (y * z - w * x)],
        [2.0 * (x * z - w * y), 2.0 * (y * z + w * x), 1.0 - 2.0 * (x * x + y * y)],
    ]
    sc = [jnp.exp(rows[3 + k]) for k in range(3)]
    mm = [[rq[j][k] * sc[k] for k in range(3)] for j in range(3)]
    ww = [[rot[i][0] * mm[0][k] + rot[i][1] * mm[1][k] + rot[i][2] * mm[2][k] for k in range(3)] for i in range(3)]
    ax, ay = fx * inv, fy * inv
    r1 = [ax * (ww[0][k] - px * ww[2][k]) for k in range(3)]
    r2 = [ay * (ww[1][k] - py * ww[2][k]) for k in range(3)]
    cxx = r1[0] * r1[0] + r1[1] * r1[1] + r1[2] * r1[2] + blur_floor
    cxy = r1[0] * r2[0] + r1[1] * r2[1] + r1[2] * r2[2]
    cyy = r2[0] * r2[0] + r2[1] * r2[1] + r2[2] * r2[2] + blur_floor
    idet = 1.0 / (cxx * cyy - cxy * cxy)
    fa = (-0.5 * LOG2E) * (cyy * idet)
    fb = LOG2E * (cxy * idet)
    fc = (-0.5 * LOG2E) * (cxx * idet)
    lo = (-LOG2E) * jnp.log(1.0 + jnp.exp(-rows[10]))
    eye = [-(rot[0][i] * shift[0] + rot[1][i] * shift[1] + rot[2][i] * shift[2]) for i in range(3)]
    tw = [m[i] - eye[i] for i in range(3)]
    ti = 1.0 / jnp.sqrt(tw[0] * tw[0] + tw[1] * tw[1] + tw[2] * tw[2])
    dx, dy, dz = [t * ti for t in tw]
    xx, yy, zz = dx * dx, dy * dy, dz * dz
    basis = [
        -sh_one * dy, sh_one * dz, -sh_one * dx,
        sh_two[0] * dx * dy, sh_two[1] * dy * dz, sh_two[2] * (2.0 * zz - xx - yy), sh_two[3] * dx * dz, sh_two[4] * (xx - yy),
        sh_three[0] * dy * (3.0 * xx - yy), sh_three[1] * dx * dy * dz, sh_three[2] * dy * (4.0 * zz - xx - yy),
        sh_three[3] * dz * (2.0 * zz - 3.0 * xx - 3.0 * yy), sh_three[4] * dx * (4.0 * zz - xx - yy),
        sh_three[5] * dz * (xx - yy), sh_three[6] * dx * (xx - 3.0 * yy),
    ]
    cols = []
    for c in range(3):
        acc = sh_zero * rows[11 + c] + 0.5
        for k in range(15):
            acc = acc + basis[k] * rows[14 + 3 * k + c]
        cols.append(acc)
    shape = sx.shape
    return [sx, sy, fa, fb, fc, jnp.broadcast_to(lo, shape)] + cols


def camera_columns(cam_ref):
    return [cam_ref[:, j:j + 1] for j in range(16)]


def slot_map(ids_ref, order_ref, count_ref):
    rowi = lax.broadcasted_iota(jnp.int32, (16, 128), 0)
    lane = lax.broadcasted_iota(jnp.int32, (16, 128), 1)
    owner = jnp.full((16, 128), -1, jnp.int32)
    across = jnp.full((16, 128), -1, jnp.int32)
    for k in range(16):
        o = order_ref[0, 0, k]
        own = jnp.where(o < count_ref[0, 0], ids_ref[0, 0, o] >> 1, -1)
        owner = jnp.where(rowi == k, own, owner)
        across = jnp.where(lane == k, own, across)
    one = (owner == lane).astype(f32)[:, :NT]
    back = (jnp.broadcast_to(across[0:1, :16], (NT, 16)) == lax.broadcasted_iota(jnp.int32, (NT, 16), 0)).astype(f32)
    return one, back, jnp.where(owner[:, 0:1] < 0, -1e4, 0.0)


def slab(ref, t):
    return ref.at[pl.ds(pl.multiple_of(t * ROWS, ROWS), NF)]


STEPS = sorted([(z, y, x) for z in range(2) for y in range(4) for x in range(4)][1:], key=lambda s: -(s[0] + min(s[1], 4 - s[1]) + min(s[2], 4 - s[2])))


def others(me):
    zs = [16 * lax.rem(lax.div(me, 16) + d, 2) for d in range(2)]
    ys = [4 * lax.rem(lax.div(me, 4) + d, 4) for d in range(4)]
    xs = [lax.rem(me + d, 4) for d in range(4)]
    return [zs[z] + ys[y] + xs[x] for z, y, x in STEPS]


def exchange(me, peers, send, recv, sems, wide=True):
    for t in peers:
        src, dst = (slab(send, t), slab(recv, me)) if wide else (send.at[0], recv.at[me])
        pltpu.make_async_remote_copy(src, dst, sems.at[0], sems.at[1], device_id={"tile": t}, device_id_type=MESH).start()


def passed(buf, sem, wide=True):
    whole = buf.at[pl.ds(0, (NT - 1) * (NF if wide else 1))]
    pltpu.make_async_copy(whole, whole, sem).wait()


def stack3(x):
    return jnp.concatenate(part3(x), 0).astype(bf16)


def thrice(onehot):
    return jnp.concatenate([onehot] * 3, 1).astype(bf16)


def gather_rows(recv):
    return jnp.concatenate([jnp.concatenate([recv[pl.ds(t * ROWS + f, 8, stride=ROWS), :] for t in range(0, NT, 8)], 0) for f in range(NF)], 1)


def place_rows(x, send):
    for f in range(NF):
        for t in range(0, NT, 8):
            send[pl.ds(t * ROWS + f, 8, stride=ROWS), :] = x[t:t + 8, f * 128:(f + 1) * 128]


def own_rows(me, send, recv):
    at = pl.ds(pl.multiple_of(me * ROWS, ROWS), ROWS)
    recv[at, :] = send[at, :]


def step_kernel(gauss_hbm, cons_hbm, dual_hbm, targ_hbm, step_hbm, cam_hbm, inter_hbm, ids_hbm, order_hbm, cid_ref, count_ref, upd_ref, newd_ref,
                gauss_ref, cons_ref, dual_ref, t_ref, step_ref, cam_ref, inter_ref, ids_ref, order_ref, local_sem,
                req, reqs, fbuf, send, recv, gsend, grecv, grad, base, vals, near, e1, e2, e3, s4, r4,
                alpha, wts, gbuf, lhs, k0, k1, k2, k3, tb, cb, bend, grhs, a0, a1, a2, a3, rq, ct):
    me = lax.axis_index("tile")
    grp = lax.axis_index("scene")
    last = lax.axis_size("scene") - 1
    loads = [pltpu.make_async_copy(x, y, local_sem.at[i]) for i, (x, y) in enumerate((
        (ids_hbm, ids_ref), (order_hbm, order_ref), (cam_hbm, cam_ref), (gauss_hbm, gauss_ref),
        (cons_hbm, cons_ref), (dual_hbm, dual_ref), (targ_hbm, t_ref), (step_hbm, step_ref), (inter_hbm, inter_ref)))]
    for l in loads:
        l.start()
    near[...] = jnp.zeros_like(near)
    barrier = pltpu.get_barrier_semaphore()

    peers = others(me)
    for t in peers:
        pl.semaphore_signal(barrier, inc=1, device_id={"tile": t}, device_id_type=MESH)

    @pl.when(grp < last)
    def _():
        pl.semaphore_signal(barrier, inc=1, device_id={"scene": grp + 1}, device_id_type=MESH)

    @pl.when(grp > 0)
    def _():
        pl.semaphore_signal(barrier, inc=1, device_id={"scene": grp - 1}, device_id_type=MESH)
    loads[0].wait()
    lane = lax.broadcasted_iota(jnp.int32, (1, 128), 1)
    ask = jnp.full((1, 128), cid_ref[0, 0], jnp.int32)
    for k in range(16):
        b = ids_ref[0, 0, k]
        ask = ask + jnp.where(lane == (b >> 1), (b & 1) * 16, 0)
    req[0] = ask
    reqs[me] = ask
    loads[2].wait()
    loads[3].wait()
    cam = camera_columns(cam_ref)
    outs = [features([gauss_ref[0, i, b:b + 1, :] for i in range(59)], cam) for b in range(2)]
    fbuf[...] = stack3(jnp.concatenate([jnp.concatenate(o, 1) for o in outs], 0))
    pl.semaphore_wait(barrier, NT - 1 + jnp.where(grp < last, 1, 0) + jnp.where(grp > 0, 1, 0))
    exchange(me, peers, req, reqs, e1, False)
    loads[1].wait()
    one, back, bias = slot_map(ids_ref, order_ref, count_ref)
    for l in loads[4:]:
        l.wait()
    passed(reqs, e1.at[1], False)
    asked = jnp.concatenate([reqs[t] for t in range(NT)], 0)
    lane32 = lax.broadcasted_iota(jnp.int32, (NT, 128), 1)
    col = jnp.sum(jnp.where(lane32 == me, asked, 0).astype(f32), 1, keepdims=True).astype(jnp.int32)
    sel = (col == lax.broadcasted_iota(jnp.int32, (NT, NT), 1)).astype(f32)
    place_rows(jnp.dot(thrice(sel), fbuf[...], preferred_element_type=f32), send)
    own_rows(me, send, recv)
    exchange(me, peers, send, recv, e2)
    one3 = thrice(one)
    passed(recv, e2.at[1])
    y = jnp.dot(one3, stack3(gather_rows(recv)), preferred_element_type=f32)
    targ = [jnp.concatenate([t_ref[0, c, 0:1, y0 * 128:(y0 + 1) * 128] for y0 in range(8)], 0) for c in range(3)]
    ybase = (8 * lax.rem(me, 4)).astype(f32)
    outs = render_body(ybase, [y[:, f * 128:(f + 1) * 128] for f in range(NF)], targ, bias, alpha, wts, gbuf, lhs, (k0, k1, k2, k3), tb, cb, bend, grhs, (a0, a1, (a2, a3)), rq, ct)
    place_rows(jnp.dot(jnp.concatenate([back] * 2, 1).astype(bf16), jnp.concatenate(part2(jnp.concatenate(outs, 1)), 0), preferred_element_type=f32), gsend)
    own_rows(me, gsend, grecv)
    exchange(me, peers, gsend, grecv, e3)
    turned = jnp.concatenate([jnp.broadcast_to(col, (NT, 128)).astype(f32), jnp.zeros((96, 128), f32)], 0).T
    selt = (turned[:NT, :NT].astype(jnp.int32) == lax.broadcasted_iota(jnp.int32, (NT, NT), 0)).astype(f32)
    selt = jnp.concatenate([selt] * 2, 1).astype(bf16)
    idx = jnp.concatenate([inter_ref[0, 0, 0:1, :], inter_ref[0, 0, 1:2, :]], 1)
    picks = [(lax.broadcasted_iota(jnp.int32, (128, 128), 0) + b * 128 == idx).astype(f32) for b in range(2)]
    pulls = []
    for b in range(2):
        rows = [gauss_ref[0, i, b:b + 1, :] for i in range(59)]
        pulls.append(jax.vjp(lambda r: features(r, cam), rows)[1])
    for i in range(59):
        base[i] = gauss_ref[0, i] - (penalty_weight * step_ref[i]) * (gauss_ref[0, i] - cons_ref[0, i] + dual_ref[0, i])
    passed(grecv, e3.at[1])
    df = jnp.dot(selt, jnp.concatenate(part2(gather_rows(grecv)), 0), preferred_element_type=f32)
    for b in range(2):
        (grows,) = pulls[b]([df[b * 16:(b + 1) * 16, f * 128:(f + 1) * 128] for f in range(NF)])
        for i in range(59):
            u = base[i, b:b + 1, :] - step_ref[i] * grows[i]
            upd_ref[0, i, b:b + 1, :] = u
            grad[b, i:i + 1, :] = u + dual_ref[0, i, b:b + 1, :]
    grad[:, 59:64, :] = jnp.zeros((2, 5, 128), f32)
    picks3 = [jnp.concatenate([p] * 3, 0).astype(bf16) for p in picks]
    v = sum(jnp.dot(jnp.concatenate(part3(grad[b]), 1).astype(bf16), picks3[b], preferred_element_type=f32) for b in range(2))
    lane = lax.broadcasted_iota(jnp.int32, (32, 128), 1)
    low, high = v[:32], v[32:]
    vals[0] = jnp.where(lane < 64, low, pltpu.roll(high, 64, 1))
    vals[1] = jnp.where(lane < 64, pltpu.roll(low, 64, 1), high)

    def up():
        return pltpu.make_async_remote_copy(vals.at[0], near.at[0], s4.at[0], r4.at[0], device_id={"scene": lax.rem(grp + 1, last + 1)}, device_id_type=MESH)

    def down():
        return pltpu.make_async_remote_copy(vals.at[1], near.at[1], s4.at[1], r4.at[1], device_id={"scene": lax.rem(grp + last, last + 1)}, device_id_type=MESH)

    @pl.when(grp < last)
    def _():
        up().start()

    @pl.when(grp > 0)
    def _():
        down().start()

    @pl.when(grp > 0)
    def _():
        up().wait_recv()
        down().wait_send()

    @pl.when(grp < last)
    def _():
        down().wait_recv()
        up().wait_send()
    from_above = jnp.where(grp < last, 0.5 * (vals[0] - near[1]), 0.0)
    from_below = jnp.where(grp > 0, 0.5 * (vals[1] - near[0]), 0.0)
    diff = jnp.concatenate([
        jnp.where(lane < 64, from_above, pltpu.roll(from_below, 64, 1)),
        jnp.where(lane < 64, pltpu.roll(from_above, 64, 1), from_below),
    ], 0)
    diff3 = jnp.concatenate(part3(diff), 1).astype(bf16)
    for b in range(2):
        p3 = jnp.concatenate([picks[b]] * 3, 1).astype(bf16)
        nd = lax.dot_general(diff3, p3, (((1,), (1,)), ((), ())), preferred_element_type=f32)
        for i in range(59):
            newd_ref[0, i, b:b + 1, :] = nd[i:i + 1, :]
    passed(reqs, e1.at[0], False)
    passed(send, e2.at[0])
    passed(gsend, e3.at[0])


def deliver_kernel(a_ref, b_ref, a_out, b_out, sem):
    moves = [pltpu.make_async_copy(a_ref, a_out, sem.at[0]), pltpu.make_async_copy(b_ref, b_out, sem.at[1])]
    for m in moves:
        m.start()
    for m in moves:
        m.wait()


ANY = pl.BlockSpec(memory_space=pl.ANY)
VM = pl.BlockSpec(memory_space=pltpu.VMEM)
SM = pl.BlockSpec(memory_space=pltpu.SMEM)
HB = pl.BlockSpec(memory_space=pltpu.HBM)
DMA = pltpu.SemaphoreType.DMA


def on_device(gaussians, consensus, duals, step_sizes, cameras, camera_ids, block_lists, depth_order, block_counts, targets, intersection):
    def sd(shape, t=f32):
        return jax.ShapeDtypeStruct(shape, t)
    gaussians, consensus, duals, targets = [a.transpose(0, 2, 1, 3) for a in (gaussians, consensus, duals, targets)]
    big = sd((1, 59, 2, 128))
    gaussians, consensus, duals, targets, cameras, intersection, step_sizes, block_lists, depth_order = [
        pltpu.with_memory_space_constraint(a, pltpu.HBM)
        for a in (gaussians, consensus, duals, targets, cameras, intersection, step_sizes, block_lists, depth_order)
    ]
    out = pl.pallas_call(
        step_kernel, name="step", out_shape=(big, big),
        in_specs=[HB] * 9 + [SM, SM], out_specs=(VM, VM),
        scratch_shapes=[
            pltpu.VMEM((1, 59, 2, 128), f32), pltpu.VMEM((1, 59, 2, 128), f32), pltpu.VMEM((1, 59, 2, 128), f32), pltpu.VMEM((1, 3, 1, 1024), f32),
            pltpu.SMEM((59,), f32), pltpu.VMEM((16, 16), f32), pltpu.VMEM((1, 1, 2, 64), jnp.int32), pltpu.SMEM((1, 1, 16), jnp.int32), pltpu.SMEM((1, 1, 16), jnp.int32), DMA((9,)),
            pltpu.VMEM((1, 1, 128), jnp.int32), pltpu.VMEM((NT, 1, 128), jnp.int32), pltpu.VMEM((3 * NT, NF * 128), bf16),
            pltpu.VMEM((NT * ROWS, 128), f32), pltpu.VMEM((NT * ROWS, 128), f32), pltpu.VMEM((NT * ROWS, 128), f32), pltpu.VMEM((NT * ROWS, 128), f32),
            pltpu.VMEM((2, 64, 128), f32), pltpu.VMEM((59, 2, 128), f32), pltpu.VMEM((2, 32, 128), f32), pltpu.VMEM((2, 32, 128), f32),
            DMA((2,)), DMA((2,)), DMA((2,)), DMA((2,)), DMA((2,)),
        ] + RENDER_SCRATCH,
        compiler_params=pltpu.CompilerParams(collective_id=0, has_side_effects=True, vmem_limit_bytes=VMEM_LIMIT),
    )(gaussians, consensus, duals, targets, step_sizes, cameras, intersection, block_lists, depth_order, camera_ids, block_counts)
    out = pl.pallas_call(
        deliver_kernel, name="deliver", out_shape=(big, big),
        in_specs=[ANY, ANY], out_specs=(HB, HB), scratch_shapes=[DMA((2,))],
        compiler_params=pltpu.CompilerParams(vmem_limit_bytes=1 << 20),
    )(*out)
    return tuple(a.transpose(0, 2, 1, 3) for a in out)


def solution(mesh):
    t4, t3, t2 = P("scene", "tile", None, None), P("scene", "tile", None), P("scene", "tile")
    return jax.shard_map(
        on_device, mesh=mesh,
        in_specs=(t4, t4, t4, P(), P(), t2, t3, t3, t2, t4, t4),
        out_specs=(t4, t4), check_vma=False,
    )
```
